32 devices in a mesh: seq: 4 (over y, x), blk: 8 (over z, core).
Axes of the slice: x: 2, y: 2, z: 4, core: 2. Of those that a mesh axis runs over, the one named last changes fastest.
Arguments:
- hidden_in: bfloat16 [16384, 768], P(('seq', 'blk')), may hold values from -6 to 6
- query_weight: float32 [768, 768], P(('seq', 'blk')), may hold values from -0.3125 to 0.3125
- key_weight: float32 [768, 768], P(('seq', 'blk')), may hold values from -0.21875 to 0.21875
- value_weight: float32 [768, 768], P(('seq', 'blk')), may hold values from -0.21875 to 0.21875
- output_weight: float32 [768, 768], P(('seq', 'blk')), may hold values from -0.875 to 0.875
- inner_weight: float32 [768, 3072], P(('seq', 'blk')), may hold values from -0.21875 to 0.21875
- outer_weight: float32 [3072, 768], P(('seq', 'blk')), may hold values from -0.109375 to 0.109375
- query_bias: float32 [768], P(('seq', 'blk')), may hold values from -2 to 2
- value_bias: float32 [768], P(('seq', 'blk')), may hold values from -2 to 2
- output_bias: float32 [768], P(('seq', 'blk')), may hold values from -2 to 2
- attention_gain: float32 [768], P(('seq', 'blk')), may hold values from 0.5 to 1.5
- attention_shift: float32 [768], P(('seq', 'blk')), may hold values from -2 to 2
- inner_bias: float32 [3072], P(('seq', 'blk')), may hold values from -2 to 2
- outer_bias: float32 [768], P(('seq', 'blk')), may hold values from -2 to 2
- final_gain: float32 [768], P(('seq', 'blk')), may hold values from 0.5 to 1.5
- final_shift: float32 [768], P(('seq', 'blk')), may hold values from -2 to 2
- cotangent: bfloat16 [16384, 768], P(('seq', 'blk')), may hold values from -12 to 12
- grad_mask: int32 [16384, 768], P(('seq', 'blk')), may hold values 0 or 1
- cluster_order: int32 [4, 12, 4096], P('seq'), may hold values from 0 to 4095, each once within a row
Outputs:
- hidden_out: bfloat16 [16384, 768], P(('seq', 'blk'))
- input_grad: float32 [16384, 768], P(('seq', 'blk'))
- grad_query_weight: float32 [768, 768], P(('seq', 'blk'))
- grad_key_weight: float32 [768, 768], P(('seq', 'blk'))
- grad_value_weight: float32 [768, 768], P(('seq', 'blk'))
- grad_output_weight: float32 [768, 768], P(('seq', 'blk'))
- grad_inner_weight: float32 [768, 3072], P(('seq', 'blk'))
- grad_outer_weight: float32 [3072, 768], P(('seq', 'blk'))
- grad_query_bias: float32 [768], P(('seq', 'blk'))
- grad_value_bias: float32 [768], P(('seq', 'blk'))
- grad_output_bias: float32 [768], P(('seq', 'blk'))
- grad_attention_gain: float32 [768], P(('seq', 'blk'))
- grad_attention_shift: float32 [768], P(('seq', 'blk'))
- grad_inner_bias: float32 [3072], P(('seq', 'blk'))
- grad_outer_bias: float32 [768], P(('seq', 'blk'))
- grad_final_gain: float32 [768], P(('seq', 'blk'))
- grad_final_shift: float32 [768], P(('seq', 'blk'))
The draws below stay inside these ranges and needn't reach their ends.
Inputs may be any that keep to these rules, and one draw needn't show every extreme that they name: cluster_order[s, h] lists each position of sequence s once; the clusters of head h are its consecutive runs of 128 entries.
All inputs are finite; a program needn't handle non-finite values. No bound on the sum of `grad_mask` on one device may be relied on, other than what follows from the above.
Results may differ from the reference program's by a relative error of at most 0.015.
The reference program's roundings to bfloat16 on the way count: a program that leaves them out, or rounds other values in their place, can miss the bound.
Values may be sent and summed in bfloat16 or wider, within the bound.
A program may use at most 320 MiB of HBM per device.

```python
import math
import jax
import jax.numpy as jnp
from jax import lax

D = 768
HEADS = 12
HEAD_DIM = 64
FF = 3072
CLUSTER = 128
SEQ_LEN = 4096
SEQS = 4
TOKENS = 16384


def draw_cotangent(key, part):
    first_key = jax.random.fold_in(key, 11)
    second_key = jax.random.fold_in(key, 12)
    third_key = jax.random.fold_in(key, 13)
    base = jax.random.normal(first_key, (TOKENS, D), jnp.float32)
    tail = jnp.exp(0.6 * jax.random.normal(second_key, (TOKENS, D), jnp.float32))
    row_scale = jnp.exp(jax.random.uniform(third_key, (TOKENS, 1), jnp.float32, math.log(0.5), math.log(3.0)))
    return jnp.clip(base * tail * row_scale, -12.0, 12.0).astype(jnp.bfloat16)


def place_ends(drawn, stream_key, low, largest):
    longest = drawn.shape.index(max(drawn.shape))
    spots = []
    for shift in (0, 1):
        where = [jax.random.randint(jax.random.fold_in(stream_key, axis), (), 0, length) for axis, length in enumerate(drawn.shape)]
        where[longest] = (where[longest] + shift) % drawn.shape[longest]
        spots.append(tuple(where))
    return drawn.at[spots[0]].set(low).at[spots[1]].set(largest)


def steps_of(rng, dims, cuts, low, high):
    level = 1.0
    for dim, parts in cuts:
        heights = jax.random.uniform(jax.random.fold_in(jax.random.fold_in(rng, 6), dim), (parts,), jnp.float32, low / len(cuts), high / len(cuts))
        level = level * jnp.repeat(jnp.exp(heights), dims[dim] // parts).reshape((-1,) + (1,) * (len(dims) - 1 - dim))
    return level


def scatter_about(stream_key, dims, deviation, most, cuts=(), dtype=jnp.bfloat16):
    array = jax.random.normal(stream_key, dims, jnp.float32) * deviation
    if len(cuts) > 0:
        array = steps_of(stream_key, dims, cuts, -0.22, 0.18) * array
    return jnp.clip(array, min=-most, max=most).astype(dtype)


def setup_inputs(seed: int = 0) -> dict:
    arg_keys = jax.random.split(jax.random.key(seed), 20)
    hidden_in = scatter_about(arg_keys[0], (TOKENS, D), 1.0, 6.0, ((0, 32),))
    query_weight = scatter_about(arg_keys[1], (D, D), (D // 2) ** -0.5, 0.3125, ((0, 32),), jnp.float32)
    key_weight = scatter_about(arg_keys[2], (D, D), D ** -0.5, 0.21875, ((0, 32),), jnp.float32)
    value_weight = scatter_about(arg_keys[3], (D, D), D ** -0.5, 0.21875, ((0, 32),), jnp.float32)
    output_weight = scatter_about(arg_keys[4], (D, D), (D // 16) ** -0.5, 0.875, ((0, 32),), jnp.float32)
    inner_weight = scatter_about(arg_keys[5], (D, FF), D ** -0.5, 0.21875, ((0, 32),), jnp.float32)
    outer_weight = scatter_about(arg_keys[6], (FF, D), FF ** -0.5, 0.109375, ((0, 32),), jnp.float32)
    query_bias = scatter_about(arg_keys[7], (D,), 0.3, 2.0, ((0, 32),), jnp.float32)
    value_bias = scatter_about(arg_keys[8], (D,), 0.3, 2.0, ((0, 32),), jnp.float32)
    output_bias = scatter_about(arg_keys[9], (D,), 0.3, 2.0, ((0, 32),), jnp.float32)
    attention_gain = jnp.clip(1.0 + 0.1 * jax.random.normal(arg_keys[10], (D,), jnp.float32), 0.5, 1.5)
    attention_shift = scatter_about(arg_keys[11], (D,), 0.3, 2.0, ((0, 32),), jnp.float32)
    inner_bias = scatter_about(arg_keys[12], (FF,), 0.3, 2.0, ((0, 32),), jnp.float32)
    outer_bias = scatter_about(arg_keys[13], (D,), 0.3, 2.0, ((0, 32),), jnp.float32)
    final_gain = jnp.clip(1.0 + 0.1 * jax.random.normal(arg_keys[14], (D,), jnp.float32), 0.5, 1.5)
    final_shift = scatter_about(arg_keys[15], (D,), 0.3, 2.0, ((0, 32),), jnp.float32)
    cotangent = draw_cotangent(jax.random.fold_in(arg_keys[19], 71), 0)
    grad_mask = place_ends((jax.random.randint(arg_keys[17], (TOKENS, D), 0, 4) < 3).astype(jnp.int32), jax.random.fold_in(arg_keys[17], 1), 0, 1)
    cluster_order = jax.vmap(lambda own: jax.random.permutation(own, SEQ_LEN))(jax.random.split(arg_keys[18], SEQS * HEADS)).reshape((SEQS, HEADS, SEQ_LEN)).astype(jnp.int32)
    return {"hidden_in": hidden_in, "query_weight": query_weight, "key_weight": key_weight, "value_weight": value_weight, "output_weight": output_weight, "inner_weight": inner_weight, "outer_weight": outer_weight, "query_bias": query_bias, "value_bias": value_bias, "output_bias": output_bias, "attention_gain": attention_gain, "attention_shift": attention_shift, "inner_bias": inner_bias, "outer_bias": outer_bias, "final_gain": final_gain, "final_shift": final_shift, "cotangent": cotangent, "grad_mask": grad_mask, "cluster_order": cluster_order}


@jax.custom_vjp
def low(v):
    return lax.optimization_barrier(v.astype(jnp.bfloat16)).astype(jnp.float32)

@jax.custom_vjp
def low_back(v):
    return v

def low_keep(v):
    return (low(v), None)

def low_pass(kept, grad):
    return (grad,)

def back_keep(v):
    return (v, None)

def back_low(kept, grad):
    return (low(grad),)
low.defvjp(low_keep, low_pass)
low_back.defvjp(back_keep, back_low)
epsilon = 1e-06

def dense(left, right):
    return jnp.dot(left, right, precision=lax.Precision.HIGHEST)

def layer_norm(value, gain, shift):
    center = value - lax.optimization_barrier(jnp.mean(value, axis=-1, keepdims=True))
    spread = lax.optimization_barrier(jnp.mean(center * center, axis=-1, keepdims=True))
    return center * lax.rsqrt(spread + epsilon) * gain + shift

def cluster_attention(query, keys, values, order):
    length = query.shape[0]
    picker = order[:, :, None]

    def grouped(value):
        heads_first = value.reshape(length, HEADS, HEAD_DIM).transpose(1, 0, 2)
        taken = jnp.take_along_axis(heads_first, picker, axis=1)
        return taken.reshape(HEADS, length // CLUSTER, CLUSTER, HEAD_DIM)
    scale = 1.0 / math.sqrt(HEAD_DIM)
    scores = jnp.einsum('hcid,hcjd->hcij', grouped(query), grouped(keys), precision=lax.Precision.HIGHEST)
    scores = low_back(scores * scale)
    probs = low(jax.nn.softmax(scores, axis=-1))
    mixed = jnp.einsum('hcij,hcjd->hcid', probs, grouped(values), precision=lax.Precision.HIGHEST)
    mixed = mixed.reshape(HEADS, length, HEAD_DIM)
    back = jnp.argsort(order, axis=-1)
    natural = jnp.take_along_axis(mixed, back[:, :, None], axis=1)
    return natural.transpose(1, 0, 2).reshape(length, HEADS * HEAD_DIM)

def forward(hidden, params, order):
    lowered = [low(param) for param in params]
    query_w, key_w, value_w, output_w, inner_w, outer_w = lowered[0:6]
    query_b, value_b, output_b, attn_gain, attn_shift, inner_b, outer_b, fin_gain, fin_shift = lowered[6:15]
    query = low(low_back(dense(hidden, query_w) + query_b))
    keys = low(low_back(dense(hidden, key_w)))
    values = low(low_back(dense(hidden, value_w) + value_b))
    sequences = order.shape[0]

    def one_sequence(item):
        return cluster_attention(item[0], item[1], item[2], item[3])
    context = lax.map(jax.checkpoint(one_sequence), (query.reshape(sequences, SEQ_LEN, D), keys.reshape(sequences, SEQ_LEN, D), values.reshape(sequences, SEQ_LEN, D), order))
    context = low(low_back(context.reshape(sequences * SEQ_LEN, D)))
    attention_out = low_back(dense(context, output_w) + output_b)
    first = layer_norm(hidden + attention_out, attn_gain, attn_shift)
    inner = low_back(dense(low(first), inner_w) + inner_b)
    activated = low(jax.nn.gelu(inner, approximate=False))
    outer = low_back(dense(activated, outer_w) + outer_b)
    return layer_norm(first + outer, fin_gain, fin_shift)

def reference(hidden_in, query_weight, key_weight, value_weight, output_weight, inner_weight, outer_weight, query_bias, value_bias, output_bias, attention_gain, attention_shift, inner_bias, outer_bias, final_gain, final_shift, cotangent, grad_mask, cluster_order):
    params = (query_weight, key_weight, value_weight, output_weight, inner_weight, outer_weight, query_bias, value_bias, output_bias, attention_gain, attention_shift, inner_bias, outer_bias, final_gain, final_shift)
    hidden = hidden_in.astype(jnp.float32)

    def run(hidden_value, param_values):
        return forward(hidden_value, param_values, cluster_order)
    result, pull = jax.vjp(run, hidden, params)
    out_grad = cotangent.astype(jnp.float32) * grad_mask.astype(jnp.float32)
    hidden_grad, grads = pull(out_grad)
    return (result.astype(jnp.bfloat16), hidden_grad, grads[0], grads[1], grads[2], grads[3], grads[4], grads[5], grads[6], grads[7], grads[8], grads[9], grads[10], grads[11], grads[12], grads[13], grads[14])
```

```python
import functools
import math

import jax
import jax.numpy as jnp
from jax import lax
from jax.experimental import pallas as pl
from jax.experimental.pallas import tpu as pltpu
from jax.sharding import PartitionSpec as P

MESH = pl.DeviceIdType.MESH
ANY = pl.ANY
LOW = jnp.bfloat16
F32 = jnp.float32
BIG = 60 * 2**20
GROUP = 4
CLUSTER = 128


def spec(space):
    return pl.BlockSpec(memory_space=space)


def nt_dot(left, right):
    return lax.dot_general(left, right, (((1,), (1,)), ((), ())), preferred_element_type=F32)


def tn_dot(left, right):
    return lax.dot_general(left, right, (((0,), (0,)), ((), ())), preferred_element_type=F32)


def nn_dot(left, right):
    return jnp.dot(left, right, preferred_element_type=F32)


def greet(targets):
    sem = pltpu.get_barrier_semaphore()
    for target in targets:
        pl.semaphore_signal(sem, inc=1, device_id=target, device_id_type=MESH)
    pl.semaphore_wait(sem, len(targets))


def send(src, dst, send_sem, recv_sem, target):
    return pltpu.make_async_remote_copy(
        src_ref=src,
        dst_ref=dst,
        send_sem=send_sem,
        recv_sem=recv_sem,
        device_id=target,
        device_id_type=MESH,
    )


epsilon = 1e-06


def layer_norm(value, gain, shift):
    center = value - jnp.mean(value, axis=-1, keepdims=True)
    spread = jnp.mean(center * center, axis=-1, keepdims=True)
    return center * lax.rsqrt(spread + epsilon) * gain + shift


def exact_gelu(value):
    return jax.nn.gelu(value, approximate=False)


def row_contract(left, right):
    return lax.dot_general(
        left, right, (((0,), (0,)), ((), ())), preferred_element_type=jnp.float32
    )


def back_product(grad, weight):
    return lax.dot_general(
        grad, weight, (((1,), (1,)), ((), ())), preferred_element_type=jnp.float32
    )


def column_sum(value):
    return jnp.sum(value.astype(jnp.float32), axis=0)


def head_major(value, heads):
    return value.reshape(value.shape[0], heads, -1).transpose(1, 0, 2)


def token_major(value):
    return value.transpose(1, 0, 2).reshape(value.shape[1], value.shape[0] * value.shape[2])


def entry_kernel(
    seqs, blks, parts, x_ref, w_ref, o_ref, wall_ref,
    own_sem, ssem, rsem, wl, ws, wr, us, ur,
):
    half = blks // 2
    s = lax.axis_index("seq")
    b = lax.axis_index("blk")
    k = b // 2
    c = lax.rem(b, 2)
    mate = b + 1 - 2 * c
    left = lax.rem(b + blks - 2, blks)
    right = lax.rem(b + 2, blks)
    has_left = k > 0
    has_right = k < half - 1
    blk_peers = [{"blk": lax.rem(b + d, blks)} for d in range(1, blks)]
    seq_peers = [{"seq": lax.rem(s + d, seqs)} for d in range(1, seqs)]
    greet(blk_peers + seq_peers)

    def slab(d):
        peer = lax.rem(b + d, blks)
        return send(w_ref.at[peer], wall_ref.at[s, b], ws.at[d], wr.at[d], {"blk": peer})

    def group(d):
        return send(
            wall_ref.at[s], wall_ref.at[s], us.at[d], ur.at[d], {"seq": lax.rem(s + d, seqs)}
        )

    def piece(src, blk, p, to, way):
        return send(src, o_ref.at[blk, p], ssem.at[way, blk, p], rsem.at[blk, p], {"blk": to})

    for d in range(1, blks):
        slab(d).start()
    own_slab = pltpu.make_async_copy(w_ref.at[b], wall_ref.at[s, b], wl)
    own_slab.start()
    for p in range(parts):
        @pl.when(has_left)
        def _():
            piece(x_ref.at[p], b, p, left, 0).start()

        @pl.when(has_right)
        def _():
            piece(x_ref.at[p], b, p, right, 1).start()
    for p in range(parts):
        piece(x_ref.at[p], b, p, mate, 2).start()
    own = pltpu.make_async_copy(x_ref, o_ref.at[b], own_sem)
    own.start()
    own_slab.wait()
    for d in range(1, blks):
        slab(d).wait_recv()
    for d in range(1, seqs):
        group(d).start()
    for t in range(1, half):
        for p in range(parts):
            @pl.when(k - t >= 0)
            def _():
                blk = b - 2 * t
                piece(o_ref.at[blk, p], blk, p, right, 1).wait_recv()

                @pl.when(has_right)
                def _():
                    piece(o_ref.at[blk, p], blk, p, right, 1).start()

                piece(o_ref.at[blk, p], blk, p, mate, 2).start()

            @pl.when(k + t < half)
            def _():
                blk = b + 2 * t
                piece(o_ref.at[blk, p], blk, p, left, 0).wait_recv()

                @pl.when(has_left)
                def _():
                    piece(o_ref.at[blk, p], blk, p, left, 0).start()

                piece(o_ref.at[blk, p], blk, p, mate, 2).start()
    for j in range(half):
        blk = 2 * j + 1 - c
        for p in range(parts):
            piece(o_ref.at[blk, p], blk, p, mate, 2).wait_recv()
    for j in range(half):
        blk = 2 * j + c
        for p in range(parts):
            piece(o_ref.at[blk, p], blk, p, mate, 2).wait_send()

            @pl.when(jnp.logical_and(has_right, j <= k))
            def _():
                piece(o_ref.at[blk, p], blk, p, right, 1).wait_send()

            @pl.when(jnp.logical_and(has_left, j >= k))
            def _():
                piece(o_ref.at[blk, p], blk, p, left, 0).wait_send()
    own.wait()
    for d in range(1, blks):
        slab(d).wait_send()
    for d in range(1, seqs):
        group(d).wait()


def entry(hidden, slabs, seqs, blks, parts):
    rows, width = hidden.shape
    dma = pltpu.SemaphoreType.DMA
    return pl.pallas_call(
        functools.partial(entry_kernel, seqs, blks, parts),
        name="entry",
        out_shape=(
            jax.ShapeDtypeStruct((blks, parts, rows // parts, width), LOW),
            jax.ShapeDtypeStruct((seqs,) + slabs.shape, LOW),
        ),
        in_specs=[spec(pltpu.VMEM)] * 2,
        out_specs=(spec(ANY), spec(ANY)),
        scratch_shapes=[
            dma, dma((3, blks, parts)), dma((blks, parts)), dma,
            dma((blks,)), dma((blks,)), dma((seqs,)), dma((seqs,)),
        ],
        compiler_params=pltpu.CompilerParams(collective_id=0, has_side_effects=True),
        cost_estimate=pl.CostEstimate(flops=0, transcendentals=0, bytes_accessed=200 * 10**6),
    )(hidden.reshape(parts, rows // parts, width), slabs)


def return_kernel(blks, nat_ref, pack_ref, even_ref, odd_ref, buf, lsem, ssem, rsem):
    b = lax.axis_index("blk")
    k = b // 2
    c = lax.rem(b, 2)
    greet([{"blk": lax.rem(b + d, blks)} for d in range(1, blks)])
    start_return(blks, b, k, c, nat_ref, pack_ref, even_ref, odd_ref, buf, lsem, ssem, rsem)
    finish_return(blks, b, k, c, nat_ref, pack_ref, even_ref, odd_ref, ssem, rsem)


def full_way(blks, b, d, nat_ref, even_ref, ssem, rsem, slot):
    peer = lax.rem(b + d, blks)
    return send(nat_ref.at[peer], even_ref.at[slot], ssem.at[d], rsem.at[d], {"blk": peer})


def start_return(blks, b, k, c, nat_ref, pack_ref, even_ref, odd_ref, buf, lsem, ssem, rsem):
    @pl.when(c == 0)
    def _():
        for d in range(1, blks):
            full_way(blks, b, d, nat_ref, even_ref, ssem, rsem, k).start()
        inward = pltpu.make_async_copy(nat_ref.at[b], buf, lsem)
        inward.start()
        inward.wait()
        outward = pltpu.make_async_copy(buf, even_ref.at[k], lsem)
        outward.start()
        outward.wait()

    @pl.when(c == 1)
    def _():
        for d in range(1, blks):
            full_way(blks, b, d, pack_ref, odd_ref, ssem, rsem, k).start()
        part = buf.at[pl.ds(0, pack_ref.shape[1])]
        inward = pltpu.make_async_copy(pack_ref.at[b], part, lsem)
        inward.start()
        inward.wait()
        outward = pltpu.make_async_copy(part, odd_ref.at[k], lsem)
        outward.start()
        outward.wait()


def finish_return(blks, b, k, c, nat_ref, pack_ref, even_ref, odd_ref, ssem, rsem):
    for d in range(1, blks):
        source = lax.rem(b + blks - d, blks)

        @pl.when(lax.rem(source, 2) == 0)
        def _():
            full_way(blks, b, d, nat_ref, even_ref, ssem, rsem, source // 2).wait_recv()

        @pl.when(lax.rem(source, 2) == 1)
        def _():
            full_way(blks, b, d, pack_ref, odd_ref, ssem, rsem, source // 2).wait_recv()

    @pl.when(c == 0)
    def _():
        for d in range(1, blks):
            full_way(blks, b, d, nat_ref, even_ref, ssem, rsem, k).wait_send()

    @pl.when(c == 1)
    def _():
        for d in range(1, blks):
            full_way(blks, b, d, pack_ref, odd_ref, ssem, rsem, k).wait_send()


def return_rows(nat, pack, collective_id):
    blks = nat.shape[0]
    dma = pltpu.SemaphoreType.DMA
    return pl.pallas_call(
        functools.partial(return_kernel, blks),
        name="return_rows",
        out_shape=(
            jax.ShapeDtypeStruct((blks // 2,) + nat.shape[1:], LOW),
            jax.ShapeDtypeStruct((blks // 2,) + pack.shape[1:], LOW),
        ),
        in_specs=[spec(ANY)] * 2,
        out_specs=(spec(ANY), spec(ANY)),
        scratch_shapes=[pltpu.VMEM(nat.shape[1:], LOW), dma, dma((blks,)), dma((blks,))],
        compiler_params=pltpu.CompilerParams(collective_id=collective_id, has_side_effects=True),
        cost_estimate=pl.CostEstimate(flops=0, transcendentals=0, bytes_accessed=80 * 10**6),
    )(nat, pack)


def spread_kernel(blks, even_ref, odd_ref, nat_ref, pack_ref, buf, lsem, ssem, rsem):
    b = lax.axis_index("blk")
    c = lax.rem(b, 2)
    greet([{"blk": lax.rem(b + d, blks)} for d in range(1, blks)])

    def full(d, slot):
        peer = lax.rem(b + d, blks)
        return send(
            even_ref.at[peer // 2], nat_ref.at[slot], ssem.at[d], rsem.at[d], {"blk": peer}
        )

    def packed(d, slot):
        peer = lax.rem(b + d, blks)
        return send(
            odd_ref.at[peer // 2], pack_ref.at[slot], ssem.at[d], rsem.at[d], {"blk": peer}
        )

    for d in range(1, blks):
        to_even = lax.rem(b + d, 2) == 0

        @pl.when(to_even)
        def _():
            full(d, b).start()

        @pl.when(jnp.logical_not(to_even))
        def _():
            packed(d, b).start()

    @pl.when(c == 0)
    def _():
        inward = pltpu.make_async_copy(even_ref.at[b // 2], buf, lsem)
        inward.start()
        inward.wait()
        outward = pltpu.make_async_copy(buf, nat_ref.at[b], lsem)
        outward.start()
        outward.wait()
        for d in range(1, blks):
            full(d, lax.rem(b + blks - d, blks)).wait_recv()

    @pl.when(c == 1)
    def _():
        part = buf.at[pl.ds(0, odd_ref.shape[1])]
        inward = pltpu.make_async_copy(odd_ref.at[b // 2], part, lsem)
        inward.start()
        inward.wait()
        outward = pltpu.make_async_copy(part, pack_ref.at[b], lsem)
        outward.start()
        outward.wait()
        for d in range(1, blks):
            packed(d, lax.rem(b + blks - d, blks)).wait_recv()

    for d in range(1, blks):
        to_even = lax.rem(b + d, 2) == 0

        @pl.when(to_even)
        def _():
            full(d, b).wait_send()

        @pl.when(jnp.logical_not(to_even))
        def _():
            packed(d, b).wait_send()


def spread_rows(even, odd, collective_id):
    blks = 2 * even.shape[0]
    dma = pltpu.SemaphoreType.DMA
    return pl.pallas_call(
        functools.partial(spread_kernel, blks),
        name="spread_rows",
        out_shape=(
            jax.ShapeDtypeStruct((blks,) + even.shape[1:], LOW),
            jax.ShapeDtypeStruct((blks,) + odd.shape[1:], LOW),
        ),
        in_specs=[spec(ANY)] * 2,
        out_specs=(spec(ANY), spec(ANY)),
        scratch_shapes=[pltpu.VMEM(even.shape[1:], LOW), dma, dma((blks,)), dma((blks,))],
        compiler_params=pltpu.CompilerParams(collective_id=collective_id, has_side_effects=True),
        cost_estimate=pl.CostEstimate(flops=0, transcendentals=0, bytes_accessed=80 * 10**6),
    )(even, odd)


def exit_kernel(
    seqs, blks, nat_ref, pack_ref, grad_ref, even_ref, odd_ref, out_ref,
    buf, stage, total, lsem, ssem, rsem, us, ur, gl, gs, gr,
):
    s = lax.axis_index("seq")
    b = lax.axis_index("blk")
    k = b // 2
    c = lax.rem(b, 2)
    blk_peers = [{"blk": lax.rem(b + d, blks)} for d in range(1, blks)]
    seq_peers = [{"seq": lax.rem(s + d, seqs)} for d in range(1, seqs)]
    greet(blk_peers + seq_peers)

    def group(d):
        peer = lax.rem(s + d, seqs)
        return send(grad_ref.at[peer], stage.at[d], us.at[d], ur.at[d], {"seq": peer})

    def slab(d):
        peer = lax.rem(b + d, blks)
        return send(total.at[peer], out_ref.at[b], gs.at[d], gr.at[d], {"blk": peer})

    for d in range(1, seqs):
        group(d).start()
    start_return(blks, b, k, c, nat_ref, pack_ref, even_ref, odd_ref, buf, lsem, ssem, rsem)
    for d in range(1, seqs):
        group(d).wait_recv()
    for o in range(blks):
        acc = grad_ref[s, o].astype(F32)
        for d in range(1, seqs):
            acc = acc + stage[d, o].astype(F32)
        total[o] = acc.astype(LOW)
    for d in range(1, blks):
        slab(d).start()
    own = pltpu.make_async_copy(total.at[b], out_ref.at[b], gl)
    own.start()
    own.wait()
    finish_return(blks, b, k, c, nat_ref, pack_ref, even_ref, odd_ref, ssem, rsem)
    for d in range(1, blks):
        slab(d).wait()
    for d in range(1, seqs):
        group(d).wait_send()


def leave(nat, pack, grads):
    blks = nat.shape[0]
    seqs = grads.shape[0]
    dma = pltpu.SemaphoreType.DMA
    return pl.pallas_call(
        functools.partial(exit_kernel, seqs, blks),
        name="leave",
        out_shape=(
            jax.ShapeDtypeStruct((blks // 2,) + nat.shape[1:], LOW),
            jax.ShapeDtypeStruct((blks // 2,) + pack.shape[1:], LOW),
            jax.ShapeDtypeStruct(grads.shape[1:], LOW),
        ),
        in_specs=[spec(ANY), spec(ANY), spec(pltpu.VMEM)],
        out_specs=(spec(ANY), spec(ANY), spec(ANY)),
        scratch_shapes=[
            pltpu.VMEM(nat.shape[1:], LOW),
            pltpu.VMEM(grads.shape, LOW),
            pltpu.VMEM(grads.shape[1:], LOW),
            dma, dma((blks,)), dma((blks,)), dma((seqs,)), dma((seqs,)),
            dma, dma((blks,)), dma((blks,)),
        ],
        compiler_params=pltpu.CompilerParams(collective_id=3, has_side_effects=True),
        cost_estimate=pl.CostEstimate(flops=0, transcendentals=0, bytes_accessed=200 * 10**6),
    )(nat, pack, grads)


def lane_of(rows):
    return lax.broadcasted_iota(jnp.int32, (rows, 128), 1)


def low_lanes(value, slot, hd):
    lane = lane_of(value.shape[0])
    keep = jnp.logical_and(lane >= slot * hd, lane < (slot + 1) * hd)
    return jnp.where(keep, value, 0.0).astype(LOW)


def attend_kernel(
    hd, scale, order, count, hid, weight, bias, proj, nat, pack, rows4, take, mix, back
):
    length = hid.shape[0]
    step = nat.shape[1]

    @pl.loop(0, length // step)
    def _(i):
        at = pl.multiple_of(i * step, step)
        low = (nn_dot(hid[pl.ds(at, step), :], weight[...]) + bias[...]).astype(LOW)
        proj[pl.ds(at, step), :] = low
        wide = low.astype(F32)
        for t in range(3):
            rows4[pl.ds(at, step), t, :] = wide[:, t * 128 : (t + 1) * 128]

    span = GROUP * 128

    @pl.loop(0, count[0])
    def _(slot):
        @pl.loop(0, length // span)
        def _(i):
            base = slot * length + i * span
            for j in range(span):
                take[j] = rows4[order[base + j]]
            for u in range(GROUP):
                own = pl.ds(u * 128, 128)
                query = low_lanes(take[own, 0, :], slot, hd)
                scores = nt_dot(query, take[own, 1, :].astype(LOW)) * scale
                weights = jnp.exp(scores - jnp.max(scores, axis=-1, keepdims=True))
                probs = weights / jnp.sum(weights, axis=-1, keepdims=True)
                mix[own, :] = nn_dot(probs.astype(LOW), take[own, 2, :].astype(LOW))
            for j in range(span):
                back[pl.ds(slot * length + order[base + j], 1), :] = mix[pl.ds(j, 1), :]

    lane = lane_of(step)

    @pl.when(count[0] == 2)
    def _():
        @pl.loop(0, length // step)
        def _(i):
            at = pl.multiple_of(i * step, step)
            nat[i] = jnp.where(
                lane < hd, back[pl.ds(at, step), :], back[pl.ds(length + at, step), :]
            ).astype(LOW)

    half = step // 2

    @pl.when(count[0] == 1)
    def _():
        @pl.loop(0, length // step)
        def _(i):
            at = pl.multiple_of(i * step, step)
            upper = pltpu.roll(back[pl.ds(at + half, half), :], hd, 1)
            pack[i] = jnp.where(lane[:half] < hd, back[pl.ds(at, half), :], upper).astype(LOW)


def attend(order, count, hid, weight, bias, blks, hd, scale):
    length = hid.shape[0]
    step = length // blks
    return pl.pallas_call(
        functools.partial(attend_kernel, hd, scale),
        name="attend",
        out_shape=(
            jax.ShapeDtypeStruct((length, 384), LOW),
            jax.ShapeDtypeStruct((blks, step, 128), LOW),
            jax.ShapeDtypeStruct((blks, step // 2, 128), LOW),
        ),
        in_specs=[spec(pltpu.SMEM), spec(pltpu.SMEM)] + [spec(pltpu.VMEM)] * 3,
        out_specs=(spec(pltpu.VMEM),) * 3,
        scratch_shapes=[
            pltpu.VMEM((length, 4, 128), F32),
            pltpu.VMEM((GROUP * 128, 4, 128), F32),
            pltpu.VMEM((GROUP * 128, 128), F32),
            pltpu.VMEM((2 * length, 128), F32),
        ],
        compiler_params=pltpu.CompilerParams(vmem_limit_bytes=BIG),
        cost_estimate=pl.CostEstimate(
            flops=5 * 10**9, transcendentals=0, bytes_accessed=100 * 10**6
        ),
    )(order, count, hid, weight, bias)


def attend_back_kernel(
    hd, scale, order, count, proj, gnat, gpack, znat, zpack, sums, rows4, take, out4, back4
):
    length = proj.shape[0]
    step = gnat.shape[1]
    half = step // 2

    @pl.loop(0, length // step)
    def _(i):
        at = pl.multiple_of(i * step, step)
        wide = proj[pl.ds(at, step), :].astype(F32)
        for t in range(3):
            rows4[pl.ds(at, step), t, :] = wide[:, t * 128 : (t + 1) * 128]

        @pl.when(count[0] == 2)
        def _():
            rows4[pl.ds(at, step), 3, :] = gnat[i].astype(F32)

        @pl.when(count[0] == 1)
        def _():
            pair = gpack[i].astype(F32)
            rows4[pl.ds(at, half), 3, :] = pair
            rows4[pl.ds(at + half, half), 3, :] = pltpu.roll(pair, hd, 1)

    span = GROUP * 128

    @pl.loop(0, count[0])
    def _(slot):
        @pl.loop(0, length // span)
        def _(i):
            base = slot * length + i * span
            for j in range(span):
                take[j] = rows4[order[base + j]]
            for u in range(GROUP):
                own = pl.ds(u * 128, 128)
                query = low_lanes(take[own, 0, :], slot, hd)
                grad = low_lanes(take[own, 3, :], slot, hd)
                keys = take[own, 1, :].astype(LOW)
                scores = nt_dot(query, keys) * scale
                weights = jnp.exp(scores - jnp.max(scores, axis=-1, keepdims=True))
                probs = weights / jnp.sum(weights, axis=-1, keepdims=True)
                prob_grad = nt_dot(grad, take[own, 2, :].astype(LOW))
                shift = jnp.sum(probs * prob_grad, axis=-1, keepdims=True)
                score_low = (probs * (prob_grad - shift)).astype(LOW)
                out4[own, 0, :] = nn_dot(score_low, keys) * scale
                out4[own, 1, :] = tn_dot(score_low, query) * scale
                out4[own, 2, :] = tn_dot(probs.astype(LOW), grad)
            for j in range(span):
                back4[slot * length + order[base + j]] = out4[j]

    lane = lane_of(step)
    sums[...] = jnp.zeros_like(sums)

    @pl.loop(0, length // step)
    def _(i):
        at = pl.multiple_of(i * step, step)
        for t in range(3):
            cols = pl.ds(t * 128, 128)
            first = back4[pl.ds(at, step), t, :]

            @pl.when(count[0] == 2)
            def _():
                both = jnp.where(lane < hd, first, back4[pl.ds(length + at, step), t, :])
                low = both.astype(LOW)
                znat[i, :, cols] = low
                sums[0:1, cols] += jnp.sum(low.astype(F32), axis=0, keepdims=True)

            @pl.when(count[0] == 1)
            def _():
                low = jnp.where(lane < hd, first, 0.0).astype(LOW)
                znat[i, :, cols] = low
                wide = low.astype(F32)
                zpack[i, :, cols] = (wide[:half] + pltpu.roll(wide[half:], hd, 1)).astype(LOW)
                sums[0:1, cols] += jnp.sum(wide, axis=0, keepdims=True)


def attend_back(order, count, proj, gnat, gpack, hd, scale):
    length = proj.shape[0]
    blks, step, _ = gnat.shape
    return pl.pallas_call(
        functools.partial(attend_back_kernel, hd, scale),
        name="attend_back",
        out_shape=(
            jax.ShapeDtypeStruct((blks, step, 384), LOW),
            jax.ShapeDtypeStruct((blks, step // 2, 384), LOW),
            jax.ShapeDtypeStruct((8, 384), F32),
        ),
        in_specs=[spec(pltpu.SMEM), spec(pltpu.SMEM)] + [spec(pltpu.VMEM)] * 3,
        out_specs=(spec(pltpu.VMEM),) * 3,
        scratch_shapes=[
            pltpu.VMEM((length, 4, 128), F32),
            pltpu.VMEM((GROUP * 128, 4, 128), F32),
            pltpu.VMEM((GROUP * 128, 4, 128), F32),
            pltpu.VMEM((2 * length, 4, 128), F32),
        ],
        compiler_params=pltpu.CompilerParams(vmem_limit_bytes=BIG),
        cost_estimate=pl.CostEstimate(
            flops=8 * 10**9, transcendentals=0, bytes_accessed=120 * 10**6
        ),
    )(order, count, proj, gnat, gpack)


def join_columns(even, odd, hd):
    rows = even.shape[1]
    first = even.transpose(1, 0, 2).reshape(rows, -1)
    spread = jnp.concatenate([odd[:, :, :hd], odd[:, :, hd:]], axis=1)
    return jnp.concatenate([first, spread.transpose(1, 0, 2).reshape(rows, -1)], axis=1)


def split_columns(value, chips, hd):
    rows = value.shape[0]
    wide = chips * 2 * hd
    even = value[:, :wide].reshape(rows, chips, 2 * hd).transpose(1, 0, 2)
    odd = value[:, wide:].reshape(rows, chips, hd).transpose(1, 0, 2)
    return even, jnp.concatenate([odd[:, : rows // 2], odd[:, rows // 2 :]], axis=2)


def by_device(value, chips, hd):
    rows = value.shape[0]
    wide = chips * 2 * hd
    even = value[:, :wide].reshape(rows, chips, 2 * hd).transpose(1, 0, 2)
    odd = value[:, wide:].reshape(rows, chips, hd).transpose(1, 0, 2)
    odd = jnp.pad(odd, ((0, 0), (0, 0), (0, hd)))
    return jnp.stack([even, odd], axis=1).reshape(2 * chips, rows, 2 * hd)


def from_device(value, chips, hd):
    rows = value.shape[1]
    pairs = value.reshape(chips, 2, rows, 2 * hd)
    even = pairs[:, 0].transpose(1, 0, 2).reshape(rows, -1)
    odd = pairs[:, 1, :, :hd].transpose(1, 0, 2).reshape(rows, -1)
    return jnp.concatenate([even, odd], axis=1)


def fast_body(seqs, blks, heads):
    def run(
        hidden_in, query_weight, key_weight, value_weight, output_weight, inner_weight,
        outer_weight, query_bias, value_bias, output_bias, attention_gain, attention_shift,
        inner_bias, outer_bias, final_gain, final_shift, cotangent, grad_mask, cluster_order,
    ):
        rows, width = hidden_in.shape
        own = query_weight.shape[0]
        hidden_units = inner_weight.shape[1]
        length = cluster_order.shape[2]
        hd = width // heads
        chips = blks // 2
        scale = 1.0 / math.sqrt(hd)
        devices = seqs * blks
        b = lax.axis_index("blk")
        k = b // 2
        even_core = lax.rem(b, 2) == 0
        query_low, key_low, value_low, output_low, inner_low_w, outer_low_w = [
            w.astype(LOW)
            for w in (
                query_weight, key_weight, value_weight, output_weight, inner_weight, outer_weight,
            )
        ]
        small = jnp.concatenate(
            [
                query_bias, value_bias, output_bias, attention_gain, attention_shift,
                outer_bias, final_gain, final_shift, inner_bias,
            ]
        ).astype(LOW)
        slabs = jnp.concatenate(
            [by_device(w, chips, hd) for w in (query_low, key_low, value_low)], axis=2
        )
        extra = jnp.pad(small[None, :], ((0, 7), (0, 384 - small.shape[0])))
        slabs = jnp.concatenate(
            [slabs, jnp.broadcast_to(extra[None], (blks,) + extra.shape)], axis=1
        )
        axes = ("seq", "blk")
        first_half = lax.all_gather(
            jnp.concatenate([output_low, inner_low_w], axis=1), axes, axis=0, tiled=True
        )
        outer_full = lax.all_gather(outer_low_w, axes, axis=0, tiled=True)
        projections = lax.all_gather(
            jnp.concatenate([query_low, key_low, value_low], axis=1), axes, axis=0, tiled=True
        )
        hidden_all, gathered = entry(hidden_in, slabs, seqs, blks, 2)
        hidden_all = hidden_all.reshape(length, width)
        gathered = gathered.reshape(devices, own + 8, 384)
        weight_own = gathered[:, :own].reshape(width, 384)
        vec = gathered[:, own, : small.shape[0]]
        vecs = (
            vec[:, : 8 * own].reshape(devices, 8, own).transpose(1, 0, 2).reshape(8, width)
        ).astype(F32)
        bias_inner = vec[:, 8 * own :].reshape(1, hidden_units).astype(F32)
        bias_query, bias_value = [
            by_device(vecs[i : i + 1], chips, hd) for i in (0, 1)
        ]
        bias_output, gain_first, shift_first, bias_outer, gain_final, shift_final = [
            vecs[i] for i in range(2, 8)
        ]
        bias_own = lax.dynamic_index_in_dim(
            jnp.concatenate([bias_query, jnp.zeros_like(bias_query), bias_value], axis=2),
            b, 0, keepdims=False,
        )
        order = cluster_order[0]
        head_first = jnp.where(even_core, 2 * k, 2 * chips + k)
        order_own = jnp.concatenate(
            [
                lax.dynamic_index_in_dim(order, head_first, 0, keepdims=False),
                lax.dynamic_index_in_dim(order, 2 * k + 1, 0, keepdims=False),
            ]
        )
        count = jnp.where(even_core, 2, 1).astype(jnp.int32).reshape(1)
        proj, cnat, cpack = attend(
            order_own, count, hidden_all, weight_own, bias_own, blks, hd, scale
        )
        ceven, codd = return_rows(cnat, cpack, 1)
        context_low = join_columns(ceven, codd, hd)

        output_full = first_half[:, :width]
        inner_full = first_half[:, width:]
        hidden = hidden_in.astype(F32)
        attention_out = nn_dot(context_low, output_full) + bias_output
        first_norm, first_pull = jax.vjp(layer_norm, hidden + attention_out, gain_first, shift_first)
        first_low = first_norm.astype(LOW)
        inner_pre = nn_dot(first_low, inner_full) + bias_inner
        activated, gelu_pull = jax.vjp(exact_gelu, inner_pre)
        activated_low = activated.astype(LOW)
        outer_out = nn_dot(activated_low, outer_full) + bias_outer
        final_norm, final_pull = jax.vjp(layer_norm, first_norm + outer_out, gain_final, shift_final)
        hidden_out = final_norm.astype(LOW)
        out_grad = cotangent.astype(F32) * grad_mask.astype(F32)
        second_grad, grad_final_gain, grad_final_shift = final_pull(out_grad)
        outer_low = second_grad.astype(LOW)
        grad_outer_weight = tn_dot(activated_low, outer_low)
        grad_outer_bias = column_sum(outer_low)
        inner_low = gelu_pull(nt_dot(outer_low, outer_full))[0].astype(LOW)
        grad_inner_weight = tn_dot(first_low, inner_low)
        grad_inner_bias = column_sum(inner_low)
        first_grad = nt_dot(inner_low, inner_full) + second_grad
        residual_grad, grad_attention_gain, grad_attention_shift = first_pull(first_grad)
        attn_low = residual_grad.astype(LOW)
        grad_output_weight = tn_dot(context_low, attn_low)
        grad_output_bias = column_sum(attn_low)
        context_grad = nt_dot(attn_low, output_full).astype(LOW)

        vec_grads = jnp.stack(
            [
                grad_output_bias, grad_attention_gain, grad_attention_shift,
                grad_outer_bias, grad_final_gain, grad_final_shift,
            ]
        )
        vec_grads = vec_grads.reshape(6, devices, own).transpose(1, 0, 2).reshape(devices, 6 * own)
        vec_grads = jnp.concatenate(
            [vec_grads, grad_inner_bias.reshape(devices, hidden_units // devices)], axis=1
        )
        vec_grads = jnp.pad(vec_grads, ((0, 0), (0, width - vec_grads.shape[1])))
        merged = jnp.concatenate(
            [
                grad_outer_weight.reshape(devices, hidden_units // devices, width).astype(LOW),
                grad_inner_weight.reshape(devices, own, hidden_units // width, width)
                .transpose(0, 2, 1, 3)
                .reshape(devices, -1, width)
                .astype(LOW),
                grad_output_weight.reshape(devices, own, width).astype(LOW),
                jnp.pad(vec_grads[:, None, :].astype(LOW), ((0, 0), (0, 7), (0, 0))),
            ],
            axis=1,
        )
        share = lax.psum_scatter(
            merged.reshape(-1, width), axes, scatter_dimension=0, tiled=True
        ).astype(F32)

        geven, godd = split_columns(context_grad, chips, hd)
        gnat, gpack = spread_rows(geven, godd, 2)
        znat, zpack, sums = attend_back(order_own, count, proj, gnat, gpack, hd, scale)
        own_grads = tn_dot(hidden_all, znat.reshape(length, 384)).reshape(seqs, blks, own, 384)
        grads = jnp.concatenate(
            [own_grads, jnp.broadcast_to(sums, (seqs, blks, 8, 384))], axis=2
        ).astype(LOW)
        zeven, zodd, proj_grads = leave(znat, zpack, grads)
        triple = jnp.concatenate(
            [
                join_columns(zeven[:, :, i * 128 : (i + 1) * 128], zodd[:, :, i * 128 : (i + 1) * 128], hd)
                for i in range(3)
            ],
            axis=1,
        )
        input_grad = nt_dot(triple, projections) + residual_grad
        grad_query_weight, grad_key_weight, grad_value_weight = [
            from_device(proj_grads[:, :, i * 128 : (i + 1) * 128].astype(F32), chips, hd)
            for i in range(3)
        ]
        me = lax.axis_index("seq") * blks + b
        grad_query_bias = lax.dynamic_slice_in_dim(grad_query_weight[own], me * own, own)
        grad_value_bias = lax.dynamic_slice_in_dim(grad_value_weight[own], me * own, own)
        share_outer = share[: hidden_units // devices]
        at = hidden_units // devices
        tail = at + own * (hidden_units // width)
        share_inner = (
            share[at:tail]
            .reshape(hidden_units // width, own, width)
            .transpose(1, 0, 2)
            .reshape(own, hidden_units)
        )
        share_output = share[tail : tail + own]
        vec_own = share[tail + own]
        vec_parts = [vec_own[i * own : (i + 1) * own] for i in range(6)]
        return (
            hidden_out,
            input_grad,
            grad_query_weight[:own],
            grad_key_weight[:own],
            grad_value_weight[:own],
            share_output,
            share_inner,
            share_outer,
            grad_query_bias,
            grad_value_bias,
            vec_parts[0],
            vec_parts[1],
            vec_parts[2],
            vec_own[6 * own : 6 * own + hidden_units // devices],
            vec_parts[3],
            vec_parts[4],
            vec_parts[5],
        )

    return run


def masked_scores(left, right, left_ids, right_ids, scale):
    scores = back_product(left, right) * scale
    return jnp.where(left_ids[:, None] == right_ids[None, :], scores, -jnp.inf)


def body(
    hidden_in,
    query_weight,
    key_weight,
    value_weight,
    output_weight,
    inner_weight,
    outer_weight,
    query_bias,
    value_bias,
    output_bias,
    attention_gain,
    attention_shift,
    inner_bias,
    outer_bias,
    final_gain,
    final_shift,
    cotangent,
    grad_mask,
    cluster_order,
):
    rows = hidden_in.shape[0]
    width = hidden_in.shape[1]
    heads = cluster_order.shape[1]
    length = cluster_order.shape[2]
    scale = 1.0 / math.sqrt(width // heads)
    masters = (
        query_weight,
        key_weight,
        value_weight,
        output_weight,
        inner_weight,
        outer_weight,
        query_bias,
        value_bias,
        output_bias,
        attention_gain,
        attention_shift,
        inner_bias,
        outer_bias,
        final_gain,
        final_shift,
    )
    lowered = [master.astype(jnp.bfloat16) for master in masters]
    fetched = (
        lax.all_gather(lowered[0], ("seq", "blk"), axis=0, tiled=True),
        lax.all_gather(lowered[1], ("seq", "blk"), axis=0, tiled=True),
        lax.all_gather(lowered[2], ("seq", "blk"), axis=0, tiled=True),
        lax.all_gather(lowered[3], ("seq", "blk"), axis=0, tiled=True),
        lax.all_gather(lowered[4], ("seq", "blk"), axis=0, tiled=True),
        lax.all_gather(lowered[5], ("seq", "blk"), axis=0, tiled=True),
        lax.all_gather(lowered[6], ("seq", "blk"), axis=0, tiled=True),
        lax.all_gather(lowered[7], ("seq", "blk"), axis=0, tiled=True),
        lax.all_gather(lowered[8], ("seq", "blk"), axis=0, tiled=True),
        lax.all_gather(lowered[9], ("seq", "blk"), axis=0, tiled=True),
        lax.all_gather(lowered[10], ("seq", "blk"), axis=0, tiled=True),
        lax.all_gather(lowered[11], ("seq", "blk"), axis=0, tiled=True),
        lax.all_gather(lowered[12], ("seq", "blk"), axis=0, tiled=True),
        lax.all_gather(lowered[13], ("seq", "blk"), axis=0, tiled=True),
        lax.all_gather(lowered[14], ("seq", "blk"), axis=0, tiled=True),
    )
    query_full, key_full, value_full, output_full, inner_full, outer_full = fetched[0:6]
    vectors = [vector.astype(jnp.float32) for vector in fetched[6:15]]
    (
        bias_query,
        bias_value,
        bias_output,
        gain_first,
        shift_first,
        bias_inner,
        bias_outer,
        gain_final,
        shift_final,
    ) = vectors
    hidden = hidden_in.astype(jnp.float32)
    query_low = (
        jnp.dot(hidden_in, query_full, preferred_element_type=jnp.float32) + bias_query
    ).astype(jnp.bfloat16)
    keys_low = jnp.dot(hidden_in, key_full, preferred_element_type=jnp.float32).astype(jnp.bfloat16)
    values_low = (
        jnp.dot(hidden_in, value_full, preferred_element_type=jnp.float32) + bias_value
    ).astype(jnp.bfloat16)
    all_keys, all_values = (
        lax.all_gather(keys_low, "blk", axis=0, tiled=True),
        lax.all_gather(values_low, "blk", axis=0, tiled=True),
    )
    order = cluster_order[0]
    head_rows = jnp.broadcast_to(jnp.arange(heads, dtype=jnp.int32)[:, None], (heads, length))
    positions = jnp.broadcast_to(jnp.arange(length, dtype=jnp.int32)[None, :], (heads, length))
    inverse = jnp.zeros((heads, length), jnp.int32).at[head_rows, order].set(positions)
    key_cluster = inverse // CLUSTER
    member = lax.dynamic_slice_in_dim(key_cluster, lax.axis_index("blk") * rows, rows, 1)
    query_heads = head_major(query_low, heads)
    key_heads = head_major(all_keys, heads)
    value_heads = head_major(all_values, heads)
    head_ids = jnp.arange(heads, dtype=jnp.int32)

    def attend(index):
        scores = masked_scores(
            query_heads[index], key_heads[index], member[index], key_cluster[index], scale
        )
        peak = jnp.max(scores, axis=-1, keepdims=True)
        weights = jnp.exp(scores - peak)
        total = jnp.sum(weights, axis=-1, keepdims=True)
        probs_low = (weights / total).astype(jnp.bfloat16)
        mixed = jnp.dot(probs_low, value_heads[index], preferred_element_type=jnp.float32)
        return (mixed, (peak + jnp.log(total))[:, 0])

    mixed, logsum = lax.map(attend, head_ids)
    context_low = token_major(mixed).astype(jnp.bfloat16)
    attention_out = (
        jnp.dot(context_low, output_full, preferred_element_type=jnp.float32) + bias_output
    )
    first_norm, first_pull = jax.vjp(layer_norm, hidden + attention_out, gain_first, shift_first)
    first_low = first_norm.astype(jnp.bfloat16)
    inner_pre = jnp.dot(first_low, inner_full, preferred_element_type=jnp.float32) + bias_inner
    activated, gelu_pull = jax.vjp(exact_gelu, inner_pre)
    activated_low = activated.astype(jnp.bfloat16)
    outer_out = jnp.dot(activated_low, outer_full, preferred_element_type=jnp.float32) + bias_outer
    final_norm, final_pull = jax.vjp(layer_norm, first_norm + outer_out, gain_final, shift_final)
    hidden_out = final_norm.astype(jnp.bfloat16)
    out_grad = cotangent.astype(jnp.float32) * grad_mask.astype(jnp.float32)
    second_grad, grad_final_gain, grad_final_shift = final_pull(out_grad)
    outer_low = second_grad.astype(jnp.bfloat16)
    back_weights = (
        lax.all_gather(lowered[0], ("seq", "blk"), axis=0, tiled=True),
        lax.all_gather(lowered[1], ("seq", "blk"), axis=0, tiled=True),
        lax.all_gather(lowered[2], ("seq", "blk"), axis=0, tiled=True),
        lax.all_gather(lowered[3], ("seq", "blk"), axis=0, tiled=True),
        lax.all_gather(lowered[4], ("seq", "blk"), axis=0, tiled=True),
        lax.all_gather(lowered[5], ("seq", "blk"), axis=0, tiled=True),
    )
    grad_outer_weight = row_contract(activated_low, outer_low)
    grad_outer_bias = column_sum(outer_low)
    inner_low = gelu_pull(back_product(outer_low, back_weights[5]))[0].astype(jnp.bfloat16)
    grad_inner_weight = row_contract(first_low, inner_low)
    grad_inner_bias = column_sum(inner_low)
    first_grad = back_product(inner_low, back_weights[4]) + second_grad
    residual_grad, grad_attention_gain, grad_attention_shift = first_pull(first_grad)
    attn_low = residual_grad.astype(jnp.bfloat16)
    grad_output_weight = row_contract(context_low, attn_low)
    grad_output_bias = column_sum(attn_low)
    context_grad = back_product(attn_low, back_weights[3]).astype(jnp.bfloat16)
    grad_heads = head_major(context_grad, heads)

    def own_rows_back(index):
        scores = masked_scores(
            query_heads[index], key_heads[index], member[index], key_cluster[index], scale
        )
        probs = jnp.exp(scores - logsum[index][:, None])
        probs_low = probs.astype(jnp.bfloat16)
        grad_part = grad_heads[index]
        prob_grad = back_product(grad_part, value_heads[index])
        weighted = jnp.sum(probs * prob_grad, axis=-1, keepdims=True)
        score_low = (probs * (prob_grad - weighted)).astype(jnp.bfloat16)
        query_grad = (
            jnp.dot(score_low, key_heads[index], preferred_element_type=jnp.float32) * scale
        )
        return (probs_low, score_low, query_grad, weighted[:, 0])

    def attend_back(index):
        probs_low, score_low, query_grad, weighted = own_rows_back(index)
        key_sum = row_contract(score_low, query_heads[index]) * scale
        value_sum = row_contract(probs_low, grad_heads[index])
        return (query_grad, key_sum, value_sum)

    query_grads, key_grads, value_grads = lax.map(attend_back, head_ids)
    key_own, value_own = (
        lax.psum_scatter(token_major(key_grads), "blk", scatter_dimension=0, tiled=True),
        lax.psum_scatter(token_major(value_grads), "blk", scatter_dimension=0, tiled=True),
    )
    query_grad_low = token_major(query_grads).astype(jnp.bfloat16)
    key_grad_low = key_own.astype(jnp.bfloat16)
    value_grad_low = value_own.astype(jnp.bfloat16)
    grad_query_weight = row_contract(hidden_in, query_grad_low)
    grad_key_weight = row_contract(hidden_in, key_grad_low)
    grad_value_weight = row_contract(hidden_in, value_grad_low)
    grad_query_bias = column_sum(query_grad_low)
    grad_value_bias = column_sum(value_grad_low)
    input_grad = (
        back_product(query_grad_low, back_weights[0])
        + back_product(key_grad_low, back_weights[1])
        + back_product(value_grad_low, back_weights[2])
        + residual_grad
    )
    shares = (
        lax.psum_scatter(grad_query_weight, ("seq", "blk"), scatter_dimension=0, tiled=True),
        lax.psum_scatter(grad_key_weight, ("seq", "blk"), scatter_dimension=0, tiled=True),
        lax.psum_scatter(grad_value_weight, ("seq", "blk"), scatter_dimension=0, tiled=True),
        lax.psum_scatter(grad_output_weight, ("seq", "blk"), scatter_dimension=0, tiled=True),
        lax.psum_scatter(grad_inner_weight, ("seq", "blk"), scatter_dimension=0, tiled=True),
        lax.psum_scatter(grad_outer_weight, ("seq", "blk"), scatter_dimension=0, tiled=True),
        lax.psum_scatter(grad_query_bias, ("seq", "blk"), scatter_dimension=0, tiled=True),
        lax.psum_scatter(grad_value_bias, ("seq", "blk"), scatter_dimension=0, tiled=True),
        lax.psum_scatter(grad_output_bias, ("seq", "blk"), scatter_dimension=0, tiled=True),
        lax.psum_scatter(grad_attention_gain, ("seq", "blk"), scatter_dimension=0, tiled=True),
        lax.psum_scatter(grad_attention_shift, ("seq", "blk"), scatter_dimension=0, tiled=True),
        lax.psum_scatter(grad_inner_bias, ("seq", "blk"), scatter_dimension=0, tiled=True),
        lax.psum_scatter(grad_outer_bias, ("seq", "blk"), scatter_dimension=0, tiled=True),
        lax.psum_scatter(grad_final_gain, ("seq", "blk"), scatter_dimension=0, tiled=True),
        lax.psum_scatter(grad_final_shift, ("seq", "blk"), scatter_dimension=0, tiled=True),
    )
    return (hidden_out, input_grad) + tuple(shares)


def solution(mesh):
    placed = (
        P(("seq", "blk"), None),
        P(("seq", "blk"), None),
        P(("seq", "blk"), None),
        P(("seq", "blk"), None),
        P(("seq", "blk"), None),
        P(("seq", "blk"), None),
        P(("seq", "blk"), None),
        P(("seq", "blk")),
        P(("seq", "blk")),
        P(("seq", "blk")),
        P(("seq", "blk")),
        P(("seq", "blk")),
        P(("seq", "blk")),
        P(("seq", "blk")),
        P(("seq", "blk")),
        P(("seq", "blk")),
        P(("seq", "blk"), None),
        P(("seq", "blk"), None),
        P("seq", None, None),
    )
    seqs, blks = mesh.shape["seq"], mesh.shape["blk"]
    heads = 12
    fast = blks % 2 == 0 and 3 * blks == 2 * heads
    return jax.shard_map(
        fast_body(seqs, blks, heads) if fast else body,
        mesh=mesh,
        in_specs=placed,
        out_specs=(
            P(("seq", "blk"), None),
            P(("seq", "blk"), None),
            P(("seq", "blk"), None),
            P(("seq", "blk"), None),
            P(("seq", "blk"), None),
            P(("seq", "blk"), None),
            P(("seq", "blk"), None),
            P(("seq", "blk"), None),
            P(("seq", "blk")),
            P(("seq", "blk")),
            P(("seq", "blk")),
            P(("seq", "blk")),
            P(("seq", "blk")),
            P(("seq", "blk")),
            P(("seq", "blk")),
            P(("seq", "blk")),
            P(("seq", "blk")),
        ),
        check_vma=False,
    )
```

```python
import functools
import math

import jax
import jax.numpy as jnp
from jax import lax
from jax.experimental import pallas as pl
from jax.experimental.pallas import tpu as pltpu
from jax.sharding import PartitionSpec as P

MESH = pl.DeviceIdType.MESH
ANY = pl.ANY
LOW = jnp.bfloat16
F32 = jnp.float32
BIG = 60 * 2**20
GROUP = 4
CLUSTER = 128


def spec(space):
    return pl.BlockSpec(memory_space=space)


def nt_dot(left, right):
    return lax.dot_general(left, right, (((1,), (1,)), ((), ())), preferred_element_type=F32)


def tn_dot(left, right):
    return lax.dot_general(left, right, (((0,), (0,)), ((), ())), preferred_element_type=F32)


def nn_dot(left, right):
    return jnp.dot(left, right, preferred_element_type=F32)


def greet(targets):
    sem = pltpu.get_barrier_semaphore()
    for target in targets:
        pl.semaphore_signal(sem, inc=1, device_id=target, device_id_type=MESH)
    pl.semaphore_wait(sem, len(targets))


def send(src, dst, send_sem, recv_sem, target):
    return pltpu.make_async_remote_copy(
        src_ref=src,
        dst_ref=dst,
        send_sem=send_sem,
        recv_sem=recv_sem,
        device_id=target,
        device_id_type=MESH,
    )


epsilon = 1e-06


def layer_norm(value, gain, shift):
    center = value - jnp.mean(value, axis=-1, keepdims=True)
    spread = jnp.mean(center * center, axis=-1, keepdims=True)
    return center * lax.rsqrt(spread + epsilon) * gain + shift


def exact_gelu(value):
    return jax.nn.gelu(value, approximate=False)


def row_contract(left, right):
    return lax.dot_general(
        left, right, (((0,), (0,)), ((), ())), preferred_element_type=jnp.float32
    )


def back_product(grad, weight):
    return lax.dot_general(
        grad, weight, (((1,), (1,)), ((), ())), preferred_element_type=jnp.float32
    )


def column_sum(value):
    return jnp.sum(value.astype(jnp.float32), axis=0)


def head_major(value, heads):
    return value.reshape(value.shape[0], heads, -1).transpose(1, 0, 2)


def token_major(value):
    return value.transpose(1, 0, 2).reshape(value.shape[1], value.shape[0] * value.shape[2])


def entry_kernel(
    seqs, blks, parts, x_ref, w_ref, o_ref, wall_ref,
    own_sem, ssem, rsem, wl, ws, wr, us, ur,
):
    half = blks // 2
    s = lax.axis_index("seq")
    b = lax.axis_index("blk")
    k = b // 2
    c = lax.rem(b, 2)
    mate = b + 1 - 2 * c
    left = lax.rem(b + blks - 2, blks)
    right = lax.rem(b + 2, blks)
    has_left = k > 0
    has_right = k < half - 1
    blk_peers = [{"blk": lax.rem(b + d, blks)} for d in range(1, blks)]
    seq_peers = [{"seq": lax.rem(s + d, seqs)} for d in range(1, seqs)]
    greet(blk_peers + seq_peers)

    def slab(d):
        peer = lax.rem(b + d, blks)
        return send(w_ref.at[peer], wall_ref.at[s, b], ws.at[d], wr.at[d], {"blk": peer})

    def group(d):
        return send(
            wall_ref.at[s], wall_ref.at[s], us.at[d], ur.at[d], {"seq": lax.rem(s + d, seqs)}
        )

    def piece(src, blk, p, to, way):
        return send(src, o_ref.at[blk, p], ssem.at[way, blk, p], rsem.at[blk, p], {"blk": to})

    for d in range(1, blks):
        slab(d).start()
    own_slab = pltpu.make_async_copy(w_ref.at[b], wall_ref.at[s, b], wl)
    own_slab.start()
    for p in range(parts):
        @pl.when(has_left)
        def _():
            piece(x_ref.at[p], b, p, left, 0).start()

        @pl.when(has_right)
        def _():
            piece(x_ref.at[p], b, p, right, 1).start()
    for p in range(parts):
        piece(x_ref.at[p], b, p, mate, 2).start()
    own = pltpu.make_async_copy(x_ref, o_ref.at[b], own_sem)
    own.start()
    own_slab.wait()
    for d in range(1, blks):
        slab(d).wait_recv()
    for d in range(1, seqs):
        group(d).start()
    for t in range(1, half):
        for p in range(parts):
            @pl.when(k - t >= 0)
            def _():
                blk = b - 2 * t
                piece(o_ref.at[blk, p], blk, p, right, 1).wait_recv()

                @pl.when(has_right)
                def _():
                    piece(o_ref.at[blk, p], blk, p, right, 1).start()

                piece(o_ref.at[blk, p], blk, p, mate, 2).start()

            @pl.when(k + t < half)
            def _():
                blk = b + 2 * t
                piece(o_ref.at[blk, p], blk, p, left, 0).wait_recv()

                @pl.when(has_left)
                def _():
                    piece(o_ref.at[blk, p], blk, p, left, 0).start()

                piece(o_ref.at[blk, p], blk, p, mate, 2).start()
    for j in range(half):
        blk = 2 * j + 1 - c
        for p in range(parts):
            piece(o_ref.at[blk, p], blk, p, mate, 2).wait_recv()
    for j in range(half):
        blk = 2 * j + c
        for p in range(parts):
            piece(o_ref.at[blk, p], blk, p, mate, 2).wait_send()

            @pl.when(jnp.logical_and(has_right, j <= k))
            def _():
                piece(o_ref.at[blk, p], blk, p, right, 1).wait_send()

            @pl.when(jnp.logical_and(has_left, j >= k))
            def _():
                piece(o_ref.at[blk, p], blk, p, left, 0).wait_send()
    own.wait()
    for d in range(1, blks):
        slab(d).wait_send()
    for d in range(1, seqs):
        group(d).wait()


def entry(hidden, slabs, seqs, blks, parts):
    rows, width = hidden.shape
    dma = pltpu.SemaphoreType.DMA
    return pl.pallas_call(
        functools.partial(entry_kernel, seqs, blks, parts),
        name="entry",
        out_shape=(
            jax.ShapeDtypeStruct((blks, parts, rows // parts, width), LOW),
            jax.ShapeDtypeStruct((seqs,) + slabs.shape, LOW),
        ),
        in_specs=[spec(pltpu.VMEM)] * 2,
        out_specs=(spec(ANY), spec(ANY)),
        scratch_shapes=[
            dma, dma((3, blks, parts)), dma((blks, parts)), dma,
            dma((blks,)), dma((blks,)), dma((seqs,)), dma((seqs,)),
        ],
        compiler_params=pltpu.CompilerParams(collective_id=0, has_side_effects=True),
        cost_estimate=pl.CostEstimate(flops=0, transcendentals=0, bytes_accessed=200 * 10**6),
    )(hidden.reshape(parts, rows // parts, width), slabs)


def return_kernel(blks, nat_ref, pack_ref, even_ref, odd_ref, buf, lsem, ssem, rsem):
    b = lax.axis_index("blk")
    k = b // 2
    c = lax.rem(b, 2)
    greet([{"blk": lax.rem(b + d, blks)} for d in range(1, blks)])
    start_return(blks, b, k, c, nat_ref, pack_ref, even_ref, odd_ref, buf, lsem, ssem, rsem)
    finish_return(blks, b, k, c, nat_ref, pack_ref, even_ref, odd_ref, ssem, rsem)


def full_way(blks, b, d, nat_ref, even_ref, ssem, rsem, slot):
    peer = lax.rem(b + d, blks)
    return send(nat_ref.at[peer], even_ref.at[slot], ssem.at[d], rsem.at[d], {"blk": peer})


def start_return(blks, b, k, c, nat_ref, pack_ref, even_ref, odd_ref, buf, lsem, ssem, rsem):
    @pl.when(c == 0)
    def _():
        for d in range(1, blks):
            full_way(blks, b, d, nat_ref, even_ref, ssem, rsem, k).start()
        inward = pltpu.make_async_copy(nat_ref.at[b], buf, lsem)
        inward.start()
        inward.wait()
        outward = pltpu.make_async_copy(buf, even_ref.at[k], lsem)
        outward.start()
        outward.wait()

    @pl.when(c == 1)
    def _():
        for d in range(1, blks):
            full_way(blks, b, d, pack_ref, odd_ref, ssem, rsem, k).start()
        part = buf.at[pl.ds(0, pack_ref.shape[1])]
        inward = pltpu.make_async_copy(pack_ref.at[b], part, lsem)
        inward.start()
        inward.wait()
        outward = pltpu.make_async_copy(part, odd_ref.at[k], lsem)
        outward.start()
        outward.wait()


def finish_return(blks, b, k, c, nat_ref, pack_ref, even_ref, odd_ref, ssem, rsem):
    for d in range(1, blks):
        source = lax.rem(b + blks - d, blks)

        @pl.when(lax.rem(source, 2) == 0)
        def _():
            full_way(blks, b, d, nat_ref, even_ref, ssem, rsem, source // 2).wait_recv()

        @pl.when(lax.rem(source, 2) == 1)
        def _():
            full_way(blks, b, d, pack_ref, odd_ref, ssem, rsem, source // 2).wait_recv()

    @pl.when(c == 0)
    def _():
        for d in range(1, blks):
            full_way(blks, b, d, nat_ref, even_ref, ssem, rsem, k).wait_send()

    @pl.when(c == 1)
    def _():
        for d in range(1, blks):
            full_way(blks, b, d, pack_ref, odd_ref, ssem, rsem, k).wait_send()


def return_rows(nat, pack, collective_id):
    blks = nat.shape[0]
    dma = pltpu.SemaphoreType.DMA
    return pl.pallas_call(
        functools.partial(return_kernel, blks),
        name="return_rows",
        out_shape=(
            jax.ShapeDtypeStruct((blks // 2,) + nat.shape[1:], LOW),
            jax.ShapeDtypeStruct((blks // 2,) + pack.shape[1:], LOW),
        ),
        in_specs=[spec(ANY)] * 2,
        out_specs=(spec(ANY), spec(ANY)),
        scratch_shapes=[pltpu.VMEM(nat.shape[1:], LOW), dma, dma((blks,)), dma((blks,))],
        compiler_params=pltpu.CompilerParams(collective_id=collective_id, has_side_effects=True),
        cost_estimate=pl.CostEstimate(flops=0, transcendentals=0, bytes_accessed=80 * 10**6),
    )(nat, pack)


def spread_kernel(blks, even_ref, odd_ref, nat_ref, pack_ref, buf, lsem, ssem, rsem):
    b = lax.axis_index("blk")
    c = lax.rem(b, 2)
    greet([{"blk": lax.rem(b + d, blks)} for d in range(1, blks)])

    def full(d, slot):
        peer = lax.rem(b + d, blks)
        return send(
            even_ref.at[peer // 2], nat_ref.at[slot], ssem.at[d], rsem.at[d], {"blk": peer}
        )

    def packed(d, slot):
        peer = lax.rem(b + d, blks)
        return send(
            odd_ref.at[peer // 2], pack_ref.at[slot], ssem.at[d], rsem.at[d], {"blk": peer}
        )

    for d in range(1, blks):
        to_even = lax.rem(b + d, 2) == 0

        @pl.when(to_even)
        def _():
            full(d, b).start()

        @pl.when(jnp.logical_not(to_even))
        def _():
            packed(d, b).start()

    @pl.when(c == 0)
    def _():
        inward = pltpu.make_async_copy(even_ref.at[b // 2], buf, lsem)
        inward.start()
        inward.wait()
        outward = pltpu.make_async_copy(buf, nat_ref.at[b], lsem)
        outward.start()
        outward.wait()
        for d in range(1, blks):
            full(d, lax.rem(b + blks - d, blks)).wait_recv()

    @pl.when(c == 1)
    def _():
        part = buf.at[pl.ds(0, odd_ref.shape[1])]
        inward = pltpu.make_async_copy(odd_ref.at[b // 2], part, lsem)
        inward.start()
        inward.wait()
        outward = pltpu.make_async_copy(part, pack_ref.at[b], lsem)
        outward.start()
        outward.wait()
        for d in range(1, blks):
            packed(d, lax.rem(b + blks - d, blks)).wait_recv()

    for d in range(1, blks):
        to_even = lax.rem(b + d, 2) == 0

        @pl.when(to_even)
        def _():
            full(d, b).wait_send()

        @pl.when(jnp.logical_not(to_even))
        def _():
            packed(d, b).wait_send()


def spread_rows(even, odd, collective_id):
    blks = 2 * even.shape[0]
    dma = pltpu.SemaphoreType.DMA
    return pl.pallas_call(
        functools.partial(spread_kernel, blks),
        name="spread_rows",
        out_shape=(
            jax.ShapeDtypeStruct((blks,) + even.shape[1:], LOW),
            jax.ShapeDtypeStruct((blks,) + odd.shape[1:], LOW),
        ),
        in_specs=[spec(ANY)] * 2,
        out_specs=(spec(ANY), spec(ANY)),
        scratch_shapes=[pltpu.VMEM(even.shape[1:], LOW), dma, dma((blks,)), dma((blks,))],
        compiler_params=pltpu.CompilerParams(collective_id=collective_id, has_side_effects=True),
        cost_estimate=pl.CostEstimate(flops=0, transcendentals=0, bytes_accessed=80 * 10**6),
    )(even, odd)


def exit_kernel(
    seqs, blks, nat_ref, pack_ref, grad_ref, even_ref, odd_ref, out_ref,
    buf, stage, total, lsem, ssem, rsem, us, ur, gl, gs, gr,
):
    s = lax.axis_index("seq")
    b = lax.axis_index("blk")
    k = b // 2
    c = lax.rem(b, 2)
    blk_peers = [{"blk": lax.rem(b + d, blks)} for d in range(1, blks)]
    seq_peers = [{"seq": lax.rem(s + d, seqs)} for d in range(1, seqs)]
    greet(blk_peers + seq_peers)

    def group(d):
        peer = lax.rem(s + d, seqs)
        return send(grad_ref.at[peer], stage.at[d], us.at[d], ur.at[d], {"seq": peer})

    def slab(d):
        peer = lax.rem(b + d, blks)
        return send(total.at[peer], out_ref.at[b], gs.at[d], gr.at[d], {"blk": peer})

    for d in range(1, seqs):
        group(d).start()
    start_return(blks, b, k, c, nat_ref, pack_ref, even_ref, odd_ref, buf, lsem, ssem, rsem)
    for d in range(1, seqs):
        group(d).wait_recv()
    for o in range(blks):
        acc = grad_ref[s, o].astype(F32)
        for d in range(1, seqs):
            acc = acc + stage[d, o].astype(F32)
        total[o] = acc.astype(LOW)
    for d in range(1, blks):
        slab(d).start()
    own = pltpu.make_async_copy(total.at[b], out_ref.at[b], gl)
    own.start()
    own.wait()
    finish_return(blks, b, k, c, nat_ref, pack_ref, even_ref, odd_ref, ssem, rsem)
    for d in range(1, blks):
        slab(d).wait()
    for d in range(1, seqs):
        group(d).wait_send()


def leave(nat, pack, grads):
    blks = nat.shape[0]
    seqs = grads.shape[0]
    dma = pltpu.SemaphoreType.DMA
    return pl.pallas_call(
        functools.partial(exit_kernel, seqs, blks),
        name="leave",
        out_shape=(
            jax.ShapeDtypeStruct((blks // 2,) + nat.shape[1:], LOW),
            jax.ShapeDtypeStruct((blks // 2,) + pack.shape[1:], LOW),
            jax.ShapeDtypeStruct(grads.shape[1:], LOW),
        ),
        in_specs=[spec(ANY), spec(ANY), spec(pltpu.VMEM)],
        out_specs=(spec(ANY), spec(ANY), spec(ANY)),
        scratch_shapes=[
            pltpu.VMEM(nat.shape[1:], LOW),
            pltpu.VMEM(grads.shape, LOW),
            pltpu.VMEM(grads.shape[1:], LOW),
            dma, dma((blks,)), dma((blks,)), dma((seqs,)), dma((seqs,)),
            dma, dma((blks,)), dma((blks,)),
        ],
        compiler_params=pltpu.CompilerParams(collective_id=3, has_side_effects=True),
        cost_estimate=pl.CostEstimate(flops=0, transcendentals=0, bytes_accessed=200 * 10**6),
    )(nat, pack, grads)


def lane_of(rows):
    return lax.broadcasted_iota(jnp.int32, (rows, 128), 1)


def low_lanes(value, slot, hd):
    lane = lane_of(value.shape[0])
    keep = jnp.logical_and(lane >= slot * hd, lane < (slot + 1) * hd)
    return jnp.where(keep, value, 0.0).astype(LOW)


def attend_kernel(
    hd, scale, order, count, hid, weight, bias, proj, nat, pack, rows4, take, mix, back
):
    length = hid.shape[0]
    step = nat.shape[1]

    @pl.loop(0, length // step)
    def _(i):
        at = pl.multiple_of(i * step, step)
        low = (nn_dot(hid[pl.ds(at, step), :], weight[...]) + bias[...]).astype(LOW)
        proj[pl.ds(at, step), :] = low
        wide = low.astype(F32)
        for t in range(3):
            rows4[pl.ds(at, step), t, :] = wide[:, t * 128 : (t + 1) * 128]

    span = GROUP * 128

    @pl.loop(0, count[0])
    def _(slot):
        @pl.loop(0, length // span)
        def _(i):
            base = slot * length + i * span
            for j in range(span):
                take[j] = rows4[order[base + j]]
            for u in range(GROUP):
                own = pl.ds(u * 128, 128)
                query = low_lanes(take[own, 0, :], slot, hd)
                scores = nt_dot(query, take[own, 1, :].astype(LOW)) * scale
                weights = jnp.exp(scores - jnp.max(scores, axis=-1, keepdims=True))
                probs = weights / jnp.sum(weights, axis=-1, keepdims=True)
                mix[own, :] = nn_dot(probs.astype(LOW), take[own, 2, :].astype(LOW))
            for j in range(span):
                back[pl.ds(slot * length + order[base + j], 1), :] = mix[pl.ds(j, 1), :]

    lane = lane_of(step)

    @pl.when(count[0] == 2)
    def _():
        @pl.loop(0, length // step)
        def _(i):
            at = pl.multiple_of(i * step, step)
            nat[i] = jnp.where(
                lane < hd, back[pl.ds(at, step), :], back[pl.ds(length + at, step), :]
            ).astype(LOW)

    half = step // 2

    @pl.when(count[0] == 1)
    def _():
        @pl.loop(0, length // step)
        def _(i):
            at = pl.multiple_of(i * step, step)
            upper = pltpu.roll(back[pl.ds(at + half, half), :], hd, 1)
            pack[i] = jnp.where(lane[:half] < hd, back[pl.ds(at, half), :], upper).astype(LOW)


def attend(order, count, hid, weight, bias, blks, hd, scale):
    length = hid.shape[0]
    step = length // blks
    return pl.pallas_call(
        functools.partial(attend_kernel, hd, scale),
        name="attend",
        out_shape=(
            jax.ShapeDtypeStruct((length, 384), LOW),
            jax.ShapeDtypeStruct((blks, step, 128), LOW),
            jax.ShapeDtypeStruct((blks, step // 2, 128), LOW),
        ),
        in_specs=[spec(pltpu.SMEM), spec(pltpu.SMEM)] + [spec(pltpu.VMEM)] * 3,
        out_specs=(spec(pltpu.VMEM),) * 3,
        scratch_shapes=[
            pltpu.VMEM((length, 4, 128), F32),
            pltpu.VMEM((GROUP * 128, 4, 128), F32),
            pltpu.VMEM((GROUP * 128, 128), F32),
            pltpu.VMEM((2 * length, 128), F32),
        ],
        compiler_params=pltpu.CompilerParams(vmem_limit_bytes=BIG),
        cost_estimate=pl.CostEstimate(
            flops=5 * 10**9, transcendentals=0, bytes_accessed=100 * 10**6
        ),
    )(order, count, hid, weight, bias)


def attend_back_kernel(
    hd, scale, order, count, hidden_hbm, proj, gnat, gpack, extra, znat, zpack, slabs,
    rows4, take, out4, back4, hid, wide_grad, sem,
):
    length = proj.shape[0]
    step = gnat.shape[1]
    half = step // 2
    fetch = pltpu.make_async_copy(hidden_hbm, hid, sem)
    fetch.start()

    @pl.loop(0, length // step)
    def _(i):
        at = pl.multiple_of(i * step, step)
        wide = proj[pl.ds(at, step), :].astype(F32)
        for t in range(3):
            rows4[pl.ds(at, step), t, :] = wide[:, t * 128 : (t + 1) * 128]

        @pl.when(count[0] == 2)
        def _():
            rows4[pl.ds(at, step), 3, :] = gnat[i].astype(F32)

        @pl.when(count[0] == 1)
        def _():
            pair = gpack[i].astype(F32)
            rows4[pl.ds(at, half), 3, :] = pair
            rows4[pl.ds(at + half, half), 3, :] = pltpu.roll(pair, hd, 1)

    span = GROUP * 128

    @pl.loop(0, count[0])
    def _(slot):
        @pl.loop(0, length // span)
        def _(i):
            base = slot * length + i * span
            for j in range(span):
                take[j] = rows4[order[base + j]]
            for u in range(GROUP):
                own = pl.ds(u * 128, 128)
                query = low_lanes(take[own, 0, :], slot, hd)
                grad = low_lanes(take[own, 3, :], slot, hd)
                keys = take[own, 1, :].astype(LOW)
                scores = nt_dot(query, keys) * scale
                weights = jnp.exp(scores - jnp.max(scores, axis=-1, keepdims=True))
                probs = weights / jnp.sum(weights, axis=-1, keepdims=True)
                prob_grad = nt_dot(grad, take[own, 2, :].astype(LOW))
                shift = jnp.sum(probs * prob_grad, axis=-1, keepdims=True)
                score_low = (probs * (prob_grad - shift)).astype(LOW)
                out4[own, 0, :] = nn_dot(score_low, keys) * scale
                out4[own, 1, :] = tn_dot(score_low, query) * scale
                out4[own, 2, :] = tn_dot(probs.astype(LOW), grad)
            for j in range(span):
                back4[slot * length + order[base + j]] = out4[j]

    lane = lane_of(step)
    fetch.wait()
    wide_grad[...] = jnp.zeros_like(wide_grad)
    zero = jnp.zeros((1, 384), F32)

    def settle(i, sums):
        at = pl.multiple_of(i * step, step)
        parts = []
        for t in range(3):
            cols = pl.ds(t * 128, 128)
            first = back4[pl.ds(at, step), t, :]
            second = back4[pl.ds(length + at, step), t, :]
            second = jnp.where(count[0] == 2, second, jnp.zeros_like(second))
            low = jnp.where(lane < hd, first, second).astype(LOW)
            znat[i, :, cols] = low
            wide = low.astype(F32)
            parts.append(jnp.sum(wide, axis=0, keepdims=True))
            zpack[i, :, cols] = (wide[:half] + pltpu.roll(wide[half:], hd, 1)).astype(LOW)
        wide_grad[...] += tn_dot(hid[pl.ds(at, step), :], znat[i])
        return sums + jnp.concatenate(parts, axis=1)

    sums = lax.fori_loop(0, length // step, settle, zero)
    devices = slabs.shape[0]
    own = hid.shape[1] // devices
    lane8 = lane_of(8)
    row8 = lax.broadcasted_iota(jnp.int32, (8, 128), 0)
    first_col = count[1]
    limit = count[2]
    q_row = jnp.broadcast_to(sums[:, :128], (8, 128))
    v_row = jnp.broadcast_to(sums[:, 256:], (8, 128))
    for i in range(devices):
        begin = i * own - first_col
        q_lane = lane8 + begin
        v_lane = q_lane - 64
        q_part = pltpu.roll(q_row, lax.rem(4096 - begin, 128), 1)
        v_part = pltpu.roll(v_row, lax.rem(4096 - begin + 64, 128), 1)
        q_ok = (lane8 < own) & (q_lane >= 0) & (q_lane < limit)
        v_ok = (lane8 >= 64) & (lane8 < 64 + own) & (v_lane >= 0) & (v_lane < limit)
        line = jnp.where(q_ok, q_part, jnp.where(v_ok, v_part, 0.0))
        tile = jnp.where(row8 == 0, line, extra[i])
        tail = jnp.concatenate([tile, jnp.zeros((8, 256), F32)], axis=1)
        at = i * own
        slabs[i, : own - 8, :] = wide_grad[at : at + own - 8, :].astype(LOW)
        slabs[i, own - 8 :, :] = jnp.concatenate(
            [wide_grad[at + own - 8 : at + own, :], tail], axis=0
        ).astype(LOW)


def attend_back(order, count, hidden_all, proj, gnat, gpack, extra, hd, scale):
    length = proj.shape[0]
    blks, step, _ = gnat.shape
    devices = extra.shape[0]
    width = hidden_all.shape[1]
    return pl.pallas_call(
        functools.partial(attend_back_kernel, hd, scale),
        name="attend_back",
        out_shape=(
            jax.ShapeDtypeStruct((blks, step, 384), LOW),
            jax.ShapeDtypeStruct((blks, step // 2, 384), LOW),
            jax.ShapeDtypeStruct((devices, width // devices + 8, 384), LOW),
        ),
        in_specs=[spec(pltpu.SMEM), spec(pltpu.SMEM), spec(ANY)] + [spec(pltpu.VMEM)] * 4,
        out_specs=(spec(pltpu.VMEM),) * 3,
        scratch_shapes=[
            pltpu.VMEM((length, 4, 128), F32),
            pltpu.VMEM((GROUP * 128, 4, 128), F32),
            pltpu.VMEM((GROUP * 128, 4, 128), F32),
            pltpu.VMEM((2 * length, 4, 128), F32),
            pltpu.VMEM(hidden_all.shape, LOW),
            pltpu.VMEM((width, 384), F32),
            pltpu.SemaphoreType.DMA,
        ],
        compiler_params=pltpu.CompilerParams(vmem_limit_bytes=BIG),
        cost_estimate=pl.CostEstimate(
            flops=8 * 10**9, transcendentals=0, bytes_accessed=120 * 10**6
        ),
    )(order, count, hidden_all, proj, gnat, gpack, extra)


def middle_kernel(
    hd, ceven, codd, hidden, first_hbm, outer_hbm, vecs, bias_inner, cot, mask,
    hout, resid, geven, godd, merged, extra,
    wa, wb, ctx, act, slope, ilow, first, flow, olow, unit, acc, hid_low, sums, inner_sums, sems,
):
    rows, width = hidden.shape
    ff = outer_hbm.shape[0]
    chips = ceven.shape[0]
    get_out = pltpu.make_async_copy(
        first_hbm.at[:, pl.ds(0, width)], wa.at[:, pl.ds(0, width)], sems.at[0]
    )
    get_in = pltpu.make_async_copy(
        first_hbm.at[:, pl.ds(width, ff)], wa.at[:, pl.ds(width, ff)], sems.at[1]
    )
    get_outer = pltpu.make_async_copy(outer_hbm, wb, sems.at[2])
    get_out.start()
    get_in.start()
    get_outer.start()
    half = rows // 2
    lane = lane_of(half)
    low_half = lane < hd
    for z in range(chips):
        ctx[:, z * 128 : (z + 1) * 128] = ceven[z]
    for z in range(0, chips, 2):
        here = codd[z].astype(F32)
        there = codd[z + 1].astype(F32)
        at = chips * 128 + z * 64
        ctx[:half, at : at + 128] = jnp.where(low_half, here, pltpu.roll(there, hd, 1)).astype(LOW)
        ctx[half:, at : at + 128] = jnp.where(low_half, pltpu.roll(here, hd, 1), there).astype(LOW)
    sums[...] = jnp.zeros_like(sums)
    wide = 256
    tile = 64

    def add_rows(row, value):
        sums[row : row + 1, :] += jnp.sum(value, axis=0, keepdims=True)

    get_out.wait()

    @pl.loop(0, width // wide)
    def _(n):
        at = pl.multiple_of(n * wide, wide)
        acc[:, pl.ds(at, wide)] = nn_dot(ctx[...], wa[:, pl.ds(at, wide)])

    @pl.loop(0, rows // tile)
    def _(i):
        own = pl.ds(pl.multiple_of(i * tile, tile), tile)
        value = hidden[own, :].astype(F32) + acc[own, :] + vecs[2:3, :]
        center = value - jnp.mean(value, axis=-1, keepdims=True)
        spread = jnp.mean(center * center, axis=-1, keepdims=True)
        inv = lax.rsqrt(spread + epsilon)
        norm = center * inv * vecs[3:4, :] + vecs[4:5, :]
        first[own, :] = norm
        flow[own, :] = norm.astype(LOW)
        unit[own, :] = center * inv
        resid[own, 0:128] = jnp.broadcast_to(inv, (tile, 128))

    get_in.wait()

    @pl.loop(0, ff // wide)
    def _(j):
        at = pl.multiple_of(j * wide, wide)
        cols = pl.ds(at, wide)
        pre = nn_dot(flow[...], wa[:, pl.ds(width + at, wide)]) + bias_inner[0:1, cols]
        gate = 0.5 + 0.5 * lax.erf(pre * (0.5**0.5))
        act[:, cols] = (pre * gate).astype(LOW)
        slope[:, cols] = gate + pre * jnp.exp(-0.5 * pre * pre) * (0.5 / math.pi) ** 0.5

    get_outer.wait()

    @pl.loop(0, width // wide)
    def _(n):
        at = pl.multiple_of(n * wide, wide)
        acc[:, pl.ds(at, wide)] = nn_dot(act[...], wb[:, pl.ds(at, wide)])

    @pl.loop(0, rows // tile)
    def _(i):
        own = pl.ds(pl.multiple_of(i * tile, tile), tile)
        value = first[own, :] + acc[own, :] + vecs[5:6, :]
        center = value - jnp.mean(value, axis=-1, keepdims=True)
        spread = jnp.mean(center * center, axis=-1, keepdims=True)
        inv = lax.rsqrt(spread + epsilon)
        norm = center * inv
        hout[own, :] = (norm * vecs[6:7, :] + vecs[7:8, :]).astype(LOW)
        out_grad = cot[own, :].astype(F32) * mask[own, :].astype(F32)
        pull = out_grad * vecs[6:7, :]
        pull = pull - jnp.mean(pull, axis=-1, keepdims=True) - norm * jnp.mean(
            pull * norm, axis=-1, keepdims=True
        )
        grad = pull * inv
        low = grad.astype(LOW)
        first[own, :] = grad
        olow[own, :] = low
        add_rows(4, low.astype(F32))
        add_rows(5, out_grad * norm)
        add_rows(6, out_grad)

    @pl.loop(0, ff // wide)
    def _(j):
        cols = pl.ds(pl.multiple_of(j * wide, wide), wide)
        low = (nt_dot(olow[...], wb[cols, :]) * slope[:, cols]).astype(LOW)
        ilow[:, cols] = low
        inner_sums[0:1, cols] = jnp.sum(low.astype(F32), axis=0, keepdims=True)

    @pl.loop(0, width // wide)
    def _(n):
        at = pl.multiple_of(n * wide, wide)
        acc[:, pl.ds(at, wide)] = nt_dot(ilow[...], wa[pl.ds(at, wide), width:])

    @pl.loop(0, rows // tile)
    def _(i):
        own = pl.ds(pl.multiple_of(i * tile, tile), tile)
        grad = acc[own, :] + first[own, :]
        norm = unit[own, :]
        inv = resid[own, 0:1]
        pull = grad * vecs[3:4, :]
        pull = pull - jnp.mean(pull, axis=-1, keepdims=True) - norm * jnp.mean(
            pull * norm, axis=-1, keepdims=True
        )
        back = pull * inv
        low = back.astype(LOW)
        resid[own, :] = back
        hid_low[own, :] = low
        add_rows(1, low.astype(F32))
        add_rows(2, grad * norm)
        add_rows(3, grad)

    @pl.loop(0, width // wide)
    def _(n):
        at = pl.multiple_of(n * wide, wide)
        acc[:, pl.ds(at, wide)] = nt_dot(hid_low[...], wa[pl.ds(at, wide), :width])

    for z in range(chips):
        geven[z] = acc[:, z * 128 : (z + 1) * 128].astype(LOW)
    for z in range(0, chips, 2):
        at = chips * 128 + z * 64
        top = acc[:half, at : at + 128]
        bottom = acc[half:, at : at + 128]
        godd[z] = jnp.where(low_half, top, pltpu.roll(bottom, hd, 1)).astype(LOW)
        godd[z + 1] = jnp.where(low_half, pltpu.roll(top, hd, 1), bottom).astype(LOW)

    devices = merged.shape[0]
    own_rows = width // devices
    outer_rows = ff // devices
    block = 384
    per = block // outer_rows

    @pl.loop(0, ff // block)
    def _(j):
        part = tn_dot(act[:, pl.ds(pl.multiple_of(j * block, block), block)], olow[...])
        for i in range(per):
            merged[j * per + i, :outer_rows, :] = part[
                i * outer_rows : (i + 1) * outer_rows, :
            ].astype(LOW)

    folds = ff // width
    many = block // own_rows

    @pl.loop(0, width // block)
    def _(m):
        cols = pl.ds(pl.multiple_of(m * block, block), block)
        for h in range(0, folds, 2):
            left = tn_dot(flow[:, cols], ilow[:, h * width : (h + 1) * width])
            right = tn_dot(flow[:, cols], ilow[:, (h + 1) * width : (h + 2) * width])
            at = outer_rows + h * own_rows
            for i in range(many):
                for r in range(0, own_rows, 8):
                    base = i * own_rows + r
                    merged[m * many + i, at + 2 * r : at + 2 * r + 16, :] = jnp.concatenate(
                        [left[base : base + 8, :], right[base : base + 8, :]], axis=0
                    ).astype(LOW)
        part = tn_dot(ctx[:, cols], hid_low[...])
        at = outer_rows + folds * own_rows
        for i in range(many):
            base = i * own_rows
            merged[m * many + i, at : at + 16, :] = part[base : base + 16, :].astype(LOW)
            merged[m * many + i, at + 16 : at + 32, :] = jnp.concatenate(
                [part[base + 16 : base + 24, :], jnp.zeros((8, width), F32)], axis=0
            ).astype(LOW)

    row8 = lax.broadcasted_iota(jnp.int32, (8, 128), 0)
    for i in range(devices):
        piece = sums[:, i * own_rows : (i + 1) * own_rows]
        piece = jnp.concatenate([piece, jnp.zeros((8, 128 - own_rows), F32)], axis=1)
        inner = inner_sums[0:1, i * outer_rows : (i + 1) * outer_rows]
        inner = jnp.concatenate([inner, jnp.zeros((1, 128 - outer_rows), F32)], axis=1)
        extra[i] = jnp.where(row8 == 7, jnp.broadcast_to(inner, (8, 128)), piece)


def middle(ceven, codd, hidden, first_half, outer_full, vecs, bias_inner, cot, mask, devices, hd):
    rows, width = hidden.shape
    ff = outer_full.shape[0]
    slab = ff // devices + (ff // width + 1) * (width // devices) + 8
    wide_low = pltpu.VMEM((rows, width), LOW)
    wide_f32 = pltpu.VMEM((rows, width), F32)
    return pl.pallas_call(
        functools.partial(middle_kernel, hd),
        name="middle",
        out_shape=(
            jax.ShapeDtypeStruct((rows, width), LOW),
            jax.ShapeDtypeStruct((rows, width), F32),
            jax.ShapeDtypeStruct(ceven.shape, LOW),
            jax.ShapeDtypeStruct(codd.shape, LOW),
            jax.ShapeDtypeStruct((devices, slab, width), LOW),
            jax.ShapeDtypeStruct((devices, 8, 128), F32),
        ),
        in_specs=[spec(pltpu.VMEM)] * 3 + [spec(ANY)] * 2 + [spec(pltpu.VMEM)] * 4,
        out_specs=(spec(pltpu.VMEM),) * 6,
        scratch_shapes=[
            pltpu.VMEM(first_half.shape, LOW),
            pltpu.VMEM(outer_full.shape, LOW),
            wide_low,
            pltpu.VMEM((rows, ff), LOW),
            pltpu.VMEM((rows, ff), F32),
            pltpu.VMEM((rows, ff), LOW),
            wide_f32, wide_low, wide_low, wide_f32, wide_f32, wide_low,
            pltpu.VMEM((8, width), F32),
            pltpu.VMEM((8, ff), F32),
            pltpu.SemaphoreType.DMA((3,)),
        ],
        compiler_params=pltpu.CompilerParams(vmem_limit_bytes=BIG),
        cost_estimate=pl.CostEstimate(
            flops=17 * 10**9, transcendentals=0, bytes_accessed=40 * 10**6
        ),
    )(ceven, codd, hidden, first_half, outer_full, vecs, bias_inner, cot, mask)


def final_kernel(
    hd, zeven, zodd, proj_hbm, resid, proj_grads, share,
    out, gq, gk, gv, go, gi, gu, g0, g1, g2, g3, g4, g5, g6, g7, g8, wp, triple, sem,
):
    rows, width = resid.shape
    chips = zeven.shape[0]
    fetch = pltpu.make_async_copy(proj_hbm, wp, sem)
    fetch.start()
    half = rows // 2
    low_half = lane_of(half) < hd
    for t in range(3):
        cols = slice(t * 128, (t + 1) * 128)
        for z in range(chips):
            at = t * width + z * 128
            triple[:, at : at + 128] = zeven[z, :, cols]
        for z in range(0, chips, 2):
            at = t * width + chips * 128 + z * 64
            here = zodd[z, :, cols].astype(F32)
            there = zodd[z + 1, :, cols].astype(F32)
            triple[:half, at : at + 128] = jnp.where(
                low_half, here, pltpu.roll(there, hd, 1)
            ).astype(LOW)
            triple[half:, at : at + 128] = jnp.where(
                low_half, pltpu.roll(here, hd, 1), there
            ).astype(LOW)
    own = gq.shape[0]
    keep = lane_of(own) < hd
    for t, ref in enumerate((gq, gk, gv)):
        cols = slice(t * 128, (t + 1) * 128)
        for z in range(chips):
            ref[:, z * 128 : (z + 1) * 128] = proj_grads[2 * z, :, cols].astype(F32)[:own]
        for z in range(0, chips, 2):
            here = proj_grads[2 * z + 1, :, cols].astype(F32)[:own]
            there = proj_grads[2 * z + 3, :, cols].astype(F32)[:own]
            at = chips * 128 + z * 64
            ref[:, at : at + 128] = jnp.where(keep, here, pltpu.roll(there, hd, 1))
    ff = gi.shape[1]
    outer_rows = gu.shape[0]
    folds = ff // width
    gu[...] = share[:outer_rows, :].astype(F32)
    for h in range(0, folds, 2):
        at = outer_rows + h * own
        for r in range(0, own, 8):
            pair = share[at + 2 * r : at + 2 * r + 16, :].astype(F32)
            gi[r : r + 8, h * width : (h + 1) * width] = pair[:8]
            gi[r : r + 8, (h + 1) * width : (h + 2) * width] = pair[8:]
    at = outer_rows + folds * own
    go[...] = share[at : at + own + 8, :].astype(F32)[:own]
    total = proj_grads[0, :, :128].astype(F32)[own:]
    for d in range(1, 2 * chips):
        total = total + proj_grads[d, :, :128].astype(F32)[own:]
    g0[...] = total[0, :own]
    g1[...] = total[0, 64 : 64 + own]
    for v, ref in enumerate((g2, g3, g4)):
        ref[...] = total[1 + v, :own]
    g5[...] = total[7, : g5.shape[0]]
    for v, ref in enumerate((g6, g7, g8)):
        ref[...] = total[4 + v, :own]
    fetch.wait()
    wide = 256

    @pl.loop(0, width // wide)
    def _(n):
        at = pl.multiple_of(n * wide, wide)
        cols = pl.ds(at, wide)
        out[:, cols] = nt_dot(triple[...], wp[pl.ds(at, wide), :]) + resid[:, cols]


def final(zeven, zodd, projections, resid, proj_grads, share, own, ff, hd):
    rows, width = resid.shape
    mats = [(rows, width)] + [(own, width)] * 4 + [(own, ff), (ff * own // width, width)]
    vectors = [(own,)] * 5 + [(ff * own // width,)] + [(own,)] * 3
    return pl.pallas_call(
        functools.partial(final_kernel, hd),
        name="final",
        out_shape=tuple(jax.ShapeDtypeStruct(shape, F32) for shape in mats + vectors),
        in_specs=[spec(pltpu.VMEM)] * 2 + [spec(ANY)] + [spec(pltpu.VMEM)] * 3,
        out_specs=(spec(pltpu.VMEM),) * 16,
        scratch_shapes=[
            pltpu.VMEM(projections.shape, LOW),
            pltpu.VMEM((rows, 3 * width), LOW),
            pltpu.SemaphoreType.DMA,
        ],
        compiler_params=pltpu.CompilerParams(vmem_limit_bytes=BIG),
        cost_estimate=pl.CostEstimate(
            flops=2 * 10**9, transcendentals=0, bytes_accessed=12 * 10**6
        ),
    )(zeven, zodd, projections, resid, proj_grads, share)


def by_device(value, chips, hd):
    rows = value.shape[0]
    wide = chips * 2 * hd
    even = value[:, :wide].reshape(rows, chips, 2 * hd).transpose(1, 0, 2)
    odd = value[:, wide:].reshape(rows, chips, hd).transpose(1, 0, 2)
    odd = jnp.pad(odd, ((0, 0), (0, 0), (0, hd)))
    return jnp.stack([even, odd], axis=1).reshape(2 * chips, rows, 2 * hd)


def fast_body(seqs, blks, heads):
    def run(
        hidden_in, query_weight, key_weight, value_weight, output_weight, inner_weight,
        outer_weight, query_bias, value_bias, output_bias, attention_gain, attention_shift,
        inner_bias, outer_bias, final_gain, final_shift, cotangent, grad_mask, cluster_order,
    ):
        rows, width = hidden_in.shape
        own = query_weight.shape[0]
        hidden_units = inner_weight.shape[1]
        length = cluster_order.shape[2]
        hd = width // heads
        chips = blks // 2
        scale = 1.0 / math.sqrt(hd)
        devices = seqs * blks
        b = lax.axis_index("blk")
        k = b // 2
        even_core = lax.rem(b, 2) == 0
        query_low, key_low, value_low, output_low, inner_low_w, outer_low_w = [
            w.astype(LOW)
            for w in (
                query_weight, key_weight, value_weight, output_weight, inner_weight, outer_weight,
            )
        ]
        small = jnp.concatenate(
            [
                query_bias, value_bias, output_bias, attention_gain, attention_shift,
                outer_bias, final_gain, final_shift, inner_bias,
            ]
        ).astype(LOW)
        slabs = jnp.concatenate(
            [by_device(w, chips, hd) for w in (query_low, key_low, value_low)], axis=2
        )
        extra = jnp.pad(small[None, :], ((0, 7), (0, 384 - small.shape[0])))
        slabs = jnp.concatenate(
            [slabs, jnp.broadcast_to(extra[None], (blks,) + extra.shape)], axis=1
        )
        axes = ("seq", "blk")
        first_half = lax.all_gather(
            jnp.concatenate([output_low, inner_low_w], axis=1), axes, axis=0, tiled=True
        )
        outer_full = lax.all_gather(outer_low_w, axes, axis=0, tiled=True)
        projections = lax.all_gather(
            jnp.concatenate([query_low, key_low, value_low], axis=1), axes, axis=0, tiled=True
        )
        hidden_all, gathered = entry(hidden_in, slabs, seqs, blks, 2)
        hidden_all = hidden_all.reshape(length, width)
        gathered = gathered.reshape(devices, own + 8, 384)
        weight_own = gathered[:, :own].reshape(width, 384)
        vec = gathered[:, own, : small.shape[0]]
        vecs = (
            vec[:, : 8 * own].reshape(devices, 8, own).transpose(1, 0, 2).reshape(8, width)
        ).astype(F32)
        bias_inner = vec[:, 8 * own :].reshape(1, hidden_units).astype(F32)
        bias_query, bias_value = [
            by_device(vecs[i : i + 1], chips, hd) for i in (0, 1)
        ]
        bias_own = lax.dynamic_index_in_dim(
            jnp.concatenate([bias_query, jnp.zeros_like(bias_query), bias_value], axis=2),
            b, 0, keepdims=False,
        )
        order = cluster_order[0]
        head_first = jnp.where(even_core, 2 * k, 2 * chips + k)
        order_own = jnp.concatenate(
            [
                lax.dynamic_index_in_dim(order, head_first, 0, keepdims=False),
                lax.dynamic_index_in_dim(order, 2 * k + 1, 0, keepdims=False),
            ]
        )
        count = jnp.stack(
            [
                jnp.where(even_core, 2, 1),
                jnp.where(even_core, 2 * hd * k, (2 * chips + k) * hd),
                jnp.where(even_core, 2 * hd, hd),
            ]
        ).astype(jnp.int32)
        proj, cnat, cpack = attend(
            order_own, count, hidden_all, weight_own, bias_own, blks, hd, scale
        )
        ceven, codd = return_rows(cnat, cpack, 1)
        hidden_out, residual_grad, geven, godd, merged, extra = middle(
            ceven, codd, hidden_in, first_half, outer_full, vecs, bias_inner, cotangent,
            grad_mask, devices, hd,
        )
        share = lax.psum_scatter(
            merged.reshape(-1, width), axes, scatter_dimension=0, tiled=True
        )
        gnat, gpack = spread_rows(geven, godd, 2)
        znat, zpack, grads = attend_back(
            order_own, count, hidden_all, proj, gnat, gpack, extra, hd, scale
        )
        zeven, zodd, proj_grads = leave(
            znat, zpack, grads.reshape((seqs, blks) + grads.shape[1:])
        )
        return (hidden_out,) + tuple(
            final(
                zeven, zodd, projections, residual_grad, proj_grads, share, own, hidden_units, hd
            )
        )

    return run


def masked_scores(left, right, left_ids, right_ids, scale):
    scores = back_product(left, right) * scale
    return jnp.where(left_ids[:, None] == right_ids[None, :], scores, -jnp.inf)


def body(
    hidden_in,
    query_weight,
    key_weight,
    value_weight,
    output_weight,
    inner_weight,
    outer_weight,
    query_bias,
    value_bias,
    output_bias,
    attention_gain,
    attention_shift,
    inner_bias,
    outer_bias,
    final_gain,
    final_shift,
    cotangent,
    grad_mask,
    cluster_order,
):
    rows = hidden_in.shape[0]
    width = hidden_in.shape[1]
    heads = cluster_order.shape[1]
    length = cluster_order.shape[2]
    scale = 1.0 / math.sqrt(width // heads)
    masters = (
        query_weight,
        key_weight,
        value_weight,
        output_weight,
        inner_weight,
        outer_weight,
        query_bias,
        value_bias,
        output_bias,
        attention_gain,
        attention_shift,
        inner_bias,
        outer_bias,
        final_gain,
        final_shift,
    )
    lowered = [master.astype(jnp.bfloat16) for master in masters]
    fetched = (
        lax.all_gather(lowered[0], ("seq", "blk"), axis=0, tiled=True),
        lax.all_gather(lowered[1], ("seq", "blk"), axis=0, tiled=True),
        lax.all_gather(lowered[2], ("seq", "blk"), axis=0, tiled=True),
        lax.all_gather(lowered[3], ("seq", "blk"), axis=0, tiled=True),
        lax.all_gather(lowered[4], ("seq", "blk"), axis=0, tiled=True),
        lax.all_gather(lowered[5], ("seq", "blk"), axis=0, tiled=True),
        lax.all_gather(lowered[6], ("seq", "blk"), axis=0, tiled=True),
        lax.all_gather(lowered[7], ("seq", "blk"), axis=0, tiled=True),
        lax.all_gather(lowered[8], ("seq", "blk"), axis=0, tiled=True),
        lax.all_gather(lowered[9], ("seq", "blk"), axis=0, tiled=True),
        lax.all_gather(lowered[10], ("seq", "blk"), axis=0, tiled=True),
        lax.all_gather(lowered[11], ("seq", "blk"), axis=0, tiled=True),
        lax.all_gather(lowered[12], ("seq", "blk"), axis=0, tiled=True),
        lax.all_gather(lowered[13], ("seq", "blk"), axis=0, tiled=True),
        lax.all_gather(lowered[14], ("seq", "blk"), axis=0, tiled=True),
    )
    query_full, key_full, value_full, output_full, inner_full, outer_full = fetched[0:6]
    vectors = [vector.astype(jnp.float32) for vector in fetched[6:15]]
    (
        bias_query,
        bias_value,
        bias_output,
        gain_first,
        shift_first,
        bias_inner,
        bias_outer,
        gain_final,
        shift_final,
    ) = vectors
    hidden = hidden_in.astype(jnp.float32)
    query_low = (
        jnp.dot(hidden_in, query_full, preferred_element_type=jnp.float32) + bias_query
    ).astype(jnp.bfloat16)
    keys_low = jnp.dot(hidden_in, key_full, preferred_element_type=jnp.float32).astype(jnp.bfloat16)
    values_low = (
        jnp.dot(hidden_in, value_full, preferred_element_type=jnp.float32) + bias_value
    ).astype(jnp.bfloat16)
    all_keys, all_values = (
        lax.all_gather(keys_low, "blk", axis=0, tiled=True),
        lax.all_gather(values_low, "blk", axis=0, tiled=True),
    )
    order = cluster_order[0]
    head_rows = jnp.broadcast_to(jnp.arange(heads, dtype=jnp.int32)[:, None], (heads, length))
    positions = jnp.broadcast_to(jnp.arange(length, dtype=jnp.int32)[None, :], (heads, length))
    inverse = jnp.zeros((heads, length), jnp.int32).at[head_rows, order].set(positions)
    key_cluster = inverse // CLUSTER
    member = lax.dynamic_slice_in_dim(key_cluster, lax.axis_index("blk") * rows, rows, 1)
    query_heads = head_major(query_low, heads)
    key_heads = head_major(all_keys, heads)
    value_heads = head_major(all_values, heads)
    head_ids = jnp.arange(heads, dtype=jnp.int32)

    def attend(index):
        scores = masked_scores(
            query_heads[index], key_heads[index], member[index], key_cluster[index], scale
        )
        peak = jnp.max(scores, axis=-1, keepdims=True)
        weights = jnp.exp(scores - peak)
        total = jnp.sum(weights, axis=-1, keepdims=True)
        probs_low = (weights / total).astype(jnp.bfloat16)
        mixed = jnp.dot(probs_low, value_heads[index], preferred_element_type=jnp.float32)
        return (mixed, (peak + jnp.log(total))[:, 0])

    mixed, logsum = lax.map(attend, head_ids)
    context_low = token_major(mixed).astype(jnp.bfloat16)
    attention_out = (
        jnp.dot(context_low, output_full, preferred_element_type=jnp.float32) + bias_output
    )
    first_norm, first_pull = jax.vjp(layer_norm, hidden + attention_out, gain_first, shift_first)
    first_low = first_norm.astype(jnp.bfloat16)
    inner_pre = jnp.dot(first_low, inner_full, preferred_element_type=jnp.float32) + bias_inner
    activated, gelu_pull = jax.vjp(exact_gelu, inner_pre)
    activated_low = activated.astype(jnp.bfloat16)
    outer_out = jnp.dot(activated_low, outer_full, preferred_element_type=jnp.float32) + bias_outer
    final_norm, final_pull = jax.vjp(layer_norm, first_norm + outer_out, gain_final, shift_final)
    hidden_out = final_norm.astype(jnp.bfloat16)
    out_grad = cotangent.astype(jnp.float32) * grad_mask.astype(jnp.float32)
    second_grad, grad_final_gain, grad_final_shift = final_pull(out_grad)
    outer_low = second_grad.astype(jnp.bfloat16)
    back_weights = (
        lax.all_gather(lowered[0], ("seq", "blk"), axis=0, tiled=True),
        lax.all_gather(lowered[1], ("seq", "blk"), axis=0, tiled=True),
        lax.all_gather(lowered[2], ("seq", "blk"), axis=0, tiled=True),
        lax.all_gather(lowered[3], ("seq", "blk"), axis=0, tiled=True),
        lax.all_gather(lowered[4], ("seq", "blk"), axis=0, tiled=True),
        lax.all_gather(lowered[5], ("seq", "blk"), axis=0, tiled=True),
    )
    grad_outer_weight = row_contract(activated_low, outer_low)
    grad_outer_bias = column_sum(outer_low)
    inner_low = gelu_pull(back_product(outer_low, back_weights[5]))[0].astype(jnp.bfloat16)
    grad_inner_weight = row_contract(first_low, inner_low)
    grad_inner_bias = column_sum(inner_low)
    first_grad = back_product(inner_low, back_weights[4]) + second_grad
    residual_grad, grad_attention_gain, grad_attention_shift = first_pull(first_grad)
    attn_low = residual_grad.astype(jnp.bfloat16)
    grad_output_weight = row_contract(context_low, attn_low)
    grad_output_bias = column_sum(attn_low)
    context_grad = back_product(attn_low, back_weights[3]).astype(jnp.bfloat16)
    grad_heads = head_major(context_grad, heads)

    def own_rows_back(index):
        scores = masked_scores(
            query_heads[index], key_heads[index], member[index], key_cluster[index], scale
        )
        probs = jnp.exp(scores - logsum[index][:, None])
        probs_low = probs.astype(jnp.bfloat16)
        grad_part = grad_heads[index]
        prob_grad = back_product(grad_part, value_heads[index])
        weighted = jnp.sum(probs * prob_grad, axis=-1, keepdims=True)
        score_low = (probs * (prob_grad - weighted)).astype(jnp.bfloat16)
        query_grad = (
            jnp.dot(score_low, key_heads[index], preferred_element_type=jnp.float32) * scale
        )
        return (probs_low, score_low, query_grad, weighted[:, 0])

    def attend_back(index):
        probs_low, score_low, query_grad, weighted = own_rows_back(index)
        key_sum = row_contract(score_low, query_heads[index]) * scale
        value_sum = row_contract(probs_low, grad_heads[index])
        return (query_grad, key_sum, value_sum)

    query_grads, key_grads, value_grads = lax.map(attend_back, head_ids)
    key_own, value_own = (
        lax.psum_scatter(token_major(key_grads), "blk", scatter_dimension=0, tiled=True),
        lax.psum_scatter(token_major(value_grads), "blk", scatter_dimension=0, tiled=True),
    )
    query_grad_low = token_major(query_grads).astype(jnp.bfloat16)
    key_grad_low = key_own.astype(jnp.bfloat16)
    value_grad_low = value_own.astype(jnp.bfloat16)
    grad_query_weight = row_contract(hidden_in, query_grad_low)
    grad_key_weight = row_contract(hidden_in, key_grad_low)
    grad_value_weight = row_contract(hidden_in, value_grad_low)
    grad_query_bias = column_sum(query_grad_low)
    grad_value_bias = column_sum(value_grad_low)
    input_grad = (
        back_product(query_grad_low, back_weights[0])
        + back_product(key_grad_low, back_weights[1])
        + back_product(value_grad_low, back_weights[2])
        + residual_grad
    )
    shares = (
        lax.psum_scatter(grad_query_weight, ("seq", "blk"), scatter_dimension=0, tiled=True),
        lax.psum_scatter(grad_key_weight, ("seq", "blk"), scatter_dimension=0, tiled=True),
        lax.psum_scatter(grad_value_weight, ("seq", "blk"), scatter_dimension=0, tiled=True),
        lax.psum_scatter(grad_output_weight, ("seq", "blk"), scatter_dimension=0, tiled=True),
        lax.psum_scatter(grad_inner_weight, ("seq", "blk"), scatter_dimension=0, tiled=True),
        lax.psum_scatter(grad_outer_weight, ("seq", "blk"), scatter_dimension=0, tiled=True),
        lax.psum_scatter(grad_query_bias, ("seq", "blk"), scatter_dimension=0, tiled=True),
        lax.psum_scatter(grad_value_bias, ("seq", "blk"), scatter_dimension=0, tiled=True),
        lax.psum_scatter(grad_output_bias, ("seq", "blk"), scatter_dimension=0, tiled=True),
        lax.psum_scatter(grad_attention_gain, ("seq", "blk"), scatter_dimension=0, tiled=True),
        lax.psum_scatter(grad_attention_shift, ("seq", "blk"), scatter_dimension=0, tiled=True),
        lax.psum_scatter(grad_inner_bias, ("seq", "blk"), scatter_dimension=0, tiled=True),
        lax.psum_scatter(grad_outer_bias, ("seq", "blk"), scatter_dimension=0, tiled=True),
        lax.psum_scatter(grad_final_gain, ("seq", "blk"), scatter_dimension=0, tiled=True),
        lax.psum_scatter(grad_final_shift, ("seq", "blk"), scatter_dimension=0, tiled=True),
    )
    return (hidden_out, input_grad) + tuple(shares)


def solution(mesh):
    placed = (
        P(("seq", "blk"), None),
        P(("seq", "blk"), None),
        P(("seq", "blk"), None),
        P(("seq", "blk"), None),
        P(("seq", "blk"), None),
        P(("seq", "blk"), None),
        P(("seq", "blk"), None),
        P(("seq", "blk")),
        P(("seq", "blk")),
        P(("seq", "blk")),
        P(("seq", "blk")),
        P(("seq", "blk")),
        P(("seq", "blk")),
        P(("seq", "blk")),
        P(("seq", "blk")),
        P(("seq", "blk")),
        P(("seq", "blk"), None),
        P(("seq", "blk"), None),
        P("seq", None, None),
    )
    seqs, blks = mesh.shape["seq"], mesh.shape["blk"]
    heads = 12
    fast = blks % 2 == 0 and 3 * blks == 2 * heads
    return jax.shard_map(
        fast_body(seqs, blks, heads) if fast else body,
        mesh=mesh,
        in_specs=placed,
        out_specs=(
            P(("seq", "blk"), None),
            P(("seq", "blk"), None),
            P(("seq", "blk"), None),
            P(("seq", "blk"), None),
            P(("seq", "blk"), None),
            P(("seq", "blk"), None),
            P(("seq", "blk"), None),
            P(("seq", "blk"), None),
            P(("seq", "blk")),
            P(("seq", "blk")),
            P(("seq", "blk")),
            P(("seq", "blk")),
            P(("seq", "blk")),
            P(("seq", "blk")),
            P(("seq", "blk")),
            P(("seq", "blk")),
            P(("seq", "blk")),
        ),
        check_vma=False,
    )
```

```python
import functools
import math

import jax
import jax.numpy as jnp
from jax import lax
from jax.experimental import pallas as pl
from jax.experimental.pallas import tpu as pltpu
from jax.sharding import PartitionSpec as P

MESH = pl.DeviceIdType.MESH
ANY = pl.ANY
LOW = jnp.bfloat16
F32 = jnp.float32
BIG = 60 * 2**20
GROUP = 4
CLUSTER = 128


def spec(space):
    return pl.BlockSpec(memory_space=space)


def nt_dot(left, right):
    return lax.dot_general(left, right, (((1,), (1,)), ((), ())), preferred_element_type=F32)


def tn_dot(left, right):
    return lax.dot_general(left, right, (((0,), (0,)), ((), ())), preferred_element_type=F32)


def nn_dot(left, right):
    return jnp.dot(left, right, preferred_element_type=F32)


def greet(targets):
    sem = pltpu.get_barrier_semaphore()
    for target in targets:
        pl.semaphore_signal(sem, inc=1, device_id=target, device_id_type=MESH)
    pl.semaphore_wait(sem, len(targets))


def send(src, dst, send_sem, recv_sem, target):
    return pltpu.make_async_remote_copy(
        src_ref=src,
        dst_ref=dst,
        send_sem=send_sem,
        recv_sem=recv_sem,
        device_id=target,
        device_id_type=MESH,
    )


epsilon = 1e-06


def layer_norm(value, gain, shift):
    center = value - jnp.mean(value, axis=-1, keepdims=True)
    spread = jnp.mean(center * center, axis=-1, keepdims=True)
    return center * lax.rsqrt(spread + epsilon) * gain + shift


def exact_gelu(value):
    return jax.nn.gelu(value, approximate=False)


def row_contract(left, right):
    return lax.dot_general(
        left, right, (((0,), (0,)), ((), ())), preferred_element_type=jnp.float32
    )


def back_product(grad, weight):
    return lax.dot_general(
        grad, weight, (((1,), (1,)), ((), ())), preferred_element_type=jnp.float32
    )


def column_sum(value):
    return jnp.sum(value.astype(jnp.float32), axis=0)


def head_major(value, heads):
    return value.reshape(value.shape[0], heads, -1).transpose(1, 0, 2)


def token_major(value):
    return value.transpose(1, 0, 2).reshape(value.shape[1], value.shape[0] * value.shape[2])


def entry_kernel(
    seqs, blks, parts, x_ref, w_ref, a0, a1, a2, o_ref, wall_ref, f0, f1, f2,
    own_sem, ssem, rsem, wl, ws, wr, us, ur, al, zs, zr, ns, nr, ms, mr,
):
    half = blks // 2
    s = lax.axis_index("seq")
    b = lax.axis_index("blk")
    k = b // 2
    c = lax.rem(b, 2)
    mate = b + 1 - 2 * c
    left = lax.rem(b + blks - 2, blks)
    right = lax.rem(b + 2, blks)
    has_left = k > 0
    has_right = k < half - 1
    blk_peers = [{"blk": lax.rem(b + d, blks)} for d in range(1, blks)]
    seq_peers = [{"seq": lax.rem(s + d, seqs)} for d in range(1, seqs)]
    greet(blk_peers + seq_peers)

    def slab(d):
        peer = lax.rem(b + d, blks)
        return send(w_ref.at[peer], wall_ref.at[s, b], ws.at[d], wr.at[d], {"blk": peer})

    def group(d):
        return send(
            wall_ref.at[s], wall_ref.at[s], us.at[d], ur.at[d], {"seq": lax.rem(s + d, seqs)}
        )

    def piece(src, blk, p, to, way):
        return send(src, o_ref.at[blk, p], ssem.at[way, blk, p], rsem.at[blk, p], {"blk": to})

    shards = ((a0, f0), (a1, f1), (a2, f2))
    x_next = s + 1 - 2 * lax.rem(s, 2)
    y_next = s + 2 - 4 * (s // 2)
    across = 3 - s
    low_part = pl.ds(0, half // 2)
    high_part = pl.ds(half // 2, half // 2)

    def along(a, d):
        own_ref, full = shards[a]
        to = 2 * lax.rem(k + d, half) + c
        return send(own_ref, full.at[s, k, c], zs.at[a, d], zr.at[a, d], {"blk": to})

    def beside(a, way):
        full = shards[a][1]
        whole = full.at[s, :, c]
        if way == 0:
            return send(whole, whole, ns.at[a, 0], nr.at[a, 0], {"seq": x_next})
        if way == 1:
            return send(whole, whole, ns.at[a, 1], nr.at[a, 1], {"seq": y_next})
        if way == 2:
            part = full.at[y_next, low_part, c]
            return send(part, part, ns.at[a, 2], nr.at[a, 2], {"seq": x_next})
        part = full.at[x_next, high_part, c]
        return send(part, part, ns.at[a, 3], nr.at[a, 3], {"seq": y_next})

    def pair(a, i, src):
        part = shards[a][1].at[src, :, c]
        return send(part, part, ms.at[a, i], mr.at[a, i], {"blk": mate})

    for d in range(1, blks):
        slab(d).start()
    for a in range(3):
        for d in range(1, half):
            along(a, d).start()
        pltpu.make_async_copy(shards[a][0], shards[a][1].at[s, k, c], al.at[a]).start()
    own_slab = pltpu.make_async_copy(w_ref.at[b], wall_ref.at[s, b], wl)
    own_slab.start()
    for p in range(parts):
        @pl.when(has_left)
        def _():
            piece(x_ref.at[p], b, p, left, 0).start()

        @pl.when(has_right)
        def _():
            piece(x_ref.at[p], b, p, right, 1).start()
    for p in range(parts):
        piece(x_ref.at[p], b, p, mate, 2).start()
    own = pltpu.make_async_copy(x_ref, o_ref.at[b], own_sem)
    own.start()
    own_slab.wait()
    for d in range(1, blks):
        slab(d).wait_recv()
    for d in range(1, seqs):
        group(d).start()
    for a in range(3):
        pltpu.make_async_copy(shards[a][0], shards[a][1].at[s, k, c], al.at[a]).wait()
        for d in range(1, half):
            along(a, d).wait_recv()
        beside(a, 0).start()
        beside(a, 1).start()
        pair(a, 0, s).start()

    def second(a):
        beside(a, 1).wait_recv()
        beside(a, 2).start()
        pair(a, 2, y_next).start()
        beside(a, 0).wait_recv()
        beside(a, 3).start()
        pair(a, 1, x_next).start()

    for t in range(1, half):
        for p in range(parts):
            @pl.when(k - t >= 0)
            def _():
                blk = b - 2 * t
                piece(o_ref.at[blk, p], blk, p, right, 1).wait_recv()

                @pl.when(has_right)
                def _():
                    piece(o_ref.at[blk, p], blk, p, right, 1).start()

                piece(o_ref.at[blk, p], blk, p, mate, 2).start()

            @pl.when(k + t < half)
            def _():
                blk = b + 2 * t
                piece(o_ref.at[blk, p], blk, p, left, 0).wait_recv()

                @pl.when(has_left)
                def _():
                    piece(o_ref.at[blk, p], blk, p, left, 0).start()

                piece(o_ref.at[blk, p], blk, p, mate, 2).start()

        second(t - 1)
    for a in range(3):
        beside(a, 2).wait_recv()
        beside(a, 3).wait_recv()
        pair(a, 3, across).start()
    for j in range(half):
        blk = 2 * j + 1 - c
        for p in range(parts):
            piece(o_ref.at[blk, p], blk, p, mate, 2).wait_recv()
    for j in range(half):
        blk = 2 * j + c
        for p in range(parts):
            piece(o_ref.at[blk, p], blk, p, mate, 2).wait_send()

            @pl.when(jnp.logical_and(has_right, j <= k))
            def _():
                piece(o_ref.at[blk, p], blk, p, right, 1).wait_send()

            @pl.when(jnp.logical_and(has_left, j >= k))
            def _():
                piece(o_ref.at[blk, p], blk, p, left, 0).wait_send()
    own.wait()
    for d in range(1, blks):
        slab(d).wait_send()
    for d in range(1, seqs):
        group(d).wait()
    for a in range(3):
        for i, src in enumerate((s, x_next, y_next, across)):
            pair(a, i, src).wait()
        for way in range(4):
            beside(a, way).wait_send()
        for d in range(1, half):
            along(a, d).wait_send()


def entry(hidden, slabs, shards, seqs, blks, parts):
    rows, width = hidden.shape
    dma = pltpu.SemaphoreType.DMA
    return pl.pallas_call(
        functools.partial(entry_kernel, seqs, blks, parts),
        name="entry",
        out_shape=(
            jax.ShapeDtypeStruct((blks, parts, rows // parts, width), LOW),
            jax.ShapeDtypeStruct((seqs,) + slabs.shape, LOW),
        )
        + tuple(jax.ShapeDtypeStruct((seqs, blks // 2, 2) + x.shape, LOW) for x in shards),
        in_specs=[spec(pltpu.VMEM)] * 5,
        out_specs=(spec(ANY),) * 5,
        scratch_shapes=[
            dma, dma((3, blks, parts)), dma((blks, parts)), dma,
            dma((blks,)), dma((blks,)), dma((seqs,)), dma((seqs,)),
            dma((3,)), dma((3, blks // 2)), dma((3, blks // 2)),
            dma((3, 4)), dma((3, 4)), dma((3, 4)), dma((3, 4)),
        ],
        compiler_params=pltpu.CompilerParams(collective_id=0, has_side_effects=True),
        cost_estimate=pl.CostEstimate(flops=0, transcendentals=0, bytes_accessed=200 * 10**6),
    )(hidden.reshape(parts, rows // parts, width), slabs, *shards)


def return_kernel(blks, nat_ref, pack_ref, even_ref, odd_ref, buf, lsem, ssem, rsem):
    b = lax.axis_index("blk")
    k = b // 2
    c = lax.rem(b, 2)
    greet([{"blk": lax.rem(b + d, blks)} for d in range(1, blks)])
    start_return(blks, b, k, c, nat_ref, pack_ref, even_ref, odd_ref, buf, lsem, ssem, rsem)
    finish_return(blks, b, k, c, nat_ref, pack_ref, even_ref, odd_ref, ssem, rsem)


def full_way(blks, b, d, nat_ref, even_ref, ssem, rsem, slot):
    peer = lax.rem(b + d, blks)
    return send(nat_ref.at[peer], even_ref.at[slot], ssem.at[d], rsem.at[d], {"blk": peer})


def start_return(blks, b, k, c, nat_ref, pack_ref, even_ref, odd_ref, buf, lsem, ssem, rsem):
    @pl.when(c == 0)
    def _():
        for d in range(1, blks):
            full_way(blks, b, d, nat_ref, even_ref, ssem, rsem, k).start()
        inward = pltpu.make_async_copy(nat_ref.at[b], buf, lsem)
        inward.start()
        inward.wait()
        outward = pltpu.make_async_copy(buf, even_ref.at[k], lsem)
        outward.start()
        outward.wait()

    @pl.when(c == 1)
    def _():
        for d in range(1, blks):
            full_way(blks, b, d, pack_ref, odd_ref, ssem, rsem, k).start()
        part = buf.at[pl.ds(0, pack_ref.shape[1])]
        inward = pltpu.make_async_copy(pack_ref.at[b], part, lsem)
        inward.start()
        inward.wait()
        outward = pltpu.make_async_copy(part, odd_ref.at[k], lsem)
        outward.start()
        outward.wait()


def finish_return(blks, b, k, c, nat_ref, pack_ref, even_ref, odd_ref, ssem, rsem):
    for d in range(1, blks):
        source = lax.rem(b + blks - d, blks)

        @pl.when(lax.rem(source, 2) == 0)
        def _():
            full_way(blks, b, d, nat_ref, even_ref, ssem, rsem, source // 2).wait_recv()

        @pl.when(lax.rem(source, 2) == 1)
        def _():
            full_way(blks, b, d, pack_ref, odd_ref, ssem, rsem, source // 2).wait_recv()

    @pl.when(c == 0)
    def _():
        for d in range(1, blks):
            full_way(blks, b, d, nat_ref, even_ref, ssem, rsem, k).wait_send()

    @pl.when(c == 1)
    def _():
        for d in range(1, blks):
            full_way(blks, b, d, pack_ref, odd_ref, ssem, rsem, k).wait_send()


def return_rows(nat, pack, collective_id):
    blks = nat.shape[0]
    dma = pltpu.SemaphoreType.DMA
    return pl.pallas_call(
        functools.partial(return_kernel, blks),
        name="return_rows",
        out_shape=(
            jax.ShapeDtypeStruct((blks // 2,) + nat.shape[1:], LOW),
            jax.ShapeDtypeStruct((blks // 2,) + pack.shape[1:], LOW),
        ),
        in_specs=[spec(ANY)] * 2,
        out_specs=(spec(ANY), spec(ANY)),
        scratch_shapes=[pltpu.VMEM(nat.shape[1:], LOW), dma, dma((blks,)), dma((blks,))],
        compiler_params=pltpu.CompilerParams(collective_id=collective_id, has_side_effects=True),
        cost_estimate=pl.CostEstimate(flops=0, transcendentals=0, bytes_accessed=80 * 10**6),
    )(nat, pack)


def spread_kernel(
    blks, even_ref, odd_ref, grad_ref, nat_ref, pack_ref, total,
    buf, mine, theirs, lsem, ssem, rsem, ml, ms, mr,
):
    b = lax.axis_index("blk")
    c = lax.rem(b, 2)
    mate = b + 1 - 2 * c
    greet([{"blk": lax.rem(b + d, blks)} for d in range(1, blks)])
    swap = send(grad_ref.at[:, 1 - c], theirs, ms, mr, {"blk": mate})
    swap.start()
    load = pltpu.make_async_copy(grad_ref.at[:, c], mine, ml)
    load.start()

    def full(d, slot):
        peer = lax.rem(b + d, blks)
        return send(
            even_ref.at[peer // 2], nat_ref.at[slot], ssem.at[d], rsem.at[d], {"blk": peer}
        )

    def packed(d, slot):
        peer = lax.rem(b + d, blks)
        return send(
            odd_ref.at[peer // 2], pack_ref.at[slot], ssem.at[d], rsem.at[d], {"blk": peer}
        )

    for d in range(1, blks):
        to_even = lax.rem(b + d, 2) == 0

        @pl.when(to_even)
        def _():
            full(d, b).start()

        @pl.when(jnp.logical_not(to_even))
        def _():
            packed(d, b).start()

    load.wait()
    swap.wait()

    @pl.loop(0, total.shape[0])
    def _(o):
        total[o] = (mine[o].astype(F32) + theirs[o].astype(F32)).astype(LOW)

    @pl.when(c == 0)
    def _():
        inward = pltpu.make_async_copy(even_ref.at[b // 2], buf, lsem)
        inward.start()
        inward.wait()
        outward = pltpu.make_async_copy(buf, nat_ref.at[b], lsem)
        outward.start()
        outward.wait()
        for d in range(1, blks):
            full(d, lax.rem(b + blks - d, blks)).wait_recv()

    @pl.when(c == 1)
    def _():
        part = buf.at[pl.ds(0, odd_ref.shape[1])]
        inward = pltpu.make_async_copy(odd_ref.at[b // 2], part, lsem)
        inward.start()
        inward.wait()
        outward = pltpu.make_async_copy(part, pack_ref.at[b], lsem)
        outward.start()
        outward.wait()
        for d in range(1, blks):
            packed(d, lax.rem(b + blks - d, blks)).wait_recv()

    for d in range(1, blks):
        to_even = lax.rem(b + d, 2) == 0

        @pl.when(to_even)
        def _():
            full(d, b).wait_send()

        @pl.when(jnp.logical_not(to_even))
        def _():
            packed(d, b).wait_send()


def spread_rows(even, odd, grads, collective_id):
    blks = 2 * even.shape[0]
    half_shape = grads.shape[:1] + grads.shape[2:]
    dma = pltpu.SemaphoreType.DMA
    return pl.pallas_call(
        functools.partial(spread_kernel, blks),
        name="spread_rows",
        out_shape=(
            jax.ShapeDtypeStruct((blks,) + even.shape[1:], LOW),
            jax.ShapeDtypeStruct((blks,) + odd.shape[1:], LOW),
            jax.ShapeDtypeStruct(half_shape, LOW),
        ),
        in_specs=[spec(ANY)] * 3,
        out_specs=(spec(ANY), spec(ANY), spec(pltpu.VMEM)),
        scratch_shapes=[
            pltpu.VMEM(even.shape[1:], LOW),
            pltpu.VMEM(half_shape, LOW),
            pltpu.VMEM(half_shape, LOW),
            dma, dma((blks,)), dma((blks,)), dma, dma, dma,
        ],
        compiler_params=pltpu.CompilerParams(
            collective_id=collective_id, has_side_effects=True, vmem_limit_bytes=BIG
        ),
        cost_estimate=pl.CostEstimate(flops=0, transcendentals=0, bytes_accessed=80 * 10**6),
    )(even, odd, grads)


def exit_kernel(
    seqs, blks, nat_ref, pack_ref, grad_ref, big_ref, even_ref, odd_ref, out_ref, big_out,
    buf, stage, total, big_stage, big_total,
    lsem, ssem, rsem, us, ur, gl, gs, gr, bl, bu, bv, cl, cs, cr,
):
    s = lax.axis_index("seq")
    b = lax.axis_index("blk")
    k = b // 2
    c = lax.rem(b, 2)
    blk_peers = [{"blk": lax.rem(b + d, blks)} for d in range(1, blks)]
    seq_peers = [{"seq": lax.rem(s + d, seqs)} for d in range(1, seqs)]
    greet(blk_peers + seq_peers)

    def group(d):
        peer = lax.rem(s + d, seqs)
        return send(grad_ref.at[peer], stage.at[d], us.at[d], ur.at[d], {"seq": peer})

    def slab(d):
        peer = lax.rem(b + d, blks)
        return send(total.at[peer], out_ref.at[b], gs.at[d], gr.at[d], {"blk": peer})

    chips = blks // 2
    pieces = big_ref.shape[2]

    def big_group(p, d):
        peer = lax.rem(s + d, seqs)
        return send(
            big_ref.at[peer, :, p], big_stage.at[p, d], bu.at[p, d], bv.at[p, d], {"seq": peer}
        )

    def big_slab(p, d):
        to = lax.rem(k + d, chips)
        return send(
            big_total.at[p, to], big_out.at[k, p], cs.at[p, d], cr.at[p, d], {"blk": 2 * to + c}
        )

    def big_own(p):
        return pltpu.make_async_copy(big_ref.at[s, :, p], big_stage.at[p, 0], bl.at[p])

    for p in range(pieces):
        big_own(p).start()
    for d in range(1, seqs):
        group(d).start()
    for p in range(pieces):
        for d in range(1, seqs):
            big_group(p, d).start()
    start_return(blks, b, k, c, nat_ref, pack_ref, even_ref, odd_ref, buf, lsem, ssem, rsem)
    for d in range(1, seqs):
        group(d).wait_recv()
    for o in range(blks):
        acc = grad_ref[s, o].astype(F32)
        for d in range(1, seqs):
            acc = acc + stage[d, o].astype(F32)
        total[o] = acc.astype(LOW)
    for d in range(1, blks):
        slab(d).start()
    own = pltpu.make_async_copy(total.at[b], out_ref.at[b], gl)
    own.start()
    own.wait()
    for p in range(pieces):
        big_own(p).wait()
        for d in range(1, seqs):
            big_group(p, d).wait_recv()

        @pl.loop(0, chips)
        def _(o):
            acc = big_stage[p, 0, o].astype(F32)
            for d in range(1, seqs):
                acc = acc + big_stage[p, d, o].astype(F32)
            big_total[p, o] = acc.astype(LOW)

        for d in range(1, chips):
            big_slab(p, d).start()
        keep = pltpu.make_async_copy(big_total.at[p, k], big_out.at[k, p], cl.at[p])
        keep.start()
        keep.wait()
    finish_return(blks, b, k, c, nat_ref, pack_ref, even_ref, odd_ref, ssem, rsem)
    for d in range(1, blks):
        slab(d).wait()
    for d in range(1, seqs):
        group(d).wait_send()
    for p in range(pieces):
        for d in range(1, chips):
            big_slab(p, d).wait()
        for d in range(1, seqs):
            big_group(p, d).wait_send()


def leave(nat, pack, grads, big):
    blks = nat.shape[0]
    seqs = grads.shape[0]
    chips, pieces = big.shape[1:3]
    dma = pltpu.SemaphoreType.DMA
    return pl.pallas_call(
        functools.partial(exit_kernel, seqs, blks),
        name="leave",
        out_shape=(
            jax.ShapeDtypeStruct((blks // 2,) + nat.shape[1:], LOW),
            jax.ShapeDtypeStruct((blks // 2,) + pack.shape[1:], LOW),
            jax.ShapeDtypeStruct(grads.shape[1:], LOW),
            jax.ShapeDtypeStruct(big.shape[1:], LOW),
        ),
        in_specs=[spec(ANY), spec(ANY), spec(pltpu.VMEM), spec(ANY)],
        out_specs=(spec(ANY),) * 4,
        scratch_shapes=[
            pltpu.VMEM(nat.shape[1:], LOW),
            pltpu.VMEM(grads.shape, LOW),
            pltpu.VMEM(grads.shape[1:], LOW),
            pltpu.VMEM((pieces, seqs, chips) + big.shape[3:], LOW),
            pltpu.VMEM((pieces, chips) + big.shape[3:], LOW),
            dma, dma((blks,)), dma((blks,)), dma((seqs,)), dma((seqs,)),
            dma, dma((blks,)), dma((blks,)),
            dma((pieces,)), dma((pieces, seqs)), dma((pieces, seqs)),
            dma((pieces,)), dma((pieces, chips)), dma((pieces, chips)),
        ],
        compiler_params=pltpu.CompilerParams(
            collective_id=3, has_side_effects=True, vmem_limit_bytes=BIG
        ),
        cost_estimate=pl.CostEstimate(flops=0, transcendentals=0, bytes_accessed=200 * 10**6),
    )(nat, pack, grads, big)


def owner_facts(hd, chips):
    b = lax.axis_index("blk")
    k = b // 2
    odd = lax.rem(b, 2)
    first = jnp.where(odd == 0, 2 * hd * k, (2 * chips + k) * hd)
    return 2 - odd, first, (2 - odd) * hd


def lane_of(rows):
    return lax.broadcasted_iota(jnp.int32, (rows, 128), 1)


def low_lanes(value, slot, hd):
    lane = lane_of(value.shape[0])
    keep = jnp.logical_and(lane >= slot * hd, lane < (slot + 1) * hd)
    return jnp.where(keep, value, 0.0).astype(LOW)


def part_of(u, t):
    return pl.ds(u * 512 + t, 128, stride=4)


def row_part(ref, u, t):
    return ref[part_of(u, t), :]


def column_softmax(scores):
    weights = jnp.exp(scores - jnp.max(scores, axis=0, keepdims=True))
    return weights * (1.0 / jnp.sum(weights, axis=0, keepdims=True))


def attend_kernel(
    hd, scale, order, hid, gathered, proj, nat, pack, vecs, bias_inner,
    rows4, take, take_b, mix, mix_b, back, wide_weight, weight,
):
    length, width = hid.shape
    blks, step, _ = nat.shape
    devices = gathered.shape[0]
    own_rows = width // devices
    per = bias_inner.shape[1] // devices
    heads_here, first, _ = owner_facts(hd, blks // 2)
    for i in range(devices):
        slab = gathered[i].astype(F32)
        wide_weight[i * own_rows : (i + 1) * own_rows, :] = slab[:own_rows, :]
        vecs[:, i * own_rows : (i + 1) * own_rows] = slab[own_rows:, :own_rows]
        bias_inner[0:1, i * per : (i + 1) * per] = slab[own_rows : own_rows + 1, 128 : 128 + per]
    weight[...] = wide_weight[...].astype(LOW)
    tile = vecs[:, pl.ds(pl.multiple_of(first // 128 * 128, 128), 128)]
    tile = jnp.where(lax.rem(first, 128) == 0, tile, pltpu.roll(tile, 64, 1))
    bias = jnp.concatenate([tile[0:1], jnp.zeros((1, 128), F32), tile[1:2]], axis=1)

    @pl.loop(0, length // step)
    def _(i):
        at = pl.multiple_of(i * step, step)
        low = (nn_dot(hid[pl.ds(at, step), :], weight[...]) + bias).astype(LOW)
        proj[pl.ds(at, step), :] = low
        wide = low.astype(F32)
        for t in range(3):
            rows4[pl.ds(4 * at + t, step, stride=4), :] = wide[:, t * 128 : (t + 1) * 128]

    span = GROUP * 128

    def gather(buf, base):
        for j in range(span):
            buf[4 * j : 4 * j + 4, :] = rows4[pl.ds(pl.multiple_of(4 * order[base + j], 4), 4), :]

    def attend_group(slot, buf, out):
        for u in range(GROUP):
            own = pl.ds(u * 128, 128)
            query = low_lanes(row_part(buf, u, 0) * scale, slot, hd)
            probs = column_softmax(nt_dot(row_part(buf, u, 1).astype(LOW), query))
            out[own, :] = tn_dot(probs.astype(LOW), row_part(buf, u, 2).astype(LOW))

    def scatter(slot, out, base):
        for j in range(span):
            back[pl.ds(slot * length + order[base + j], 1), :] = out[pl.ds(j, 1), :]

    @pl.loop(0, heads_here)
    def _(slot):
        begin = slot * length
        gather(take, begin)

        @pl.loop(0, length // (2 * span))
        def _(i):
            base = begin + 2 * i * span
            gather(take_b, base + span)
            attend_group(slot, take, mix)
            scatter(slot, mix, base)
            gather(take, jnp.minimum(base + 2 * span, begin + length - span))
            attend_group(slot, take_b, mix_b)
            scatter(slot, mix_b, base + span)

    lane = lane_of(step)

    @pl.when(heads_here == 2)
    def _():
        @pl.loop(0, length // step)
        def _(i):
            at = pl.multiple_of(i * step, step)
            nat[i] = jnp.where(
                lane < hd, back[pl.ds(at, step), :], back[pl.ds(length + at, step), :]
            ).astype(LOW)

    half = step // 2

    @pl.when(heads_here == 1)
    def _():
        @pl.loop(0, length // step)
        def _(i):
            at = pl.multiple_of(i * step, step)
            upper = pltpu.roll(back[pl.ds(at + half, half), :], hd, 1)
            pack[i] = jnp.where(lane[:half] < hd, back[pl.ds(at, half), :], upper).astype(LOW)


def attend(order, hid, gathered, blks, ff, hd, scale):
    length, width = hid.shape
    step = length // blks
    return pl.pallas_call(
        functools.partial(attend_kernel, hd, scale),
        name="attend",
        out_shape=(
            jax.ShapeDtypeStruct((length, 384), LOW),
            jax.ShapeDtypeStruct((blks, step, 128), LOW),
            jax.ShapeDtypeStruct((blks, step // 2, 128), LOW),
            jax.ShapeDtypeStruct((8, width), F32),
            jax.ShapeDtypeStruct((8, ff), F32),
        ),
        in_specs=[spec(pltpu.SMEM)] + [spec(pltpu.VMEM)] * 2,
        out_specs=(spec(pltpu.VMEM),) * 5,
        scratch_shapes=[
            pltpu.VMEM((4 * length, 128), F32),
            pltpu.VMEM((GROUP * 512, 128), F32),
            pltpu.VMEM((GROUP * 512, 128), F32),
            pltpu.VMEM((GROUP * 128, 128), F32),
            pltpu.VMEM((GROUP * 128, 128), F32),
            pltpu.VMEM((2 * length, 128), F32),
            pltpu.VMEM((width, 384), F32),
            pltpu.VMEM((width, 384), LOW),
        ],
        compiler_params=pltpu.CompilerParams(vmem_limit_bytes=BIG),
        cost_estimate=pl.CostEstimate(
            flops=5 * 10**9, transcendentals=0, bytes_accessed=100 * 10**6
        ),
    )(order, hid, gathered)


def attend_back_kernel(
    hd, scale, order, hidden_hbm, proj, gnat, gpack, extra, znat, zpack, slabs,
    rows4, take, take_b, out4, out4_b, back4, hid, wide_grad, sem,
):
    length = proj.shape[0]
    step = gnat.shape[1]
    half = step // 2
    heads_here, first_col, limit = owner_facts(hd, gnat.shape[0] // 2)
    fetch = pltpu.make_async_copy(hidden_hbm, hid, sem)
    fetch.start()

    @pl.loop(0, length // step)
    def _(i):
        at = pl.multiple_of(i * step, step)
        wide = proj[pl.ds(at, step), :].astype(F32)
        for t in range(3):
            rows4[pl.ds(4 * at + t, step, stride=4), :] = wide[:, t * 128 : (t + 1) * 128]

        @pl.when(heads_here == 2)
        def _():
            rows4[pl.ds(4 * at + 3, step, stride=4), :] = gnat[i].astype(F32)

        @pl.when(heads_here == 1)
        def _():
            pair = gpack[i].astype(F32)
            rows4[pl.ds(4 * at + 3, half, stride=4), :] = pair
            rows4[pl.ds(4 * (at + half) + 3, half, stride=4), :] = pltpu.roll(pair, hd, 1)

    span = GROUP * 128

    def gather(buf, base):
        for j in range(span):
            buf[4 * j : 4 * j + 4, :] = rows4[pl.ds(pl.multiple_of(4 * order[base + j], 4), 4), :]

    def attend_group(slot, buf, out):
        for u in range(GROUP):
            own = pl.ds(u * 128, 128)
            query = low_lanes(row_part(buf, u, 0) * scale, slot, hd)
            grad = low_lanes(row_part(buf, u, 3), slot, hd)
            keys = row_part(buf, u, 1).astype(LOW)
            probs = column_softmax(nt_dot(keys, query))
            prob_grad = nt_dot(row_part(buf, u, 2).astype(LOW), grad)
            shift = jnp.sum(probs * prob_grad, axis=0, keepdims=True)
            score_low = (probs * (prob_grad - shift)).astype(LOW)
            out[part_of(u, 0), :] = tn_dot(score_low, keys) * scale
            out[part_of(u, 1), :] = nn_dot(score_low, query)
            out[part_of(u, 2), :] = nn_dot(probs.astype(LOW), grad)

    def scatter(slot, out, base):
        for j in range(span):
            at = pl.multiple_of(4 * (slot * length + order[base + j]), 4)
            back4[pl.ds(at, 4), :] = out[4 * j : 4 * j + 4, :]

    @pl.loop(0, heads_here)
    def _(slot):
        begin = slot * length
        gather(take, begin)

        @pl.loop(0, length // (2 * span))
        def _(i):
            base = begin + 2 * i * span
            gather(take_b, base + span)
            attend_group(slot, take, out4)
            scatter(slot, out4, base)
            gather(take, jnp.minimum(base + 2 * span, begin + length - span))
            attend_group(slot, take_b, out4_b)
            scatter(slot, out4_b, base + span)

    lane = lane_of(step)
    fetch.wait()
    wide_grad[...] = jnp.zeros_like(wide_grad)
    zero = jnp.zeros((1, 384), F32)

    def settle(i, sums):
        at = pl.multiple_of(i * step, step)
        parts = []
        for t in range(3):
            cols = pl.ds(t * 128, 128)
            first = back4[pl.ds(4 * at + t, step, stride=4), :]
            second = back4[pl.ds(4 * (length + at) + t, step, stride=4), :]
            second = jnp.where(heads_here == 2, second, jnp.zeros_like(second))
            low = jnp.where(lane < hd, first, second).astype(LOW)
            znat[i, :, cols] = low
            wide = low.astype(F32)
            parts.append(jnp.sum(wide, axis=0, keepdims=True))
            zpack[i, :, cols] = (wide[:half] + pltpu.roll(wide[half:], hd, 1)).astype(LOW)
        wide_grad[...] += tn_dot(hid[pl.ds(at, step), :], znat[i])
        return sums + jnp.concatenate(parts, axis=1)

    sums = lax.fori_loop(0, length // step, settle, zero)
    devices = slabs.shape[0]
    own = hid.shape[1] // devices
    lane8 = lane_of(8)
    row8 = lax.broadcasted_iota(jnp.int32, (8, 128), 0)
    q_row = jnp.broadcast_to(sums[:, :128], (8, 128))
    v_row = jnp.broadcast_to(sums[:, 256:], (8, 128))
    for i in range(devices):
        begin = i * own - first_col
        q_lane = lane8 + begin
        v_lane = q_lane - 64
        q_part = pltpu.roll(q_row, lax.rem(4096 - begin, 128), 1)
        v_part = pltpu.roll(v_row, lax.rem(4096 - begin + 64, 128), 1)
        q_ok = (lane8 < own) & (q_lane >= 0) & (q_lane < limit)
        v_ok = (lane8 >= 64) & (lane8 < 64 + own) & (v_lane >= 0) & (v_lane < limit)
        line = jnp.where(q_ok, q_part, jnp.where(v_ok, v_part, 0.0))
        tile = jnp.where(row8 == 0, line, extra[i])
        tail = jnp.concatenate([tile, jnp.zeros((8, 256), F32)], axis=1)
        at = i * own
        slabs[i, : own - 8, :] = wide_grad[at : at + own - 8, :].astype(LOW)
        slabs[i, own - 8 :, :] = jnp.concatenate(
            [wide_grad[at + own - 8 : at + own, :], tail], axis=0
        ).astype(LOW)


def attend_back(order, hidden_all, proj, gnat, gpack, extra, hd, scale):
    length = proj.shape[0]
    blks, step, _ = gnat.shape
    devices = extra.shape[0]
    width = hidden_all.shape[1]
    return pl.pallas_call(
        functools.partial(attend_back_kernel, hd, scale),
        name="attend_back",
        out_shape=(
            jax.ShapeDtypeStruct((blks, step, 384), LOW),
            jax.ShapeDtypeStruct((blks, step // 2, 384), LOW),
            jax.ShapeDtypeStruct((devices, width // devices + 8, 384), LOW),
        ),
        in_specs=[spec(pltpu.SMEM), spec(ANY)] + [spec(pltpu.VMEM)] * 4,
        out_specs=(spec(pltpu.VMEM),) * 3,
        scratch_shapes=[
            pltpu.VMEM((4 * length, 128), F32),
            pltpu.VMEM((GROUP * 512, 128), F32),
            pltpu.VMEM((GROUP * 512, 128), F32),
            pltpu.VMEM((GROUP * 512, 128), F32),
            pltpu.VMEM((GROUP * 512, 128), F32),
            pltpu.VMEM((8 * length, 128), F32),
            pltpu.VMEM(hidden_all.shape, LOW),
            pltpu.VMEM((width, 384), F32),
            pltpu.SemaphoreType.DMA,
        ],
        compiler_params=pltpu.CompilerParams(vmem_limit_bytes=BIG),
        cost_estimate=pl.CostEstimate(
            flops=8 * 10**9, transcendentals=0, bytes_accessed=120 * 10**6
        ),
    )(order, hidden_all, proj, gnat, gpack, extra)


def middle_kernel(
    hd, ceven, codd, hidden, first_hbm, outer_hbm, vecs, bias_inner, cot, mask,
    hout, resid, geven, godd, merged, extra,
    wa, wb, ctx, act, slope, ilow, first, flow, olow, unit, acc, hid_low, sums, inner_sums, sems,
):
    rows, width = hidden.shape
    ff = outer_hbm.shape[0]
    chips = ceven.shape[0]
    get_out = pltpu.make_async_copy(
        first_hbm.at[:, pl.ds(0, width)], wa.at[:, pl.ds(0, width)], sems.at[0]
    )
    get_in = pltpu.make_async_copy(
        first_hbm.at[:, pl.ds(width, ff)], wa.at[:, pl.ds(width, ff)], sems.at[1]
    )
    get_outer = pltpu.make_async_copy(outer_hbm, wb, sems.at[2])
    get_out.start()
    get_in.start()
    get_outer.start()
    half = rows // 2
    lane = lane_of(half)
    low_half = lane < hd
    for z in range(chips):
        ctx[:, z * 128 : (z + 1) * 128] = ceven[z]
    for z in range(0, chips, 2):
        here = codd[z].astype(F32)
        there = codd[z + 1].astype(F32)
        at = chips * 128 + z * 64
        ctx[:half, at : at + 128] = jnp.where(low_half, here, pltpu.roll(there, hd, 1)).astype(LOW)
        ctx[half:, at : at + 128] = jnp.where(low_half, pltpu.roll(here, hd, 1), there).astype(LOW)
    sums[...] = jnp.zeros_like(sums)
    wide = 256
    tile = 64

    def add_rows(row, value):
        sums[row : row + 1, :] += jnp.sum(value, axis=0, keepdims=True)

    get_out.wait()

    @pl.loop(0, width // wide)
    def _(n):
        at = pl.multiple_of(n * wide, wide)
        acc[:, pl.ds(at, wide)] = nn_dot(ctx[...], wa[:, pl.ds(at, wide)])

    @pl.loop(0, rows // tile)
    def _(i):
        own = pl.ds(pl.multiple_of(i * tile, tile), tile)
        value = hidden[own, :].astype(F32) + acc[own, :] + vecs[2:3, :]
        center = value - jnp.mean(value, axis=-1, keepdims=True)
        spread = jnp.mean(center * center, axis=-1, keepdims=True)
        inv = lax.rsqrt(spread + epsilon)
        norm = center * inv * vecs[3:4, :] + vecs[4:5, :]
        first[own, :] = norm
        flow[own, :] = norm.astype(LOW)
        unit[own, :] = center * inv
        resid[own, 0:128] = jnp.broadcast_to(inv, (tile, 128))

    get_in.wait()

    @pl.loop(0, ff // wide)
    def _(j):
        at = pl.multiple_of(j * wide, wide)
        cols = pl.ds(at, wide)
        pre = nn_dot(flow[...], wa[:, pl.ds(width + at, wide)]) + bias_inner[0:1, cols]
        gate = 0.5 + 0.5 * lax.erf(pre * (0.5**0.5))
        act[:, cols] = (pre * gate).astype(LOW)
        slope[:, cols] = gate + pre * jnp.exp(-0.5 * pre * pre) * (0.5 / math.pi) ** 0.5

    get_outer.wait()

    @pl.loop(0, width // wide)
    def _(n):
        at = pl.multiple_of(n * wide, wide)
        acc[:, pl.ds(at, wide)] = nn_dot(act[...], wb[:, pl.ds(at, wide)])

    @pl.loop(0, rows // tile)
    def _(i):
        own = pl.ds(pl.multiple_of(i * tile, tile), tile)
        value = first[own, :] + acc[own, :] + vecs[5:6, :]
        center = value - jnp.mean(value, axis=-1, keepdims=True)
        spread = jnp.mean(center * center, axis=-1, keepdims=True)
        inv = lax.rsqrt(spread + epsilon)
        norm = center * inv
        hout[own, :] = (norm * vecs[6:7, :] + vecs[7:8, :]).astype(LOW)
        out_grad = cot[own, :].astype(F32) * mask[own, :].astype(F32)
        pull = out_grad * vecs[6:7, :]
        pull = pull - jnp.mean(pull, axis=-1, keepdims=True) - norm * jnp.mean(
            pull * norm, axis=-1, keepdims=True
        )
        grad = pull * inv
        low = grad.astype(LOW)
        first[own, :] = grad
        olow[own, :] = low
        add_rows(4, low.astype(F32))
        add_rows(5, out_grad * norm)
        add_rows(6, out_grad)

    @pl.loop(0, ff // wide)
    def _(j):
        cols = pl.ds(pl.multiple_of(j * wide, wide), wide)
        low = (nt_dot(olow[...], wb[cols, :]) * slope[:, cols]).astype(LOW)
        ilow[:, cols] = low
        inner_sums[0:1, cols] = jnp.sum(low.astype(F32), axis=0, keepdims=True)

    @pl.loop(0, width // wide)
    def _(n):
        at = pl.multiple_of(n * wide, wide)
        acc[:, pl.ds(at, wide)] = nt_dot(ilow[...], wa[pl.ds(at, wide), width:])

    @pl.loop(0, rows // tile)
    def _(i):
        own = pl.ds(pl.multiple_of(i * tile, tile), tile)
        grad = acc[own, :] + first[own, :]
        norm = unit[own, :]
        inv = resid[own, 0:1]
        pull = grad * vecs[3:4, :]
        pull = pull - jnp.mean(pull, axis=-1, keepdims=True) - norm * jnp.mean(
            pull * norm, axis=-1, keepdims=True
        )
        back = pull * inv
        low = back.astype(LOW)
        resid[own, :] = back
        hid_low[own, :] = low
        add_rows(1, low.astype(F32))
        add_rows(2, grad * norm)
        add_rows(3, grad)

    @pl.loop(0, width // wide)
    def _(n):
        at = pl.multiple_of(n * wide, wide)
        acc[:, pl.ds(at, wide)] = nt_dot(hid_low[...], wa[pl.ds(at, wide), :width])

    for z in range(chips):
        geven[z] = acc[:, z * 128 : (z + 1) * 128].astype(LOW)
    for z in range(0, chips, 2):
        at = chips * 128 + z * 64
        top = acc[:half, at : at + 128]
        bottom = acc[half:, at : at + 128]
        godd[z] = jnp.where(low_half, top, pltpu.roll(bottom, hd, 1)).astype(LOW)
        godd[z + 1] = jnp.where(low_half, pltpu.roll(top, hd, 1), bottom).astype(LOW)

    devices = merged.shape[0]
    own_rows = width // devices
    outer_rows = ff // devices
    block = 384
    per = block // outer_rows

    @pl.loop(0, ff // block)
    def _(j):
        part = tn_dot(act[:, pl.ds(pl.multiple_of(j * block, block), block)], olow[...])
        for i in range(per):
            merged[j * per + i, :outer_rows, :] = part[
                i * outer_rows : (i + 1) * outer_rows, :
            ].astype(LOW)

    folds = ff // width
    many = block // own_rows

    @pl.loop(0, width // block)
    def _(m):
        cols = pl.ds(pl.multiple_of(m * block, block), block)
        for h in range(0, folds, 2):
            left = tn_dot(flow[:, cols], ilow[:, h * width : (h + 1) * width])
            right = tn_dot(flow[:, cols], ilow[:, (h + 1) * width : (h + 2) * width])
            at = outer_rows + h * own_rows
            for i in range(many):
                for r in range(0, own_rows, 8):
                    base = i * own_rows + r
                    merged[m * many + i, at + 2 * r : at + 2 * r + 16, :] = jnp.concatenate(
                        [left[base : base + 8, :], right[base : base + 8, :]], axis=0
                    ).astype(LOW)
        part = tn_dot(ctx[:, cols], hid_low[...])
        at = outer_rows + folds * own_rows
        for i in range(many):
            base = i * own_rows
            merged[m * many + i, at : at + 16, :] = part[base : base + 16, :].astype(LOW)
            merged[m * many + i, at + 16 : at + 32, :] = jnp.concatenate(
                [part[base + 16 : base + 24, :], jnp.zeros((8, width), F32)], axis=0
            ).astype(LOW)

    row8 = lax.broadcasted_iota(jnp.int32, (8, 128), 0)
    for i in range(devices):
        piece = sums[:, i * own_rows : (i + 1) * own_rows]
        piece = jnp.concatenate([piece, jnp.zeros((8, 128 - own_rows), F32)], axis=1)
        inner = inner_sums[0:1, i * outer_rows : (i + 1) * outer_rows]
        inner = jnp.concatenate([inner, jnp.zeros((1, 128 - outer_rows), F32)], axis=1)
        extra[i] = jnp.where(row8 == 7, jnp.broadcast_to(inner, (8, 128)), piece)


def middle(ceven, codd, hidden, first_half, outer_full, vecs, bias_inner, cot, mask, devices, hd):
    rows, width = hidden.shape
    ff = outer_full.shape[0]
    slab = ff // devices + (ff // width + 1) * (width // devices) + 8
    wide_low = pltpu.VMEM((rows, width), LOW)
    wide_f32 = pltpu.VMEM((rows, width), F32)
    return pl.pallas_call(
        functools.partial(middle_kernel, hd),
        name="middle",
        out_shape=(
            jax.ShapeDtypeStruct((rows, width), LOW),
            jax.ShapeDtypeStruct((rows, width), F32),
            jax.ShapeDtypeStruct(ceven.shape, LOW),
            jax.ShapeDtypeStruct(codd.shape, LOW),
            jax.ShapeDtypeStruct((devices, slab, width), LOW),
            jax.ShapeDtypeStruct((devices, 8, 128), F32),
        ),
        in_specs=[spec(pltpu.VMEM)] * 3 + [spec(ANY)] * 2 + [spec(pltpu.VMEM)] * 4,
        out_specs=(spec(pltpu.VMEM),) * 6,
        scratch_shapes=[
            pltpu.VMEM(first_half.shape, LOW),
            pltpu.VMEM(outer_full.shape, LOW),
            wide_low,
            pltpu.VMEM((rows, ff), LOW),
            pltpu.VMEM((rows, ff), F32),
            pltpu.VMEM((rows, ff), LOW),
            wide_f32, wide_low, wide_low, wide_f32, wide_f32, wide_low,
            pltpu.VMEM((8, width), F32),
            pltpu.VMEM((8, ff), F32),
            pltpu.SemaphoreType.DMA((3,)),
        ],
        compiler_params=pltpu.CompilerParams(vmem_limit_bytes=BIG),
        cost_estimate=pl.CostEstimate(
            flops=17 * 10**9, transcendentals=0, bytes_accessed=40 * 10**6
        ),
    )(ceven, codd, hidden, first_half, outer_full, vecs, bias_inner, cot, mask)


def final_kernel(
    hd, zeven, zodd, proj_hbm, resid, proj_grads, shares,
    out, gq, gk, gv, go, gi, gu, g0, g1, g2, g3, g4, g5, g6, g7, g8, wp, triple, sem,
):
    rows, width = resid.shape
    chips = zeven.shape[0]
    fetch = pltpu.make_async_copy(proj_hbm, wp, sem)
    fetch.start()
    half = rows // 2
    low_half = lane_of(half) < hd
    for t in range(3):
        cols = slice(t * 128, (t + 1) * 128)
        for z in range(chips):
            at = t * width + z * 128
            triple[:, at : at + 128] = zeven[z, :, cols]
        for z in range(0, chips, 2):
            at = t * width + chips * 128 + z * 64
            here = zodd[z, :, cols].astype(F32)
            there = zodd[z + 1, :, cols].astype(F32)
            triple[:half, at : at + 128] = jnp.where(
                low_half, here, pltpu.roll(there, hd, 1)
            ).astype(LOW)
            triple[half:, at : at + 128] = jnp.where(
                low_half, pltpu.roll(here, hd, 1), there
            ).astype(LOW)
    own = gq.shape[0]
    keep = lane_of(own) < hd
    for t, ref in enumerate((gq, gk, gv)):
        cols = slice(t * 128, (t + 1) * 128)
        for z in range(chips):
            ref[:, z * 128 : (z + 1) * 128] = proj_grads[2 * z, :, cols].astype(F32)[:own]
        for z in range(0, chips, 2):
            here = proj_grads[2 * z + 1, :, cols].astype(F32)[:own]
            there = proj_grads[2 * z + 3, :, cols].astype(F32)[:own]
            at = chips * 128 + z * 64
            ref[:, at : at + 128] = jnp.where(keep, here, pltpu.roll(there, hd, 1))
    ff = gi.shape[1]
    outer_rows = gu.shape[0]
    folds = ff // width

    def share(at, size):
        total = shares[0, at : at + size, :].astype(F32)
        for z in range(1, chips):
            total = total + shares[z, at : at + size, :].astype(F32)
        return total

    for r in range(0, outer_rows, 16):
        gu[r : r + 16, :] = share(r, 16)
    for h in range(0, folds, 2):
        at = outer_rows + h * own
        for r in range(0, own, 8):
            pair = share(at + 2 * r, 16)
            gi[r : r + 8, h * width : (h + 1) * width] = pair[:8]
            gi[r : r + 8, (h + 1) * width : (h + 2) * width] = pair[8:]
    at = outer_rows + folds * own
    go[...] = share(at, own + 8)[:own]
    total = proj_grads[0, :, :128].astype(F32)[own:]
    for d in range(1, 2 * chips):
        total = total + proj_grads[d, :, :128].astype(F32)[own:]
    g0[...] = total[0, :own]
    g1[...] = total[0, 64 : 64 + own]
    for v, ref in enumerate((g2, g3, g4)):
        ref[...] = total[1 + v, :own]
    g5[...] = total[7, : g5.shape[0]]
    for v, ref in enumerate((g6, g7, g8)):
        ref[...] = total[4 + v, :own]
    fetch.wait()
    wide = 256

    @pl.loop(0, width // wide)
    def _(n):
        at = pl.multiple_of(n * wide, wide)
        cols = pl.ds(at, wide)
        out[:, cols] = nt_dot(triple[...], wp[pl.ds(at, wide), :]) + resid[:, cols]


def final(zeven, zodd, projections, resid, proj_grads, shares, own, ff, hd):
    rows, width = resid.shape
    mats = [(rows, width)] + [(own, width)] * 4 + [(own, ff), (ff * own // width, width)]
    vectors = [(own,)] * 5 + [(ff * own // width,)] + [(own,)] * 3
    return pl.pallas_call(
        functools.partial(final_kernel, hd),
        name="final",
        out_shape=tuple(jax.ShapeDtypeStruct(shape, F32) for shape in mats + vectors),
        in_specs=[spec(pltpu.VMEM)] * 2 + [spec(ANY)] + [spec(pltpu.VMEM)] * 3,
        out_specs=(spec(pltpu.VMEM),) * 16,
        scratch_shapes=[
            pltpu.VMEM(projections.shape, LOW),
            pltpu.VMEM((rows, 3 * width), LOW),
            pltpu.SemaphoreType.DMA,
        ],
        compiler_params=pltpu.CompilerParams(vmem_limit_bytes=BIG),
        cost_estimate=pl.CostEstimate(
            flops=2 * 10**9, transcendentals=0, bytes_accessed=12 * 10**6
        ),
    )(zeven, zodd, projections, resid, proj_grads, shares)


def prelude_kernel(
    hd, q, k, v, o, inner, outer, b0, b1, b2, b3, b4, b5, b6, b7, b8,
    slabs, first_half, outer_low, projections, tile,
):
    own, width = q.shape
    chips = slabs.shape[0] // 2
    first_half[:, :width] = o[...].astype(LOW)
    first_half[:, width:] = inner[...].astype(LOW)
    outer_low[...] = outer[...].astype(LOW)
    for t, ref in enumerate((q, k, v)):
        projections[:, t * width : (t + 1) * width] = ref[...].astype(LOW)
    tile[...] = jnp.zeros_like(tile)
    for i, ref in enumerate((b0, b1, b2, b3, b4, b5, b6, b7)):
        tile[i : i + 1, :own] = ref[...].reshape(1, own)
    tile[0:1, 128 : 128 + b8.shape[0]] = b8[...].reshape(1, b8.shape[0])
    keep = lane_of(own) < hd
    for t, ref in enumerate((q, k, v)):
        cols = slice(t * 128, (t + 1) * 128)
        below = tile[:, cols]
        for d in range(2 * chips):
            z = d // 2
            if d % 2 == 0:
                part = ref[:, z * 128 : (z + 1) * 128]
            else:
                at = chips * 128 + z // 2 * 128
                part = ref[:, at : at + 128]
                if z % 2:
                    part = pltpu.roll(part, hd, 1)
                part = jnp.where(keep, part, 0.0)
            slabs[d, :16, cols] = part[:16].astype(LOW)
            slabs[d, 16:, cols] = jnp.concatenate([part[16:], below], axis=0).astype(LOW)


def prelude(weights, vectors, blks, hd):
    own, width = weights[0].shape
    ff = weights[4].shape[1]
    return pl.pallas_call(
        functools.partial(prelude_kernel, hd),
        name="prelude",
        out_shape=(
            jax.ShapeDtypeStruct((blks, own + 8, 384), LOW),
            jax.ShapeDtypeStruct((own, width + ff), LOW),
            jax.ShapeDtypeStruct(weights[5].shape, LOW),
            jax.ShapeDtypeStruct((own, 3 * width), LOW),
        ),
        in_specs=[spec(pltpu.VMEM)] * 15,
        out_specs=(spec(pltpu.VMEM),) * 4,
        scratch_shapes=[pltpu.VMEM((8, 384), F32)],
        cost_estimate=pl.CostEstimate(flops=10**6, transcendentals=0, bytes_accessed=3 * 10**6),
    )(*weights, *vectors)


def fast_body(seqs, blks, heads):
    def run(
        hidden_in, query_weight, key_weight, value_weight, output_weight, inner_weight,
        outer_weight, query_bias, value_bias, output_bias, attention_gain, attention_shift,
        inner_bias, outer_bias, final_gain, final_shift, cotangent, grad_mask, cluster_order,
    ):
        rows, width = hidden_in.shape
        own = query_weight.shape[0]
        hidden_units = inner_weight.shape[1]
        length = cluster_order.shape[2]
        hd = width // heads
        chips = blks // 2
        scale = 1.0 / math.sqrt(hd)
        devices = seqs * blks
        b = lax.axis_index("blk")
        k = b // 2
        even_core = lax.rem(b, 2) == 0
        slabs, half_own, outer_own, proj_own = prelude(
            (query_weight, key_weight, value_weight, output_weight, inner_weight, outer_weight),
            (
                query_bias, value_bias, output_bias, attention_gain, attention_shift,
                outer_bias, final_gain, final_shift, inner_bias,
            ),
            blks,
            hd,
        )
        hidden_all, gathered, first_half, outer_full, projections = entry(
            hidden_in, slabs, (half_own, outer_own, proj_own), seqs, blks, 2
        )
        first_half = first_half.reshape(width, width + hidden_units)
        outer_full = outer_full.reshape(hidden_units, width)
        projections = projections.reshape(width, 3 * width)
        hidden_all = hidden_all.reshape(length, width)
        gathered = gathered.reshape((devices,) + slabs.shape[1:])
        order = cluster_order[0]
        head_first = jnp.where(even_core, 2 * k, 2 * chips + k)
        order_own = jnp.concatenate(
            [
                lax.dynamic_index_in_dim(order, head_first, 0, keepdims=False),
                lax.dynamic_index_in_dim(order, 2 * k + 1, 0, keepdims=False),
            ]
        )
        proj, cnat, cpack, vecs, bias_inner = attend(
            order_own, hidden_all, gathered, blks, hidden_units, hd, scale
        )
        ceven, codd = return_rows(cnat, cpack, 1)
        hidden_out, residual_grad, geven, godd, merged, extra = middle(
            ceven, codd, hidden_in, first_half, outer_full, vecs, bias_inner, cotangent,
            grad_mask, devices, hd,
        )
        slab = merged.shape[1:]
        gnat, gpack, summed = spread_rows(
            geven, godd, merged.reshape((seqs * chips, 2) + slab), 2
        )
        znat, zpack, grads = attend_back(
            order_own, hidden_all, proj, gnat, gpack, extra, hd, scale
        )
        pieces = 2
        zeven, zodd, proj_grads, big_grads = leave(
            znat, zpack, grads.reshape((seqs, blks) + grads.shape[1:]),
            summed.reshape(seqs, chips, pieces, slab[0] // pieces, width),
        )
        return (hidden_out,) + tuple(
            final(
                zeven, zodd, projections, residual_grad, proj_grads,
                big_grads.reshape((chips,) + slab), own, hidden_units, hd,
            )
        )

    return run


def masked_scores(left, right, left_ids, right_ids, scale):
    scores = back_product(left, right) * scale
    return jnp.where(left_ids[:, None] == right_ids[None, :], scores, -jnp.inf)


def body(
    hidden_in,
    query_weight,
    key_weight,
    value_weight,
    output_weight,
    inner_weight,
    outer_weight,
    query_bias,
    value_bias,
    output_bias,
    attention_gain,
    attention_shift,
    inner_bias,
    outer_bias,
    final_gain,
    final_shift,
    cotangent,
    grad_mask,
    cluster_order,
):
    rows = hidden_in.shape[0]
    width = hidden_in.shape[1]
    heads = cluster_order.shape[1]
    length = cluster_order.shape[2]
    scale = 1.0 / math.sqrt(width // heads)
    masters = (
        query_weight,
        key_weight,
        value_weight,
        output_weight,
        inner_weight,
        outer_weight,
        query_bias,
        value_bias,
        output_bias,
        attention_gain,
        attention_shift,
        inner_bias,
        outer_bias,
        final_gain,
        final_shift,
    )
    lowered = [master.astype(jnp.bfloat16) for master in masters]
    fetched = (
        lax.all_gather(lowered[0], ("seq", "blk"), axis=0, tiled=True),
        lax.all_gather(lowered[1], ("seq", "blk"), axis=0, tiled=True),
        lax.all_gather(lowered[2], ("seq", "blk"), axis=0, tiled=True),
        lax.all_gather(lowered[3], ("seq", "blk"), axis=0, tiled=True),
        lax.all_gather(lowered[4], ("seq", "blk"), axis=0, tiled=True),
        lax.all_gather(lowered[5], ("seq", "blk"), axis=0, tiled=True),
        lax.all_gather(lowered[6], ("seq", "blk"), axis=0, tiled=True),
        lax.all_gather(lowered[7], ("seq", "blk"), axis=0, tiled=True),
        lax.all_gather(lowered[8], ("seq", "blk"), axis=0, tiled=True),
        lax.all_gather(lowered[9], ("seq", "blk"), axis=0, tiled=True),
        lax.all_gather(lowered[10], ("seq", "blk"), axis=0, tiled=True),
        lax.all_gather(lowered[11], ("seq", "blk"), axis=0, tiled=True),
        lax.all_gather(lowered[12], ("seq", "blk"), axis=0, tiled=True),
        lax.all_gather(lowered[13], ("seq", "blk"), axis=0, tiled=True),
        lax.all_gather(lowered[14], ("seq", "blk"), axis=0, tiled=True),
    )
    query_full, key_full, value_full, output_full, inner_full, outer_full = fetched[0:6]
    vectors = [vector.astype(jnp.float32) for vector in fetched[6:15]]
    (
        bias_query,
        bias_value,
        bias_output,
        gain_first,
        shift_first,
        bias_inner,
        bias_outer,
        gain_final,
        shift_final,
    ) = vectors
    hidden = hidden_in.astype(jnp.float32)
    query_low = (
        jnp.dot(hidden_in, query_full, preferred_element_type=jnp.float32) + bias_query
    ).astype(jnp.bfloat16)
    keys_low = jnp.dot(hidden_in, key_full, preferred_element_type=jnp.float32).astype(jnp.bfloat16)
    values_low = (
        jnp.dot(hidden_in, value_full, preferred_element_type=jnp.float32) + bias_value
    ).astype(jnp.bfloat16)
    all_keys, all_values = (
        lax.all_gather(keys_low, "blk", axis=0, tiled=True),
        lax.all_gather(values_low, "blk", axis=0, tiled=True),
    )
    order = cluster_order[0]
    head_rows = jnp.broadcast_to(jnp.arange(heads, dtype=jnp.int32)[:, None], (heads, length))
    positions = jnp.broadcast_to(jnp.arange(length, dtype=jnp.int32)[None, :], (heads, length))
    inverse = jnp.zeros((heads, length), jnp.int32).at[head_rows, order].set(positions)
    key_cluster = inverse // CLUSTER
    member = lax.dynamic_slice_in_dim(key_cluster, lax.axis_index("blk") * rows, rows, 1)
    query_heads = head_major(query_low, heads)
    key_heads = head_major(all_keys, heads)
    value_heads = head_major(all_values, heads)
    head_ids = jnp.arange(heads, dtype=jnp.int32)

    def attend(index):
        scores = masked_scores(
            query_heads[index], key_heads[index], member[index], key_cluster[index], scale
        )
        peak = jnp.max(scores, axis=-1, keepdims=True)
        weights = jnp.exp(scores - peak)
        total = jnp.sum(weights, axis=-1, keepdims=True)
        probs_low = (weights / total).astype(jnp.bfloat16)
        mixed = jnp.dot(probs_low, value_heads[index], preferred_element_type=jnp.float32)
        return (mixed, (peak + jnp.log(total))[:, 0])

    mixed, logsum = lax.map(attend, head_ids)
    context_low = token_major(mixed).astype(jnp.bfloat16)
    attention_out = (
        jnp.dot(context_low, output_full, preferred_element_type=jnp.float32) + bias_output
    )
    first_norm, first_pull = jax.vjp(layer_norm, hidden + attention_out, gain_first, shift_first)
    first_low = first_norm.astype(jnp.bfloat16)
    inner_pre = jnp.dot(first_low, inner_full, preferred_element_type=jnp.float32) + bias_inner
    activated, gelu_pull = jax.vjp(exact_gelu, inner_pre)
    activated_low = activated.astype(jnp.bfloat16)
    outer_out = jnp.dot(activated_low, outer_full, preferred_element_type=jnp.float32) + bias_outer
    final_norm, final_pull = jax.vjp(layer_norm, first_norm + outer_out, gain_final, shift_final)
    hidden_out = final_norm.astype(jnp.bfloat16)
    out_grad = cotangent.astype(jnp.float32) * grad_mask.astype(jnp.float32)
    second_grad, grad_final_gain, grad_final_shift = final_pull(out_grad)
    outer_low = second_grad.astype(jnp.bfloat16)
    back_weights = (
        lax.all_gather(lowered[0], ("seq", "blk"), axis=0, tiled=True),
        lax.all_gather(lowered[1], ("seq", "blk"), axis=0, tiled=True),
        lax.all_gather(lowered[2], ("seq", "blk"), axis=0, tiled=True),
        lax.all_gather(lowered[3], ("seq", "blk"), axis=0, tiled=True),
        lax.all_gather(lowered[4], ("seq", "blk"), axis=0, tiled=True),
        lax.all_gather(lowered[5], ("seq", "blk"), axis=0, tiled=True),
    )
    grad_outer_weight = row_contract(activated_low, outer_low)
    grad_outer_bias = column_sum(outer_low)
    inner_low = gelu_pull(back_product(outer_low, back_weights[5]))[0].astype(jnp.bfloat16)
    grad_inner_weight = row_contract(first_low, inner_low)
    grad_inner_bias = column_sum(inner_low)
    first_grad = back_product(inner_low, back_weights[4]) + second_grad
    residual_grad, grad_attention_gain, grad_attention_shift = first_pull(first_grad)
    attn_low = residual_grad.astype(jnp.bfloat16)
    grad_output_weight = row_contract(context_low, attn_low)
    grad_output_bias = column_sum(attn_low)
    context_grad = back_product(attn_low, back_weights[3]).astype(jnp.bfloat16)
    grad_heads = head_major(context_grad, heads)

    def own_rows_back(index):
        scores = masked_scores(
            query_heads[index], key_heads[index], member[index], key_cluster[index], scale
        )
        probs = jnp.exp(scores - logsum[index][:, None])
        probs_low = probs.astype(jnp.bfloat16)
        grad_part = grad_heads[index]
        prob_grad = back_product(grad_part, value_heads[index])
        weighted = jnp.sum(probs * prob_grad, axis=-1, keepdims=True)
        score_low = (probs * (prob_grad - weighted)).astype(jnp.bfloat16)
        query_grad = (
            jnp.dot(score_low, key_heads[index], preferred_element_type=jnp.float32) * scale
        )
        return (probs_low, score_low, query_grad, weighted[:, 0])

    def attend_back(index):
        probs_low, score_low, query_grad, weighted = own_rows_back(index)
        key_sum = row_contract(score_low, query_heads[index]) * scale
        value_sum = row_contract(probs_low, grad_heads[index])
        return (query_grad, key_sum, value_sum)

    query_grads, key_grads, value_grads = lax.map(attend_back, head_ids)
    key_own, value_own = (
        lax.psum_scatter(token_major(key_grads), "blk", scatter_dimension=0, tiled=True),
        lax.psum_scatter(token_major(value_grads), "blk", scatter_dimension=0, tiled=True),
    )
    query_grad_low = token_major(query_grads).astype(jnp.bfloat16)
    key_grad_low = key_own.astype(jnp.bfloat16)
    value_grad_low = value_own.astype(jnp.bfloat16)
    grad_query_weight = row_contract(hidden_in, query_grad_low)
    grad_key_weight = row_contract(hidden_in, key_grad_low)
    grad_value_weight = row_contract(hidden_in, value_grad_low)
    grad_query_bias = column_sum(query_grad_low)
    grad_value_bias = column_sum(value_grad_low)
    input_grad = (
        back_product(query_grad_low, back_weights[0])
        + back_product(key_grad_low, back_weights[1])
        + back_product(value_grad_low, back_weights[2])
        + residual_grad
    )
    shares = (
        lax.psum_scatter(grad_query_weight, ("seq", "blk"), scatter_dimension=0, tiled=True),
        lax.psum_scatter(grad_key_weight, ("seq", "blk"), scatter_dimension=0, tiled=True),
        lax.psum_scatter(grad_value_weight, ("seq", "blk"), scatter_dimension=0, tiled=True),
        lax.psum_scatter(grad_output_weight, ("seq", "blk"), scatter_dimension=0, tiled=True),
        lax.psum_scatter(grad_inner_weight, ("seq", "blk"), scatter_dimension=0, tiled=True),
        lax.psum_scatter(grad_outer_weight, ("seq", "blk"), scatter_dimension=0, tiled=True),
        lax.psum_scatter(grad_query_bias, ("seq", "blk"), scatter_dimension=0, tiled=True),
        lax.psum_scatter(grad_value_bias, ("seq", "blk"), scatter_dimension=0, tiled=True),
        lax.psum_scatter(grad_output_bias, ("seq", "blk"), scatter_dimension=0, tiled=True),
        lax.psum_scatter(grad_attention_gain, ("seq", "blk"), scatter_dimension=0, tiled=True),
        lax.psum_scatter(grad_attention_shift, ("seq", "blk"), scatter_dimension=0, tiled=True),
        lax.psum_scatter(grad_inner_bias, ("seq", "blk"), scatter_dimension=0, tiled=True),
        lax.psum_scatter(grad_outer_bias, ("seq", "blk"), scatter_dimension=0, tiled=True),
        lax.psum_scatter(grad_final_gain, ("seq", "blk"), scatter_dimension=0, tiled=True),
        lax.psum_scatter(grad_final_shift, ("seq", "blk"), scatter_dimension=0, tiled=True),
    )
    return (hidden_out, input_grad) + tuple(shares)


def solution(mesh):
    placed = (
        P(("seq", "blk"), None),
        P(("seq", "blk"), None),
        P(("seq", "blk"), None),
        P(("seq", "blk"), None),
        P(("seq", "blk"), None),
        P(("seq", "blk"), None),
        P(("seq", "blk"), None),
        P(("seq", "blk")),
        P(("seq", "blk")),
        P(("seq", "blk")),
        P(("seq", "blk")),
        P(("seq", "blk")),
        P(("seq", "blk")),
        P(("seq", "blk")),
        P(("seq", "blk")),
        P(("seq", "blk")),
        P(("seq", "blk"), None),
        P(("seq", "blk"), None),
        P("seq", None, None),
    )
    seqs, blks = mesh.shape["seq"], mesh.shape["blk"]
    heads = 12
    fast = seqs == 4 and blks == 8
    return jax.shard_map(
        fast_body(seqs, blks, heads) if fast else body,
        mesh=mesh,
        in_specs=placed,
        out_specs=(
            P(("seq", "blk"), None),
            P(("seq", "blk"), None),
            P(("seq", "blk"), None),
            P(("seq", "blk"), None),
            P(("seq", "blk"), None),
            P(("seq", "blk"), None),
            P(("seq", "blk"), None),
            P(("seq", "blk"), None),
            P(("seq", "blk")),
            P(("seq", "blk")),
            P(("seq", "blk")),
            P(("seq", "blk")),
            P(("seq", "blk")),
            P(("seq", "blk")),
            P(("seq", "blk")),
            P(("seq", "blk")),
            P(("seq", "blk")),
        ),
        check_vma=False,
    )
```

```python
import functools
import math

import jax
import jax.numpy as jnp
from jax import lax
from jax.experimental import pallas as pl
from jax.experimental.pallas import tpu as pltpu
from jax.sharding import PartitionSpec as P

MESH = pl.DeviceIdType.MESH
ANY = pl.ANY
LOW = jnp.bfloat16
F32 = jnp.float32
BIG = 60 * 2**20
GROUP = 4
CLUSTER = 128


def spec(space):
    return pl.BlockSpec(memory_space=space)


def nt_dot(left, right):
    return lax.dot_general(left, right, (((1,), (1,)), ((), ())), preferred_element_type=F32)


def tn_dot(left, right):
    return lax.dot_general(left, right, (((0,), (0,)), ((), ())), preferred_element_type=F32)


def nn_dot(left, right):
    return jnp.dot(left, right, preferred_element_type=F32)


def greet(targets):
    sem = pltpu.get_barrier_semaphore()
    for target in targets:
        pl.semaphore_signal(sem, inc=1, device_id=target, device_id_type=MESH)
    pl.semaphore_wait(sem, len(targets))


def send(src, dst, send_sem, recv_sem, target):
    return pltpu.make_async_remote_copy(
        src_ref=src,
        dst_ref=dst,
        send_sem=send_sem,
        recv_sem=recv_sem,
        device_id=target,
        device_id_type=MESH,
    )


epsilon = 1e-06


def layer_norm(value, gain, shift):
    center = value - jnp.mean(value, axis=-1, keepdims=True)
    spread = jnp.mean(center * center, axis=-1, keepdims=True)
    return center * lax.rsqrt(spread + epsilon) * gain + shift


def exact_gelu(value):
    return jax.nn.gelu(value, approximate=False)


def row_contract(left, right):
    return lax.dot_general(
        left, right, (((0,), (0,)), ((), ())), preferred_element_type=jnp.float32
    )


def back_product(grad, weight):
    return lax.dot_general(
        grad, weight, (((1,), (1,)), ((), ())), preferred_element_type=jnp.float32
    )


def column_sum(value):
    return jnp.sum(value.astype(jnp.float32), axis=0)


def head_major(value, heads):
    return value.reshape(value.shape[0], heads, -1).transpose(1, 0, 2)


def token_major(value):
    return value.transpose(1, 0, 2).reshape(value.shape[1], value.shape[0] * value.shape[2])


def entry_kernel(
    seqs, blks, parts, x_ref, w_ref, a0, a1, a2, o_ref, wall_ref, f0, f1, f2,
    own_sem, ssem, rsem, wl, ws, wr, us, ur, al, zs, zr, ns, nr, ms, mr,
):
    half = blks // 2
    s = lax.axis_index("seq")
    b = lax.axis_index("blk")
    k = b // 2
    c = lax.rem(b, 2)
    mate = b + 1 - 2 * c
    left = lax.rem(b + blks - 2, blks)
    right = lax.rem(b + 2, blks)
    has_left = k > 0
    has_right = k < half - 1
    blk_peers = [{"blk": lax.rem(b + d, blks)} for d in range(1, blks)]
    seq_peers = [{"seq": lax.rem(s + d, seqs)} for d in range(1, seqs)]
    greet(blk_peers + seq_peers)

    def slab(d):
        peer = lax.rem(b + d, blks)
        return send(w_ref.at[peer], wall_ref.at[s, b], ws.at[d], wr.at[d], {"blk": peer})

    def group(d):
        return send(
            wall_ref.at[s], wall_ref.at[s], us.at[d], ur.at[d], {"seq": lax.rem(s + d, seqs)}
        )

    def piece(src, blk, p, to, way):
        return send(src, o_ref.at[blk, p], ssem.at[way, blk, p], rsem.at[blk, p], {"blk": to})

    shards = ((a0, f0), (a1, f1), (a2, f2))
    x_next = s + 1 - 2 * lax.rem(s, 2)
    y_next = s + 2 - 4 * (s // 2)
    across = 3 - s
    low_part = pl.ds(0, half // 2)
    high_part = pl.ds(half // 2, half // 2)

    def along(a, d):
        own_ref, full = shards[a]
        to = 2 * lax.rem(k + d, half) + c
        return send(own_ref, full.at[s, k, c], zs.at[a, d], zr.at[a, d], {"blk": to})

    def beside(a, way):
        full = shards[a][1]
        whole = full.at[s, :, c]
        if way == 0:
            return send(whole, whole, ns.at[a, 0], nr.at[a, 0], {"seq": x_next})
        if way == 1:
            return send(whole, whole, ns.at[a, 1], nr.at[a, 1], {"seq": y_next})
        if way == 2:
            part = full.at[y_next, low_part, c]
            return send(part, part, ns.at[a, 2], nr.at[a, 2], {"seq": x_next})
        part = full.at[x_next, high_part, c]
        return send(part, part, ns.at[a, 3], nr.at[a, 3], {"seq": y_next})

    def pair(a, i, src):
        part = shards[a][1].at[src, :, c]
        return send(part, part, ms.at[a, i], mr.at[a, i], {"blk": mate})

    for d in range(1, blks):
        slab(d).start()
    for a in range(3):
        for d in range(1, half):
            along(a, d).start()
        pltpu.make_async_copy(shards[a][0], shards[a][1].at[s, k, c], al.at[a]).start()
    own_slab = pltpu.make_async_copy(w_ref.at[b], wall_ref.at[s, b], wl)
    own_slab.start()
    for p in range(parts):
        @pl.when(has_left)
        def _():
            piece(x_ref.at[p], b, p, left, 0).start()

        @pl.when(has_right)
        def _():
            piece(x_ref.at[p], b, p, right, 1).start()
    for p in range(parts):
        piece(x_ref.at[p], b, p, mate, 2).start()
    own = pltpu.make_async_copy(x_ref, o_ref.at[b], own_sem)
    own.start()
    own_slab.wait()
    for d in range(1, blks):
        slab(d).wait_recv()
    for d in range(1, seqs):
        group(d).start()
    for a in range(3):
        pltpu.make_async_copy(shards[a][0], shards[a][1].at[s, k, c], al.at[a]).wait()
        for d in range(1, half):
            along(a, d).wait_recv()
        beside(a, 0).start()
        beside(a, 1).start()
        pair(a, 0, s).start()

    def second(a):
        beside(a, 1).wait_recv()
        beside(a, 2).start()
        pair(a, 2, y_next).start()
        beside(a, 0).wait_recv()
        beside(a, 3).start()
        pair(a, 1, x_next).start()

    for t in range(1, half):
        for p in range(parts):
            @pl.when(k - t >= 0)
            def _():
                blk = b - 2 * t
                piece(o_ref.at[blk, p], blk, p, right, 1).wait_recv()

                @pl.when(has_right)
                def _():
                    piece(o_ref.at[blk, p], blk, p, right, 1).start()

                piece(o_ref.at[blk, p], blk, p, mate, 2).start()

            @pl.when(k + t < half)
            def _():
                blk = b + 2 * t
                piece(o_ref.at[blk, p], blk, p, left, 0).wait_recv()

                @pl.when(has_left)
                def _():
                    piece(o_ref.at[blk, p], blk, p, left, 0).start()

                piece(o_ref.at[blk, p], blk, p, mate, 2).start()

        second(t - 1)
    for a in range(3):
        beside(a, 2).wait_recv()
        beside(a, 3).wait_recv()
        pair(a, 3, across).start()
    for j in range(half):
        blk = 2 * j + 1 - c
        for p in range(parts):
            piece(o_ref.at[blk, p], blk, p, mate, 2).wait_recv()
    for j in range(half):
        blk = 2 * j + c
        for p in range(parts):
            piece(o_ref.at[blk, p], blk, p, mate, 2).wait_send()

            @pl.when(jnp.logical_and(has_right, j <= k))
            def _():
                piece(o_ref.at[blk, p], blk, p, right, 1).wait_send()

            @pl.when(jnp.logical_and(has_left, j >= k))
            def _():
                piece(o_ref.at[blk, p], blk, p, left, 0).wait_send()
    own.wait()
    for d in range(1, blks):
        slab(d).wait_send()
    for d in range(1, seqs):
        group(d).wait()
    for a in range(3):
        for i, src in enumerate((s, x_next, y_next, across)):
            pair(a, i, src).wait()
        for way in range(4):
            beside(a, way).wait_send()
        for d in range(1, half):
            along(a, d).wait_send()


def entry(hidden, slabs, shards, seqs, blks, parts):
    rows, width = hidden.shape
    dma = pltpu.SemaphoreType.DMA
    return pl.pallas_call(
        functools.partial(entry_kernel, seqs, blks, parts),
        name="entry",
        out_shape=(
            jax.ShapeDtypeStruct((blks, parts, rows // parts, width), LOW),
            jax.ShapeDtypeStruct((seqs,) + slabs.shape, LOW),
        )
        + tuple(jax.ShapeDtypeStruct((seqs, blks // 2, 2) + x.shape, LOW) for x in shards),
        in_specs=[spec(pltpu.VMEM)] * 5,
        out_specs=(spec(ANY),) * 5,
        scratch_shapes=[
            dma, dma((3, blks, parts)), dma((blks, parts)), dma,
            dma((blks,)), dma((blks,)), dma((seqs,)), dma((seqs,)),
            dma((3,)), dma((3, blks // 2)), dma((3, blks // 2)),
            dma((3, 4)), dma((3, 4)), dma((3, 4)), dma((3, 4)),
        ],
        compiler_params=pltpu.CompilerParams(collective_id=0, has_side_effects=True),
        cost_estimate=pl.CostEstimate(flops=0, transcendentals=0, bytes_accessed=200 * 10**6),
    )(hidden.reshape(parts, rows // parts, width), slabs, *shards)


def return_kernel(blks, nat_ref, pack_ref, even_ref, odd_ref, buf, lsem, ssem, rsem):
    b = lax.axis_index("blk")
    k = b // 2
    c = lax.rem(b, 2)
    greet([{"blk": lax.rem(b + d, blks)} for d in range(1, blks)])
    start_return(blks, b, k, c, nat_ref, pack_ref, even_ref, odd_ref, buf, lsem, ssem, rsem)
    finish_return(blks, b, k, c, nat_ref, pack_ref, even_ref, odd_ref, ssem, rsem)


def full_way(blks, b, d, nat_ref, even_ref, ssem, rsem, slot):
    peer = lax.rem(b + d, blks)
    return send(nat_ref.at[peer], even_ref.at[slot], ssem.at[d], rsem.at[d], {"blk": peer})


def start_return(blks, b, k, c, nat_ref, pack_ref, even_ref, odd_ref, buf, lsem, ssem, rsem):
    @pl.when(c == 0)
    def _():
        for d in range(1, blks):
            full_way(blks, b, d, nat_ref, even_ref, ssem, rsem, k).start()
        inward = pltpu.make_async_copy(nat_ref.at[b], buf, lsem)
        inward.start()
        inward.wait()
        outward = pltpu.make_async_copy(buf, even_ref.at[k], lsem)
        outward.start()
        outward.wait()

    @pl.when(c == 1)
    def _():
        for d in range(1, blks):
            full_way(blks, b, d, pack_ref, odd_ref, ssem, rsem, k).start()
        part = buf.at[pl.ds(0, pack_ref.shape[1])]
        inward = pltpu.make_async_copy(pack_ref.at[b], part, lsem)
        inward.start()
        inward.wait()
        outward = pltpu.make_async_copy(part, odd_ref.at[k], lsem)
        outward.start()
        outward.wait()


def finish_return(blks, b, k, c, nat_ref, pack_ref, even_ref, odd_ref, ssem, rsem):
    for d in range(1, blks):
        source = lax.rem(b + blks - d, blks)

        @pl.when(lax.rem(source, 2) == 0)
        def _():
            full_way(blks, b, d, nat_ref, even_ref, ssem, rsem, source // 2).wait_recv()

        @pl.when(lax.rem(source, 2) == 1)
        def _():
            full_way(blks, b, d, pack_ref, odd_ref, ssem, rsem, source // 2).wait_recv()

    @pl.when(c == 0)
    def _():
        for d in range(1, blks):
            full_way(blks, b, d, nat_ref, even_ref, ssem, rsem, k).wait_send()

    @pl.when(c == 1)
    def _():
        for d in range(1, blks):
            full_way(blks, b, d, pack_ref, odd_ref, ssem, rsem, k).wait_send()


def return_rows(nat, pack, collective_id):
    blks = nat.shape[0]
    dma = pltpu.SemaphoreType.DMA
    return pl.pallas_call(
        functools.partial(return_kernel, blks),
        name="return_rows",
        out_shape=(
            jax.ShapeDtypeStruct((blks // 2,) + nat.shape[1:], LOW),
            jax.ShapeDtypeStruct((blks // 2,) + pack.shape[1:], LOW),
        ),
        in_specs=[spec(ANY)] * 2,
        out_specs=(spec(ANY), spec(ANY)),
        scratch_shapes=[pltpu.VMEM(nat.shape[1:], LOW), dma, dma((blks,)), dma((blks,))],
        compiler_params=pltpu.CompilerParams(collective_id=collective_id, has_side_effects=True),
        cost_estimate=pl.CostEstimate(flops=0, transcendentals=0, bytes_accessed=80 * 10**6),
    )(nat, pack)


def spread_kernel(
    blks, even_ref, odd_ref, grad_ref, nat_ref, pack_ref, total_hbm,
    buf, mine, theirs, total, lsem, ssem, rsem, ml, ms, mr, tl,
):
    b = lax.axis_index("blk")
    c = lax.rem(b, 2)
    mate = b + 1 - 2 * c
    greet([{"blk": lax.rem(b + d, blks)} for d in range(1, blks)])
    swap = send(grad_ref.at[:, 1 - c], theirs, ms, mr, {"blk": mate})
    swap.start()
    load = pltpu.make_async_copy(grad_ref.at[:, c], mine, ml)
    load.start()

    def full(d, slot):
        peer = lax.rem(b + d, blks)
        return send(
            even_ref.at[peer // 2], nat_ref.at[slot], ssem.at[d], rsem.at[d], {"blk": peer}
        )

    def packed(d, slot):
        peer = lax.rem(b + d, blks)
        return send(
            odd_ref.at[peer // 2], pack_ref.at[slot], ssem.at[d], rsem.at[d], {"blk": peer}
        )

    for d in range(1, blks):
        to_even = lax.rem(b + d, 2) == 0

        @pl.when(to_even)
        def _():
            full(d, b).start()

        @pl.when(jnp.logical_not(to_even))
        def _():
            packed(d, b).start()

    load.wait()
    swap.wait()

    @pl.loop(0, total.shape[0])
    def _(o):
        total[o] = (mine[o].astype(F32) + theirs[o].astype(F32)).astype(LOW)

    store = pltpu.make_async_copy(total, total_hbm, tl)
    store.start()

    @pl.when(c == 0)
    def _():
        inward = pltpu.make_async_copy(even_ref.at[b // 2], buf, lsem)
        inward.start()
        inward.wait()
        outward = pltpu.make_async_copy(buf, nat_ref.at[b], lsem)
        outward.start()
        outward.wait()
        for d in range(1, blks):
            full(d, lax.rem(b + blks - d, blks)).wait_recv()

    @pl.when(c == 1)
    def _():
        part = buf.at[pl.ds(0, odd_ref.shape[1])]
        inward = pltpu.make_async_copy(odd_ref.at[b // 2], part, lsem)
        inward.start()
        inward.wait()
        outward = pltpu.make_async_copy(part, pack_ref.at[b], lsem)
        outward.start()
        outward.wait()
        for d in range(1, blks):
            packed(d, lax.rem(b + blks - d, blks)).wait_recv()

    for d in range(1, blks):
        to_even = lax.rem(b + d, 2) == 0

        @pl.when(to_even)
        def _():
            full(d, b).wait_send()

        @pl.when(jnp.logical_not(to_even))
        def _():
            packed(d, b).wait_send()

    store.wait()


def spread_rows(even, odd, grads, collective_id):
    blks = 2 * even.shape[0]
    half_shape = grads.shape[:1] + grads.shape[2:]
    dma = pltpu.SemaphoreType.DMA
    return pl.pallas_call(
        functools.partial(spread_kernel, blks),
        name="spread_rows",
        out_shape=(
            jax.ShapeDtypeStruct((blks,) + even.shape[1:], LOW),
            jax.ShapeDtypeStruct((blks,) + odd.shape[1:], LOW),
            jax.ShapeDtypeStruct(half_shape, LOW),
        ),
        in_specs=[spec(ANY)] * 3,
        out_specs=(spec(ANY),) * 3,
        scratch_shapes=[
            pltpu.VMEM(even.shape[1:], LOW),
            pltpu.VMEM(half_shape, LOW),
            pltpu.VMEM(half_shape, LOW),
            pltpu.VMEM(half_shape, LOW),
            dma, dma((blks,)), dma((blks,)), dma, dma, dma, dma,
        ],
        compiler_params=pltpu.CompilerParams(
            collective_id=collective_id, has_side_effects=True, vmem_limit_bytes=BIG
        ),
        cost_estimate=pl.CostEstimate(flops=0, transcendentals=0, bytes_accessed=80 * 10**6),
    )(even, odd, grads)


def exit_kernel(
    seqs, blks, nat_ref, pack_ref, grad_ref, big_ref, even_ref, odd_ref, out_ref, big_out,
    buf, stage, total, big_stage, big_total,
    lsem, ssem, rsem, us, ur, gl, gs, gr, bl, bu, bv, cl, cs, cr,
):
    s = lax.axis_index("seq")
    b = lax.axis_index("blk")
    k = b // 2
    c = lax.rem(b, 2)
    blk_peers = [{"blk": lax.rem(b + d, blks)} for d in range(1, blks)]
    seq_peers = [{"seq": lax.rem(s + d, seqs)} for d in range(1, seqs)]
    greet(blk_peers + seq_peers)

    def group(d):
        peer = lax.rem(s + d, seqs)
        return send(grad_ref.at[peer], stage.at[d], us.at[d], ur.at[d], {"seq": peer})

    def slab(d):
        peer = lax.rem(b + d, blks)
        return send(total.at[peer], out_ref.at[b], gs.at[d], gr.at[d], {"blk": peer})

    chips = blks // 2
    pieces = big_ref.shape[2]

    def big_group(p, d):
        peer = lax.rem(s + d, seqs)
        return send(
            big_ref.at[peer, :, p], big_stage.at[p, d], bu.at[p, d], bv.at[p, d], {"seq": peer}
        )

    def big_slab(p, d):
        to = lax.rem(k + d, chips)
        return send(
            big_total.at[p, to], big_out.at[k, p], cs.at[p, d], cr.at[p, d], {"blk": 2 * to + c}
        )

    def big_own(p):
        return pltpu.make_async_copy(big_ref.at[s, :, p], big_stage.at[p, 0], bl.at[p])

    for p in range(pieces):
        big_own(p).start()
    for d in range(1, seqs):
        group(d).start()
    for p in range(pieces):
        for d in range(1, seqs):
            big_group(p, d).start()
    start_return(blks, b, k, c, nat_ref, pack_ref, even_ref, odd_ref, buf, lsem, ssem, rsem)
    for d in range(1, seqs):
        group(d).wait_recv()
    for o in range(blks):
        acc = grad_ref[s, o].astype(F32)
        for d in range(1, seqs):
            acc = acc + stage[d, o].astype(F32)
        total[o] = acc.astype(LOW)
    for d in range(1, blks):
        slab(d).start()
    own = pltpu.make_async_copy(total.at[b], out_ref.at[b], gl)
    own.start()
    own.wait()
    for p in range(pieces):
        big_own(p).wait()
        for d in range(1, seqs):
            big_group(p, d).wait_recv()

        @pl.loop(0, chips)
        def _(o):
            acc = big_stage[p, 0, o].astype(F32)
            for d in range(1, seqs):
                acc = acc + big_stage[p, d, o].astype(F32)
            big_total[p, o] = acc.astype(LOW)

        for d in range(1, chips):
            big_slab(p, d).start()
        keep = pltpu.make_async_copy(big_total.at[p, k], big_out.at[k, p], cl.at[p])
        keep.start()
        keep.wait()
    finish_return(blks, b, k, c, nat_ref, pack_ref, even_ref, odd_ref, ssem, rsem)
    for d in range(1, blks):
        slab(d).wait()
    for d in range(1, seqs):
        group(d).wait_send()
    for p in range(pieces):
        for d in range(1, chips):
            big_slab(p, d).wait()
        for d in range(1, seqs):
            big_group(p, d).wait_send()


def leave(nat, pack, grads, big):
    blks = nat.shape[0]
    seqs = grads.shape[0]
    chips, pieces = big.shape[1:3]
    dma = pltpu.SemaphoreType.DMA
    return pl.pallas_call(
        functools.partial(exit_kernel, seqs, blks),
        name="leave",
        out_shape=(
            jax.ShapeDtypeStruct((blks // 2,) + nat.shape[1:], LOW),
            jax.ShapeDtypeStruct((blks // 2,) + pack.shape[1:], LOW),
            jax.ShapeDtypeStruct(grads.shape[1:], LOW),
            jax.ShapeDtypeStruct(big.shape[1:], LOW),
        ),
        in_specs=[spec(ANY), spec(ANY), spec(pltpu.VMEM), spec(ANY)],
        out_specs=(spec(ANY),) * 4,
        scratch_shapes=[
            pltpu.VMEM(nat.shape[1:], LOW),
            pltpu.VMEM(grads.shape, LOW),
            pltpu.VMEM(grads.shape[1:], LOW),
            pltpu.VMEM((pieces, seqs, chips) + big.shape[3:], LOW),
            pltpu.VMEM((pieces, chips) + big.shape[3:], LOW),
            dma, dma((blks,)), dma((blks,)), dma((seqs,)), dma((seqs,)),
            dma, dma((blks,)), dma((blks,)),
            dma((pieces,)), dma((pieces, seqs)), dma((pieces, seqs)),
            dma((pieces,)), dma((pieces, chips)), dma((pieces, chips)),
        ],
        compiler_params=pltpu.CompilerParams(
            collective_id=3, has_side_effects=True, vmem_limit_bytes=BIG
        ),
        cost_estimate=pl.CostEstimate(flops=0, transcendentals=0, bytes_accessed=200 * 10**6),
    )(nat, pack, grads, big)


def owner_facts(hd, chips):
    b = lax.axis_index("blk")
    k = b // 2
    odd = lax.rem(b, 2)
    first = jnp.where(odd == 0, 2 * hd * k, (2 * chips + k) * hd)
    return 2 - odd, first, (2 - odd) * hd


def lane_of(rows):
    return lax.broadcasted_iota(jnp.int32, (rows, 128), 1)


def low_lanes(value, slot, hd):
    lane = lane_of(value.shape[0])
    keep = jnp.logical_and(lane >= slot * hd, lane < (slot + 1) * hd)
    return jnp.where(keep, value, 0.0).astype(LOW)


def part_of(u, t):
    return pl.ds(u * 512 + t, 128, stride=4)


def row_part(ref, u, t):
    return ref[part_of(u, t), :]


def column_softmax(scores):
    weights = jnp.exp(scores - jnp.max(scores, axis=0, keepdims=True))
    return weights * (1.0 / jnp.sum(weights, axis=0, keepdims=True))


def attend_kernel(
    hd, scale, order, hid_hbm, gathered, proj_hbm, nat, pack, vecs, bias_inner,
    rows4, take, take_b, mix, mix_b, back, wide_weight, weight, hid, proj, in_sems, out_sem,
):
    length, width = hid.shape
    blks, step, _ = nat.shape
    devices = gathered.shape[0]
    own_rows = width // devices
    per = bias_inner.shape[1] // devices
    heads_here, first, _ = owner_facts(hd, blks // 2)

    def fetch(i):
        part = pl.ds(pl.multiple_of(i * step, step), step)
        return pltpu.make_async_copy(hid_hbm.at[part], hid.at[part], in_sems.at[i])

    for i in range(length // step):
        fetch(i).start()
    for i in range(devices):
        slab = gathered[i].astype(F32)
        wide_weight[i * own_rows : (i + 1) * own_rows, :] = slab[:own_rows, :]
        vecs[:, i * own_rows : (i + 1) * own_rows] = slab[own_rows:, :own_rows]
        bias_inner[0:1, i * per : (i + 1) * per] = slab[own_rows : own_rows + 1, 128 : 128 + per]
    weight[...] = wide_weight[...].astype(LOW)
    tile = vecs[:, pl.ds(pl.multiple_of(first // 128 * 128, 128), 128)]
    tile = jnp.where(lax.rem(first, 128) == 0, tile, pltpu.roll(tile, 64, 1))
    bias = jnp.concatenate([tile[0:1], jnp.zeros((1, 128), F32), tile[1:2]], axis=1)

    @pl.loop(0, length // step)
    def _(i):
        at = pl.multiple_of(i * step, step)
        fetch(i).wait()
        low = (nn_dot(hid[pl.ds(at, step), :], weight[...]) + bias).astype(LOW)
        proj[pl.ds(at, step), :] = low
        wide = low.astype(F32)
        for t in range(3):
            rows4[pl.ds(4 * at + t, step, stride=4), :] = wide[:, t * 128 : (t + 1) * 128]

    store = pltpu.make_async_copy(proj, proj_hbm, out_sem)
    store.start()
    span = GROUP * 128

    def gather(buf, base):
        for j in range(span):
            buf[4 * j : 4 * j + 4, :] = rows4[pl.ds(pl.multiple_of(4 * order[base + j], 4), 4), :]

    def attend_group(slot, buf, out):
        for u in range(GROUP):
            own = pl.ds(u * 128, 128)
            query = low_lanes(row_part(buf, u, 0) * scale, slot, hd)
            probs = column_softmax(nt_dot(row_part(buf, u, 1).astype(LOW), query))
            out[own, :] = tn_dot(probs.astype(LOW), row_part(buf, u, 2).astype(LOW))

    def scatter(slot, out, base):
        for j in range(span):
            back[pl.ds(slot * length + order[base + j], 1), :] = out[pl.ds(j, 1), :]

    @pl.loop(0, heads_here)
    def _(slot):
        begin = slot * length
        gather(take, begin)

        @pl.loop(0, length // (2 * span))
        def _(i):
            base = begin + 2 * i * span
            gather(take_b, base + span)
            attend_group(slot, take, mix)
            scatter(slot, mix, base)
            gather(take, jnp.minimum(base + 2 * span, begin + length - span))
            attend_group(slot, take_b, mix_b)
            scatter(slot, mix_b, base + span)

    lane = lane_of(step)

    @pl.when(heads_here == 2)
    def _():
        @pl.loop(0, length // step)
        def _(i):
            at = pl.multiple_of(i * step, step)
            nat[i] = jnp.where(
                lane < hd, back[pl.ds(at, step), :], back[pl.ds(length + at, step), :]
            ).astype(LOW)

    half = step // 2

    @pl.when(heads_here == 1)
    def _():
        @pl.loop(0, length // step)
        def _(i):
            at = pl.multiple_of(i * step, step)
            upper = pltpu.roll(back[pl.ds(at + half, half), :], hd, 1)
            pack[i] = jnp.where(lane[:half] < hd, back[pl.ds(at, half), :], upper).astype(LOW)

    store.wait()


def attend(order, hid, gathered, blks, ff, hd, scale):
    length, width = hid.shape
    step = length // blks
    return pl.pallas_call(
        functools.partial(attend_kernel, hd, scale),
        name="attend",
        out_shape=(
            jax.ShapeDtypeStruct((length, 384), LOW),
            jax.ShapeDtypeStruct((blks, step, 128), LOW),
            jax.ShapeDtypeStruct((blks, step // 2, 128), LOW),
            jax.ShapeDtypeStruct((8, width), F32),
            jax.ShapeDtypeStruct((8, ff), F32),
        ),
        in_specs=[spec(pltpu.SMEM), spec(ANY), spec(pltpu.VMEM)],
        out_specs=(spec(ANY),) + (spec(pltpu.VMEM),) * 4,
        scratch_shapes=[
            pltpu.VMEM((4 * length, 128), F32),
            pltpu.VMEM((GROUP * 512, 128), F32),
            pltpu.VMEM((GROUP * 512, 128), F32),
            pltpu.VMEM((GROUP * 128, 128), F32),
            pltpu.VMEM((GROUP * 128, 128), F32),
            pltpu.VMEM((2 * length, 128), F32),
            pltpu.VMEM((width, 384), F32),
            pltpu.VMEM((width, 384), LOW),
            pltpu.VMEM((length, width), LOW),
            pltpu.VMEM((length, 384), LOW),
            pltpu.SemaphoreType.DMA((blks,)),
            pltpu.SemaphoreType.DMA,
        ],
        compiler_params=pltpu.CompilerParams(vmem_limit_bytes=BIG),
        cost_estimate=pl.CostEstimate(
            flops=5 * 10**9, transcendentals=0, bytes_accessed=100 * 10**6
        ),
    )(order, hid, gathered)


def attend_back_kernel(
    hd, scale, order, hidden_hbm, proj, gnat, gpack, extra, znat_hbm, zpack_hbm, slabs,
    rows4, take, take_b, out4, out4_b, back4, hid, wide_grad,
    znat, zpack, sem, nat_sems, pack_sems,
):
    length = proj.shape[0]
    step = gnat.shape[1]
    half = step // 2
    heads_here, first_col, limit = owner_facts(hd, gnat.shape[0] // 2)
    fetch = pltpu.make_async_copy(hidden_hbm, hid, sem)
    fetch.start()

    @pl.loop(0, length // step)
    def _(i):
        at = pl.multiple_of(i * step, step)
        wide = proj[pl.ds(at, step), :].astype(F32)
        for t in range(3):
            rows4[pl.ds(4 * at + t, step, stride=4), :] = wide[:, t * 128 : (t + 1) * 128]

        @pl.when(heads_here == 2)
        def _():
            rows4[pl.ds(4 * at + 3, step, stride=4), :] = gnat[i].astype(F32)

        @pl.when(heads_here == 1)
        def _():
            pair = gpack[i].astype(F32)
            rows4[pl.ds(4 * at + 3, half, stride=4), :] = pair
            rows4[pl.ds(4 * (at + half) + 3, half, stride=4), :] = pltpu.roll(pair, hd, 1)

    span = GROUP * 128

    def gather(buf, base):
        for j in range(span):
            buf[4 * j : 4 * j + 4, :] = rows4[pl.ds(pl.multiple_of(order[base + j], 4), 4), :]

    def attend_group(slot, buf, out):
        for u in range(GROUP):
            own = pl.ds(u * 128, 128)
            query = low_lanes(row_part(buf, u, 0) * scale, slot, hd)
            grad = low_lanes(row_part(buf, u, 3), slot, hd)
            keys = row_part(buf, u, 1).astype(LOW)
            probs = column_softmax(nt_dot(keys, query))
            prob_grad = nt_dot(row_part(buf, u, 2).astype(LOW), grad)
            shift = jnp.sum(probs * prob_grad, axis=0, keepdims=True)
            score_low = (probs * (prob_grad - shift)).astype(LOW)
            out[part_of(u, 0), :] = tn_dot(score_low, keys) * scale
            out[part_of(u, 1), :] = nn_dot(score_low, query)
            out[part_of(u, 2), :] = nn_dot(probs.astype(LOW), grad)

    def scatter(slot, out, base):
        back_slot = back4.at[pl.ds(pl.multiple_of(4 * slot * length, 4 * length), 4 * length), :]
        for j in range(span):
            at = pl.multiple_of(order[base + j], 4)
            back_slot[pl.ds(at, 4), :] = out[4 * j : 4 * j + 4, :]

    @pl.loop(0, heads_here)
    def _(slot):
        begin = slot * length
        gather(take, begin)

        @pl.loop(0, length // (2 * span))
        def _(i):
            base = begin + 2 * i * span
            gather(take_b, base + span)
            attend_group(slot, take, out4)
            scatter(slot, out4, base)
            gather(take, jnp.minimum(base + 2 * span, begin + length - span))
            attend_group(slot, take_b, out4_b)
            scatter(slot, out4_b, base + span)

    lane = lane_of(step)
    fetch.wait()
    wide_grad[...] = jnp.zeros_like(wide_grad)
    zero = jnp.zeros((1, 384), F32)

    def put_nat(i):
        return pltpu.make_async_copy(znat.at[i], znat_hbm.at[i], nat_sems.at[i])

    def put_pack(i):
        return pltpu.make_async_copy(zpack.at[i], zpack_hbm.at[i], pack_sems.at[i])

    def settle(i, sums):
        at = pl.multiple_of(i * step, step)
        parts = []
        for t in range(3):
            cols = pl.ds(t * 128, 128)
            first = back4[pl.ds(4 * at + t, step, stride=4), :]
            second = back4[pl.ds(4 * (length + at) + t, step, stride=4), :]
            second = jnp.where(heads_here == 2, second, jnp.zeros_like(second))
            low = jnp.where(lane < hd, first, second).astype(LOW)
            znat[i, :, cols] = low
            wide = low.astype(F32)
            parts.append(jnp.sum(wide, axis=0, keepdims=True))
            zpack[i, :, cols] = (wide[:half] + pltpu.roll(wide[half:], hd, 1)).astype(LOW)
        put_nat(i).start()
        put_pack(i).start()
        wide_grad[...] += tn_dot(hid[pl.ds(at, step), :], znat[i])
        return sums + jnp.concatenate(parts, axis=1)

    sums = lax.fori_loop(0, length // step, settle, zero)
    devices = slabs.shape[0]
    own = hid.shape[1] // devices
    lane8 = lane_of(8)
    row8 = lax.broadcasted_iota(jnp.int32, (8, 128), 0)
    q_row = jnp.broadcast_to(sums[:, :128], (8, 128))
    v_row = jnp.broadcast_to(sums[:, 256:], (8, 128))
    for i in range(devices):
        begin = i * own - first_col
        q_lane = lane8 + begin
        v_lane = q_lane - 64
        q_part = pltpu.roll(q_row, lax.rem(4096 - begin, 128), 1)
        v_part = pltpu.roll(v_row, lax.rem(4096 - begin + 64, 128), 1)
        q_ok = (lane8 < own) & (q_lane >= 0) & (q_lane < limit)
        v_ok = (lane8 >= 64) & (lane8 < 64 + own) & (v_lane >= 0) & (v_lane < limit)
        line = jnp.where(q_ok, q_part, jnp.where(v_ok, v_part, 0.0))
        tile = jnp.where(row8 == 0, line, extra[i])
        tail = jnp.concatenate([tile, jnp.zeros((8, 256), F32)], axis=1)
        at = i * own
        slabs[i, : own - 8, :] = wide_grad[at : at + own - 8, :].astype(LOW)
        slabs[i, own - 8 :, :] = jnp.concatenate(
            [wide_grad[at + own - 8 : at + own, :], tail], axis=0
        ).astype(LOW)
    for i in range(length // step):
        put_nat(i).wait()
        put_pack(i).wait()


def attend_back(order, hidden_all, proj, gnat, gpack, extra, hd, scale):
    order = 4 * order
    length = proj.shape[0]
    blks, step, _ = gnat.shape
    devices = extra.shape[0]
    width = hidden_all.shape[1]
    return pl.pallas_call(
        functools.partial(attend_back_kernel, hd, scale),
        name="attend_back",
        out_shape=(
            jax.ShapeDtypeStruct((blks, step, 384), LOW),
            jax.ShapeDtypeStruct((blks, step // 2, 384), LOW),
            jax.ShapeDtypeStruct((devices, width // devices + 8, 384), LOW),
        ),
        in_specs=[spec(pltpu.SMEM), spec(ANY)] + [spec(pltpu.VMEM)] * 4,
        out_specs=(spec(ANY), spec(ANY), spec(pltpu.VMEM)),
        scratch_shapes=[
            pltpu.VMEM((4 * length, 128), F32),
            pltpu.VMEM((GROUP * 512, 128), F32),
            pltpu.VMEM((GROUP * 512, 128), F32),
            pltpu.VMEM((GROUP * 512, 128), F32),
            pltpu.VMEM((GROUP * 512, 128), F32),
            pltpu.VMEM((8 * length, 128), F32),
            pltpu.VMEM(hidden_all.shape, LOW),
            pltpu.VMEM((width, 384), F32),
            pltpu.VMEM((blks, step, 384), LOW),
            pltpu.VMEM((blks, step // 2, 384), LOW),
            pltpu.SemaphoreType.DMA,
            pltpu.SemaphoreType.DMA((blks,)),
            pltpu.SemaphoreType.DMA((blks,)),
        ],
        compiler_params=pltpu.CompilerParams(vmem_limit_bytes=BIG),
        cost_estimate=pl.CostEstimate(
            flops=8 * 10**9, transcendentals=0, bytes_accessed=120 * 10**6
        ),
    )(order, hidden_all, proj, gnat, gpack, extra)


def middle_kernel(
    hd, ceven, codd, hidden, first_hbm, outer_hbm, vecs, bias_inner, cot, mask,
    hout, resid, geven, godd, merged_hbm, extra,
    wa, wb, ctx, act, slope, ilow, first, flow, olow, unit, acc, hid_low, sums, inner_sums, merged, sems,
):
    rows, width = hidden.shape
    ff = outer_hbm.shape[0]
    chips = ceven.shape[0]
    get_out = pltpu.make_async_copy(
        first_hbm.at[:, pl.ds(0, width)], wa.at[:, pl.ds(0, width)], sems.at[0]
    )
    get_in = pltpu.make_async_copy(
        first_hbm.at[:, pl.ds(width, ff)], wa.at[:, pl.ds(width, ff)], sems.at[1]
    )
    get_outer = pltpu.make_async_copy(outer_hbm, wb, sems.at[2])
    get_out.start()
    get_in.start()
    get_outer.start()
    half = rows // 2
    lane = lane_of(half)
    low_half = lane < hd
    for z in range(chips):
        ctx[:, z * 128 : (z + 1) * 128] = ceven[z]
    for z in range(0, chips, 2):
        here = codd[z].astype(F32)
        there = codd[z + 1].astype(F32)
        at = chips * 128 + z * 64
        ctx[:half, at : at + 128] = jnp.where(low_half, here, pltpu.roll(there, hd, 1)).astype(LOW)
        ctx[half:, at : at + 128] = jnp.where(low_half, pltpu.roll(here, hd, 1), there).astype(LOW)
    sums[...] = jnp.zeros_like(sums)
    wide = 256
    tile = 64

    def add_rows(row, value):
        sums[row : row + 1, :] += jnp.sum(value, axis=0, keepdims=True)

    get_out.wait()

    @pl.loop(0, width // wide)
    def _(n):
        at = pl.multiple_of(n * wide, wide)
        acc[:, pl.ds(at, wide)] = nn_dot(ctx[...], wa[:, pl.ds(at, wide)])

    @pl.loop(0, rows // tile)
    def _(i):
        own = pl.ds(pl.multiple_of(i * tile, tile), tile)
        value = hidden[own, :].astype(F32) + acc[own, :] + vecs[2:3, :]
        center = value - jnp.mean(value, axis=-1, keepdims=True)
        spread = jnp.mean(center * center, axis=-1, keepdims=True)
        inv = lax.rsqrt(spread + epsilon)
        norm = center * inv * vecs[3:4, :] + vecs[4:5, :]
        first[own, :] = norm
        flow[own, :] = norm.astype(LOW)
        unit[own, :] = center * inv
        resid[own, 0:128] = jnp.broadcast_to(inv, (tile, 128))

    get_in.wait()

    @pl.loop(0, ff // wide)
    def _(j):
        at = pl.multiple_of(j * wide, wide)
        cols = pl.ds(at, wide)
        pre = nn_dot(flow[...], wa[:, pl.ds(width + at, wide)]) + bias_inner[0:1, cols]
        gate = 0.5 + 0.5 * lax.erf(pre * (0.5**0.5))
        act[:, cols] = (pre * gate).astype(LOW)
        slope[:, cols] = gate + pre * jnp.exp(-0.5 * pre * pre) * (0.5 / math.pi) ** 0.5

    get_outer.wait()

    @pl.loop(0, width // wide)
    def _(n):
        at = pl.multiple_of(n * wide, wide)
        acc[:, pl.ds(at, wide)] = nn_dot(act[...], wb[:, pl.ds(at, wide)])

    @pl.loop(0, rows // tile)
    def _(i):
        own = pl.ds(pl.multiple_of(i * tile, tile), tile)
        value = first[own, :] + acc[own, :] + vecs[5:6, :]
        center = value - jnp.mean(value, axis=-1, keepdims=True)
        spread = jnp.mean(center * center, axis=-1, keepdims=True)
        inv = lax.rsqrt(spread + epsilon)
        norm = center * inv
        hout[own, :] = (norm * vecs[6:7, :] + vecs[7:8, :]).astype(LOW)
        out_grad = cot[own, :].astype(F32) * mask[own, :].astype(F32)
        pull = out_grad * vecs[6:7, :]
        pull = pull - jnp.mean(pull, axis=-1, keepdims=True) - norm * jnp.mean(
            pull * norm, axis=-1, keepdims=True
        )
        grad = pull * inv
        low = grad.astype(LOW)
        first[own, :] = grad
        olow[own, :] = low
        add_rows(4, low.astype(F32))
        add_rows(5, out_grad * norm)
        add_rows(6, out_grad)

    @pl.loop(0, ff // wide)
    def _(j):
        cols = pl.ds(pl.multiple_of(j * wide, wide), wide)
        low = (nt_dot(olow[...], wb[cols, :]) * slope[:, cols]).astype(LOW)
        ilow[:, cols] = low
        inner_sums[0:1, cols] = jnp.sum(low.astype(F32), axis=0, keepdims=True)

    @pl.loop(0, width // wide)
    def _(n):
        at = pl.multiple_of(n * wide, wide)
        acc[:, pl.ds(at, wide)] = nt_dot(ilow[...], wa[pl.ds(at, wide), width:])

    @pl.loop(0, rows // tile)
    def _(i):
        own = pl.ds(pl.multiple_of(i * tile, tile), tile)
        grad = acc[own, :] + first[own, :]
        norm = unit[own, :]
        inv = resid[own, 0:1]
        pull = grad * vecs[3:4, :]
        pull = pull - jnp.mean(pull, axis=-1, keepdims=True) - norm * jnp.mean(
            pull * norm, axis=-1, keepdims=True
        )
        back = pull * inv
        low = back.astype(LOW)
        resid[own, :] = back
        hid_low[own, :] = low
        add_rows(1, low.astype(F32))
        add_rows(2, grad * norm)
        add_rows(3, grad)

    @pl.loop(0, width // wide)
    def _(n):
        at = pl.multiple_of(n * wide, wide)
        acc[:, pl.ds(at, wide)] = nt_dot(hid_low[...], wa[pl.ds(at, wide), :width])

    for z in range(chips):
        geven[z] = acc[:, z * 128 : (z + 1) * 128].astype(LOW)
    for z in range(0, chips, 2):
        at = chips * 128 + z * 64
        top = acc[:half, at : at + 128]
        bottom = acc[half:, at : at + 128]
        godd[z] = jnp.where(low_half, top, pltpu.roll(bottom, hd, 1)).astype(LOW)
        godd[z + 1] = jnp.where(low_half, pltpu.roll(top, hd, 1), bottom).astype(LOW)

    devices = merged.shape[0]
    own_rows = width // devices
    outer_rows = ff // devices
    block = 384
    per = block // outer_rows

    @pl.loop(0, ff // block)
    def _(j):
        part = tn_dot(act[:, pl.ds(pl.multiple_of(j * block, block), block)], olow[...])
        for i in range(per):
            merged[j * per + i, :outer_rows, :] = part[
                i * outer_rows : (i + 1) * outer_rows, :
            ].astype(LOW)

    folds = ff // width
    many = block // own_rows
    size = merged.shape[1]
    put_outer = pltpu.make_async_copy(
        merged.at[:, pl.ds(0, outer_rows)], merged_hbm.at[:, pl.ds(0, outer_rows)], sems.at[3]
    )
    put_outer.start()

    def put_rest(m):
        part = (pl.ds(m * many, many), pl.ds(outer_rows, size - outer_rows))
        return pltpu.make_async_copy(merged.at[part], merged_hbm.at[part], sems.at[4 + m])

    for m in range(width // block):
        cols = slice(m * block, (m + 1) * block)
        for h in range(0, folds, 2):
            left = tn_dot(flow[:, cols], ilow[:, h * width : (h + 1) * width])
            right = tn_dot(flow[:, cols], ilow[:, (h + 1) * width : (h + 2) * width])
            at = outer_rows + h * own_rows
            for i in range(many):
                for r in range(0, own_rows, 8):
                    base = i * own_rows + r
                    merged[m * many + i, at + 2 * r : at + 2 * r + 16, :] = jnp.concatenate(
                        [left[base : base + 8, :], right[base : base + 8, :]], axis=0
                    ).astype(LOW)
        part = tn_dot(ctx[:, cols], hid_low[...])
        at = outer_rows + folds * own_rows
        for i in range(many):
            base = i * own_rows
            merged[m * many + i, at : at + 16, :] = part[base : base + 16, :].astype(LOW)
            merged[m * many + i, at + 16 : at + 32, :] = jnp.concatenate(
                [part[base + 16 : base + 24, :], jnp.zeros((8, width), F32)], axis=0
            ).astype(LOW)
        put_rest(m).start()

    row8 = lax.broadcasted_iota(jnp.int32, (8, 128), 0)
    for i in range(devices):
        piece = sums[:, i * own_rows : (i + 1) * own_rows]
        piece = jnp.concatenate([piece, jnp.zeros((8, 128 - own_rows), F32)], axis=1)
        inner = inner_sums[0:1, i * outer_rows : (i + 1) * outer_rows]
        inner = jnp.concatenate([inner, jnp.zeros((1, 128 - outer_rows), F32)], axis=1)
        extra[i] = jnp.where(row8 == 7, jnp.broadcast_to(inner, (8, 128)), piece)
    put_outer.wait()
    for m in range(width // block):
        put_rest(m).wait()


def middle(ceven, codd, hidden, first_half, outer_full, vecs, bias_inner, cot, mask, devices, hd):
    rows, width = hidden.shape
    ff = outer_full.shape[0]
    slab = ff // devices + (ff // width + 1) * (width // devices) + 8
    wide_low = pltpu.VMEM((rows, width), LOW)
    wide_f32 = pltpu.VMEM((rows, width), F32)
    return pl.pallas_call(
        functools.partial(middle_kernel, hd),
        name="middle",
        out_shape=(
            jax.ShapeDtypeStruct((rows, width), LOW),
            jax.ShapeDtypeStruct((rows, width), F32),
            jax.ShapeDtypeStruct(ceven.shape, LOW),
            jax.ShapeDtypeStruct(codd.shape, LOW),
            jax.ShapeDtypeStruct((devices, slab, width), LOW),
            jax.ShapeDtypeStruct((devices, 8, 128), F32),
        ),
        in_specs=[spec(pltpu.VMEM)] * 3 + [spec(ANY)] * 2 + [spec(pltpu.VMEM)] * 4,
        out_specs=(spec(pltpu.VMEM),) * 4 + (spec(ANY), spec(pltpu.VMEM)),
        scratch_shapes=[
            pltpu.VMEM(first_half.shape, LOW),
            pltpu.VMEM(outer_full.shape, LOW),
            wide_low,
            pltpu.VMEM((rows, ff), LOW),
            pltpu.VMEM((rows, ff), F32),
            pltpu.VMEM((rows, ff), LOW),
            wide_f32, wide_low, wide_low, wide_f32, wide_f32, wide_low,
            pltpu.VMEM((8, width), F32),
            pltpu.VMEM((8, ff), F32),
            pltpu.VMEM((devices, slab, width), LOW),
            pltpu.SemaphoreType.DMA((4 + width // 384,)),
        ],
        compiler_params=pltpu.CompilerParams(vmem_limit_bytes=BIG),
        cost_estimate=pl.CostEstimate(
            flops=17 * 10**9, transcendentals=0, bytes_accessed=40 * 10**6
        ),
    )(ceven, codd, hidden, first_half, outer_full, vecs, bias_inner, cot, mask)


def final_kernel(
    hd, zeven, zodd, proj_hbm, resid, proj_grads, shares,
    out, gq, gk, gv, go, gi, gu, g0, g1, g2, g3, g4, g5, g6, g7, g8, wp, triple, sem,
):
    rows, width = resid.shape
    chips = zeven.shape[0]
    fetch = pltpu.make_async_copy(proj_hbm, wp, sem)
    fetch.start()
    half = rows // 2
    low_half = lane_of(half) < hd
    for t in range(3):
        cols = slice(t * 128, (t + 1) * 128)
        for z in range(chips):
            at = t * width + z * 128
            triple[:, at : at + 128] = zeven[z, :, cols]
        for z in range(0, chips, 2):
            at = t * width + chips * 128 + z * 64
            here = zodd[z, :, cols].astype(F32)
            there = zodd[z + 1, :, cols].astype(F32)
            triple[:half, at : at + 128] = jnp.where(
                low_half, here, pltpu.roll(there, hd, 1)
            ).astype(LOW)
            triple[half:, at : at + 128] = jnp.where(
                low_half, pltpu.roll(here, hd, 1), there
            ).astype(LOW)
    own = gq.shape[0]
    keep = lane_of(own) < hd
    for t, ref in enumerate((gq, gk, gv)):
        cols = slice(t * 128, (t + 1) * 128)
        for z in range(chips):
            ref[:, z * 128 : (z + 1) * 128] = proj_grads[2 * z, :, cols].astype(F32)[:own]
        for z in range(0, chips, 2):
            here = proj_grads[2 * z + 1, :, cols].astype(F32)[:own]
            there = proj_grads[2 * z + 3, :, cols].astype(F32)[:own]
            at = chips * 128 + z * 64
            ref[:, at : at + 128] = jnp.where(keep, here, pltpu.roll(there, hd, 1))
    ff = gi.shape[1]
    outer_rows = gu.shape[0]
    folds = ff // width

    def share(at, size):
        total = shares[0, at : at + size, :].astype(F32)
        for z in range(1, chips):
            total = total + shares[z, at : at + size, :].astype(F32)
        return total

    for r in range(0, outer_rows, 16):
        gu[r : r + 16, :] = share(r, 16)
    for h in range(0, folds, 2):
        at = outer_rows + h * own
        for r in range(0, own, 8):
            pair = share(at + 2 * r, 16)
            gi[r : r + 8, h * width : (h + 1) * width] = pair[:8]
            gi[r : r + 8, (h + 1) * width : (h + 2) * width] = pair[8:]
    at = outer_rows + folds * own
    go[...] = share(at, own + 8)[:own]
    total = proj_grads[0, :, :128].astype(F32)[own:]
    for d in range(1, 2 * chips):
        total = total + proj_grads[d, :, :128].astype(F32)[own:]
    g0[...] = total[0, :own]
    g1[...] = total[0, 64 : 64 + own]
    for v, ref in enumerate((g2, g3, g4)):
        ref[...] = total[1 + v, :own]
    g5[...] = total[7, : g5.shape[0]]
    for v, ref in enumerate((g6, g7, g8)):
        ref[...] = total[4 + v, :own]
    fetch.wait()
    wide = 256

    @pl.loop(0, width // wide)
    def _(n):
        at = pl.multiple_of(n * wide, wide)
        cols = pl.ds(at, wide)
        out[:, cols] = nt_dot(triple[...], wp[pl.ds(at, wide), :]) + resid[:, cols]


def final(zeven, zodd, projections, resid, proj_grads, shares, own, ff, hd):
    rows, width = resid.shape
    mats = [(rows, width)] + [(own, width)] * 4 + [(own, ff), (ff * own // width, width)]
    vectors = [(own,)] * 5 + [(ff * own // width,)] + [(own,)] * 3
    return pl.pallas_call(
        functools.partial(final_kernel, hd),
        name="final",
        out_shape=tuple(jax.ShapeDtypeStruct(shape, F32) for shape in mats + vectors),
        in_specs=[spec(pltpu.VMEM)] * 2 + [spec(ANY)] + [spec(pltpu.VMEM)] * 3,
        out_specs=(spec(pltpu.VMEM),) * 16,
        scratch_shapes=[
            pltpu.VMEM(projections.shape, LOW),
            pltpu.VMEM((rows, 3 * width), LOW),
            pltpu.SemaphoreType.DMA,
        ],
        compiler_params=pltpu.CompilerParams(vmem_limit_bytes=BIG),
        cost_estimate=pl.CostEstimate(
            flops=2 * 10**9, transcendentals=0, bytes_accessed=12 * 10**6
        ),
    )(zeven, zodd, projections, resid, proj_grads, shares)


def prelude_kernel(
    hd, q, k, v, o, inner, outer, b0, b1, b2, b3, b4, b5, b6, b7, b8,
    slabs, first_half, outer_low, projections, tile,
):
    own, width = q.shape
    chips = slabs.shape[0] // 2
    first_half[:, :width] = o[...].astype(LOW)
    first_half[:, width:] = inner[...].astype(LOW)
    outer_low[...] = outer[...].astype(LOW)
    for t, ref in enumerate((q, k, v)):
        projections[:, t * width : (t + 1) * width] = ref[...].astype(LOW)
    tile[...] = jnp.zeros_like(tile)
    for i, ref in enumerate((b0, b1, b2, b3, b4, b5, b6, b7)):
        tile[i : i + 1, :own] = ref[...].reshape(1, own)
    tile[0:1, 128 : 128 + b8.shape[0]] = b8[...].reshape(1, b8.shape[0])
    keep = lane_of(own) < hd
    for t, ref in enumerate((q, k, v)):
        cols = slice(t * 128, (t + 1) * 128)
        below = tile[:, cols]
        for d in range(2 * chips):
            z = d // 2
            if d % 2 == 0:
                part = ref[:, z * 128 : (z + 1) * 128]
            else:
                at = chips * 128 + z // 2 * 128
                part = ref[:, at : at + 128]
                if z % 2:
                    part = pltpu.roll(part, hd, 1)
                part = jnp.where(keep, part, 0.0)
            slabs[d, :16, cols] = part[:16].astype(LOW)
            slabs[d, 16:, cols] = jnp.concatenate([part[16:], below], axis=0).astype(LOW)


def prelude(weights, vectors, blks, hd):
    own, width = weights[0].shape
    ff = weights[4].shape[1]
    return pl.pallas_call(
        functools.partial(prelude_kernel, hd),
        name="prelude",
        out_shape=(
            jax.ShapeDtypeStruct((blks, own + 8, 384), LOW),
            jax.ShapeDtypeStruct((own, width + ff), LOW),
            jax.ShapeDtypeStruct(weights[5].shape, LOW),
            jax.ShapeDtypeStruct((own, 3 * width), LOW),
        ),
        in_specs=[spec(pltpu.VMEM)] * 15,
        out_specs=(spec(pltpu.VMEM),) * 4,
        scratch_shapes=[pltpu.VMEM((8, 384), F32)],
        cost_estimate=pl.CostEstimate(flops=10**6, transcendentals=0, bytes_accessed=3 * 10**6),
    )(*weights, *vectors)


def fast_body(seqs, blks, heads):
    def run(
        hidden_in, query_weight, key_weight, value_weight, output_weight, inner_weight,
        outer_weight, query_bias, value_bias, output_bias, attention_gain, attention_shift,
        inner_bias, outer_bias, final_gain, final_shift, cotangent, grad_mask, cluster_order,
    ):
        rows, width = hidden_in.shape
        own = query_weight.shape[0]
        hidden_units = inner_weight.shape[1]
        length = cluster_order.shape[2]
        hd = width // heads
        chips = blks // 2
        scale = 1.0 / math.sqrt(hd)
        devices = seqs * blks
        b = lax.axis_index("blk")
        k = b // 2
        even_core = lax.rem(b, 2) == 0
        slabs, half_own, outer_own, proj_own = prelude(
            (query_weight, key_weight, value_weight, output_weight, inner_weight, outer_weight),
            (
                query_bias, value_bias, output_bias, attention_gain, attention_shift,
                outer_bias, final_gain, final_shift, inner_bias,
            ),
            blks,
            hd,
        )
        hidden_all, gathered, first_half, outer_full, projections = entry(
            hidden_in, slabs, (half_own, outer_own, proj_own), seqs, blks, 2
        )
        first_half = first_half.reshape(width, width + hidden_units)
        outer_full = outer_full.reshape(hidden_units, width)
        projections = projections.reshape(width, 3 * width)
        hidden_all = hidden_all.reshape(length, width)
        gathered = gathered.reshape((devices,) + slabs.shape[1:])
        order = cluster_order[0]
        head_first = jnp.where(even_core, 2 * k, 2 * chips + k)
        order_own = jnp.concatenate(
            [
                lax.dynamic_index_in_dim(order, head_first, 0, keepdims=False),
                lax.dynamic_index_in_dim(order, 2 * k + 1, 0, keepdims=False),
            ]
        )
        proj, cnat, cpack, vecs, bias_inner = attend(
            order_own, hidden_all, gathered, blks, hidden_units, hd, scale
        )
        ceven, codd = return_rows(cnat, cpack, 1)
        hidden_out, residual_grad, geven, godd, merged, extra = middle(
            ceven, codd, hidden_in, first_half, outer_full, vecs, bias_inner, cotangent,
            grad_mask, devices, hd,
        )
        slab = merged.shape[1:]
        gnat, gpack, summed = spread_rows(
            geven, godd, merged.reshape((seqs * chips, 2) + slab), 2
        )
        znat, zpack, grads = attend_back(
            order_own, hidden_all, proj, gnat, gpack, extra, hd, scale
        )
        pieces = 2
        zeven, zodd, proj_grads, big_grads = leave(
            znat, zpack, grads.reshape((seqs, blks) + grads.shape[1:]),
            summed.reshape(seqs, chips, pieces, slab[0] // pieces, width),
        )
        return (hidden_out,) + tuple(
            final(
                zeven, zodd, projections, residual_grad, proj_grads,
                big_grads.reshape((chips,) + slab), own, hidden_units, hd,
            )
        )

    return run


def masked_scores(left, right, left_ids, right_ids, scale):
    scores = back_product(left, right) * scale
    return jnp.where(left_ids[:, None] == right_ids[None, :], scores, -jnp.inf)


def body(
    hidden_in,
    query_weight,
    key_weight,
    value_weight,
    output_weight,
    inner_weight,
    outer_weight,
    query_bias,
    value_bias,
    output_bias,
    attention_gain,
    attention_shift,
    inner_bias,
    outer_bias,
    final_gain,
    final_shift,
    cotangent,
    grad_mask,
    cluster_order,
):
    rows = hidden_in.shape[0]
    width = hidden_in.shape[1]
    heads = cluster_order.shape[1]
    length = cluster_order.shape[2]
    scale = 1.0 / math.sqrt(width // heads)
    masters = (
        query_weight,
        key_weight,
        value_weight,
        output_weight,
        inner_weight,
        outer_weight,
        query_bias,
        value_bias,
        output_bias,
        attention_gain,
        attention_shift,
        inner_bias,
        outer_bias,
        final_gain,
        final_shift,
    )
    lowered = [master.astype(jnp.bfloat16) for master in masters]
    fetched = (
        lax.all_gather(lowered[0], ("seq", "blk"), axis=0, tiled=True),
        lax.all_gather(lowered[1], ("seq", "blk"), axis=0, tiled=True),
        lax.all_gather(lowered[2], ("seq", "blk"), axis=0, tiled=True),
        lax.all_gather(lowered[3], ("seq", "blk"), axis=0, tiled=True),
        lax.all_gather(lowered[4], ("seq", "blk"), axis=0, tiled=True),
        lax.all_gather(lowered[5], ("seq", "blk"), axis=0, tiled=True),
        lax.all_gather(lowered[6], ("seq", "blk"), axis=0, tiled=True),
        lax.all_gather(lowered[7], ("seq", "blk"), axis=0, tiled=True),
        lax.all_gather(lowered[8], ("seq", "blk"), axis=0, tiled=True),
        lax.all_gather(lowered[9], ("seq", "blk"), axis=0, tiled=True),
        lax.all_gather(lowered[10], ("seq", "blk"), axis=0, tiled=True),
        lax.all_gather(lowered[11], ("seq", "blk"), axis=0, tiled=True),
        lax.all_gather(lowered[12], ("seq", "blk"), axis=0, tiled=True),
        lax.all_gather(lowered[13], ("seq", "blk"), axis=0, tiled=True),
        lax.all_gather(lowered[14], ("seq", "blk"), axis=0, tiled=True),
    )
    query_full, key_full, value_full, output_full, inner_full, outer_full = fetched[0:6]
    vectors = [vector.astype(jnp.float32) for vector in fetched[6:15]]
    (
        bias_query,
        bias_value,
        bias_output,
        gain_first,
        shift_first,
        bias_inner,
        bias_outer,
        gain_final,
        shift_final,
    ) = vectors
    hidden = hidden_in.astype(jnp.float32)
    query_low = (
        jnp.dot(hidden_in, query_full, preferred_element_type=jnp.float32) + bias_query
    ).astype(jnp.bfloat16)
    keys_low = jnp.dot(hidden_in, key_full, preferred_element_type=jnp.float32).astype(jnp.bfloat16)
    values_low = (
        jnp.dot(hidden_in, value_full, preferred_element_type=jnp.float32) + bias_value
    ).astype(jnp.bfloat16)
    all_keys, all_values = (
        lax.all_gather(keys_low, "blk", axis=0, tiled=True),
        lax.all_gather(values_low, "blk", axis=0, tiled=True),
    )
    order = cluster_order[0]
    head_rows = jnp.broadcast_to(jnp.arange(heads, dtype=jnp.int32)[:, None], (heads, length))
    positions = jnp.broadcast_to(jnp.arange(length, dtype=jnp.int32)[None, :], (heads, length))
    inverse = jnp.zeros((heads, length), jnp.int32).at[head_rows, order].set(positions)
    key_cluster = inverse // CLUSTER
    member = lax.dynamic_slice_in_dim(key_cluster, lax.axis_index("blk") * rows, rows, 1)
    query_heads = head_major(query_low, heads)
    key_heads = head_major(all_keys, heads)
    value_heads = head_major(all_values, heads)
    head_ids = jnp.arange(heads, dtype=jnp.int32)

    def attend(index):
        scores = masked_scores(
            query_heads[index], key_heads[index], member[index], key_cluster[index], scale
        )
        peak = jnp.max(scores, axis=-1, keepdims=True)
        weights = jnp.exp(scores - peak)
        total = jnp.sum(weights, axis=-1, keepdims=True)
        probs_low = (weights / total).astype(jnp.bfloat16)
        mixed = jnp.dot(probs_low, value_heads[index], preferred_element_type=jnp.float32)
        return (mixed, (peak + jnp.log(total))[:, 0])

    mixed, logsum = lax.map(attend, head_ids)
    context_low = token_major(mixed).astype(jnp.bfloat16)
    attention_out = (
        jnp.dot(context_low, output_full, preferred_element_type=jnp.float32) + bias_output
    )
    first_norm, first_pull = jax.vjp(layer_norm, hidden + attention_out, gain_first, shift_first)
    first_low = first_norm.astype(jnp.bfloat16)
    inner_pre = jnp.dot(first_low, inner_full, preferred_element_type=jnp.float32) + bias_inner
    activated, gelu_pull = jax.vjp(exact_gelu, inner_pre)
    activated_low = activated.astype(jnp.bfloat16)
    outer_out = jnp.dot(activated_low, outer_full, preferred_element_type=jnp.float32) + bias_outer
    final_norm, final_pull = jax.vjp(layer_norm, first_norm + outer_out, gain_final, shift_final)
    hidden_out = final_norm.astype(jnp.bfloat16)
    out_grad = cotangent.astype(jnp.float32) * grad_mask.astype(jnp.float32)
    second_grad, grad_final_gain, grad_final_shift = final_pull(out_grad)
    outer_low = second_grad.astype(jnp.bfloat16)
    back_weights = (
        lax.all_gather(lowered[0], ("seq", "blk"), axis=0, tiled=True),
        lax.all_gather(lowered[1], ("seq", "blk"), axis=0, tiled=True),
        lax.all_gather(lowered[2], ("seq", "blk"), axis=0, tiled=True),
        lax.all_gather(lowered[3], ("seq", "blk"), axis=0, tiled=True),
        lax.all_gather(lowered[4], ("seq", "blk"), axis=0, tiled=True),
        lax.all_gather(lowered[5], ("seq", "blk"), axis=0, tiled=True),
    )
    grad_outer_weight = row_contract(activated_low, outer_low)
    grad_outer_bias = column_sum(outer_low)
    inner_low = gelu_pull(back_product(outer_low, back_weights[5]))[0].astype(jnp.bfloat16)
    grad_inner_weight = row_contract(first_low, inner_low)
    grad_inner_bias = column_sum(inner_low)
    first_grad = back_product(inner_low, back_weights[4]) + second_grad
    residual_grad, grad_attention_gain, grad_attention_shift = first_pull(first_grad)
    attn_low = residual_grad.astype(jnp.bfloat16)
    grad_output_weight = row_contract(context_low, attn_low)
    grad_output_bias = column_sum(attn_low)
    context_grad = back_product(attn_low, back_weights[3]).astype(jnp.bfloat16)
    grad_heads = head_major(context_grad, heads)

    def own_rows_back(index):
        scores = masked_scores(
            query_heads[index], key_heads[index], member[index], key_cluster[index], scale
        )
        probs = jnp.exp(scores - logsum[index][:, None])
        probs_low = probs.astype(jnp.bfloat16)
        grad_part = grad_heads[index]
        prob_grad = back_product(grad_part, value_heads[index])
        weighted = jnp.sum(probs * prob_grad, axis=-1, keepdims=True)
        score_low = (probs * (prob_grad - weighted)).astype(jnp.bfloat16)
        query_grad = (
            jnp.dot(score_low, key_heads[index], preferred_element_type=jnp.float32) * scale
        )
        return (probs_low, score_low, query_grad, weighted[:, 0])

    def attend_back(index):
        probs_low, score_low, query_grad, weighted = own_rows_back(index)
        key_sum = row_contract(score_low, query_heads[index]) * scale
        value_sum = row_contract(probs_low, grad_heads[index])
        return (query_grad, key_sum, value_sum)

    query_grads, key_grads, value_grads = lax.map(attend_back, head_ids)
    key_own, value_own = (
        lax.psum_scatter(token_major(key_grads), "blk", scatter_dimension=0, tiled=True),
        lax.psum_scatter(token_major(value_grads), "blk", scatter_dimension=0, tiled=True),
    )
    query_grad_low = token_major(query_grads).astype(jnp.bfloat16)
    key_grad_low = key_own.astype(jnp.bfloat16)
    value_grad_low = value_own.astype(jnp.bfloat16)
    grad_query_weight = row_contract(hidden_in, query_grad_low)
    grad_key_weight = row_contract(hidden_in, key_grad_low)
    grad_value_weight = row_contract(hidden_in, value_grad_low)
    grad_query_bias = column_sum(query_grad_low)
    grad_value_bias = column_sum(value_grad_low)
    input_grad = (
        back_product(query_grad_low, back_weights[0])
        + back_product(key_grad_low, back_weights[1])
        + back_product(value_grad_low, back_weights[2])
        + residual_grad
    )
    shares = (
        lax.psum_scatter(grad_query_weight, ("seq", "blk"), scatter_dimension=0, tiled=True),
        lax.psum_scatter(grad_key_weight, ("seq", "blk"), scatter_dimension=0, tiled=True),
        lax.psum_scatter(grad_value_weight, ("seq", "blk"), scatter_dimension=0, tiled=True),
        lax.psum_scatter(grad_output_weight, ("seq", "blk"), scatter_dimension=0, tiled=True),
        lax.psum_scatter(grad_inner_weight, ("seq", "blk"), scatter_dimension=0, tiled=True),
        lax.psum_scatter(grad_outer_weight, ("seq", "blk"), scatter_dimension=0, tiled=True),
        lax.psum_scatter(grad_query_bias, ("seq", "blk"), scatter_dimension=0, tiled=True),
        lax.psum_scatter(grad_value_bias, ("seq", "blk"), scatter_dimension=0, tiled=True),
        lax.psum_scatter(grad_output_bias, ("seq", "blk"), scatter_dimension=0, tiled=True),
        lax.psum_scatter(grad_attention_gain, ("seq", "blk"), scatter_dimension=0, tiled=True),
        lax.psum_scatter(grad_attention_shift, ("seq", "blk"), scatter_dimension=0, tiled=True),
        lax.psum_scatter(grad_inner_bias, ("seq", "blk"), scatter_dimension=0, tiled=True),
        lax.psum_scatter(grad_outer_bias, ("seq", "blk"), scatter_dimension=0, tiled=True),
        lax.psum_scatter(grad_final_gain, ("seq", "blk"), scatter_dimension=0, tiled=True),
        lax.psum_scatter(grad_final_shift, ("seq", "blk"), scatter_dimension=0, tiled=True),
    )
    return (hidden_out, input_grad) + tuple(shares)


def solution(mesh):
    placed = (
        P(("seq", "blk"), None),
        P(("seq", "blk"), None),
        P(("seq", "blk"), None),
        P(("seq", "blk"), None),
        P(("seq", "blk"), None),
        P(("seq", "blk"), None),
        P(("seq", "blk"), None),
        P(("seq", "blk")),
        P(("seq", "blk")),
        P(("seq", "blk")),
        P(("seq", "blk")),
        P(("seq", "blk")),
        P(("seq", "blk")),
        P(("seq", "blk")),
        P(("seq", "blk")),
        P(("seq", "blk")),
        P(("seq", "blk"), None),
        P(("seq", "blk"), None),
        P("seq", None, None),
    )
    seqs, blks = mesh.shape["seq"], mesh.shape["blk"]
    heads = 12
    fast = seqs == 4 and blks == 8
    return jax.shard_map(
        fast_body(seqs, blks, heads) if fast else body,
        mesh=mesh,
        in_specs=placed,
        out_specs=(
            P(("seq", "blk"), None),
            P(("seq", "blk"), None),
            P(("seq", "blk"), None),
            P(("seq", "blk"), None),
            P(("seq", "blk"), None),
            P(("seq", "blk"), None),
            P(("seq", "blk"), None),
            P(("seq", "blk"), None),
            P(("seq", "blk")),
            P(("seq", "blk")),
            P(("seq", "blk")),
            P(("seq", "blk")),
            P(("seq", "blk")),
            P(("seq", "blk")),
            P(("seq", "blk")),
            P(("seq", "blk")),
            P(("seq", "blk")),
        ),
        check_vma=False,
    )
```

```python
import functools
import math

import jax
import jax.numpy as jnp
from jax import lax
from jax.experimental import pallas as pl
from jax.experimental.pallas import tpu as pltpu
from jax.sharding import PartitionSpec as P

MESH = pl.DeviceIdType.MESH
ANY = pl.ANY
LOW = jnp.bfloat16
F32 = jnp.float32
BIG = 60 * 2**20
GROUP = 4
CLUSTER = 128


def spec(space):
    return pl.BlockSpec(memory_space=space)


def nt_dot(left, right):
    return lax.dot_general(left, right, (((1,), (1,)), ((), ())), preferred_element_type=F32)


def tn_dot(left, right):
    return lax.dot_general(left, right, (((0,), (0,)), ((), ())), preferred_element_type=F32)


def nn_dot(left, right):
    return jnp.dot(left, right, preferred_element_type=F32)


def greet(targets):
    sem = pltpu.get_barrier_semaphore()
    for target in targets:
        pl.semaphore_signal(sem, inc=1, device_id=target, device_id_type=MESH)
    pl.semaphore_wait(sem, len(targets))


def send(src, dst, send_sem, recv_sem, target):
    return pltpu.make_async_remote_copy(
        src_ref=src,
        dst_ref=dst,
        send_sem=send_sem,
        recv_sem=recv_sem,
        device_id=target,
        device_id_type=MESH,
    )


epsilon = 1e-06


def layer_norm(value, gain, shift):
    center = value - jnp.mean(value, axis=-1, keepdims=True)
    spread = jnp.mean(center * center, axis=-1, keepdims=True)
    return center * lax.rsqrt(spread + epsilon) * gain + shift


def exact_gelu(value):
    return jax.nn.gelu(value, approximate=False)


def row_contract(left, right):
    return lax.dot_general(
        left, right, (((0,), (0,)), ((), ())), preferred_element_type=jnp.float32
    )


def back_product(grad, weight):
    return lax.dot_general(
        grad, weight, (((1,), (1,)), ((), ())), preferred_element_type=jnp.float32
    )


def column_sum(value):
    return jnp.sum(value.astype(jnp.float32), axis=0)


def head_major(value, heads):
    return value.reshape(value.shape[0], heads, -1).transpose(1, 0, 2)


def token_major(value):
    return value.transpose(1, 0, 2).reshape(value.shape[1], value.shape[0] * value.shape[2])


def entry_kernel(
    seqs, blks, parts, x_ref, w_ref, a0, a1, a2, o_ref, wall_ref, f0, f1, f2,
    own_sem, ssem, rsem, wl, ws, wr, us, ur, al, zs, zr, ns, nr, ms, mr,
):
    half = blks // 2
    s = lax.axis_index("seq")
    b = lax.axis_index("blk")
    k = b // 2
    c = lax.rem(b, 2)
    mate = b + 1 - 2 * c
    left = lax.rem(b + blks - 2, blks)
    right = lax.rem(b + 2, blks)
    has_left = k > 0
    has_right = k < half - 1
    blk_peers = [{"blk": lax.rem(b + d, blks)} for d in range(1, blks)]
    seq_peers = [{"seq": lax.rem(s + d, seqs)} for d in range(1, seqs)]
    greet(blk_peers + seq_peers)

    def slab(d):
        peer = lax.rem(b + d, blks)
        return send(w_ref.at[peer], wall_ref.at[s, b], ws.at[d], wr.at[d], {"blk": peer})

    def group(d):
        return send(
            wall_ref.at[s], wall_ref.at[s], us.at[d], ur.at[d], {"seq": lax.rem(s + d, seqs)}
        )

    def piece(src, blk, p, to, way):
        return send(src, o_ref.at[blk, p], ssem.at[way, blk, p], rsem.at[blk, p], {"blk": to})

    shards = ((a0, f0), (a1, f1), (a2, f2))
    x_next = s + 1 - 2 * lax.rem(s, 2)
    y_next = s + 2 - 4 * (s // 2)
    across = 3 - s
    low_part = pl.ds(0, half // 2)
    high_part = pl.ds(half // 2, half // 2)

    def along(a, d):
        own_ref, full = shards[a]
        to = 2 * lax.rem(k + d, half) + c
        return send(own_ref, full.at[s, k, c], zs.at[a, d], zr.at[a, d], {"blk": to})

    def beside(a, way):
        full = shards[a][1]
        whole = full.at[s, :, c]
        if way == 0:
            return send(whole, whole, ns.at[a, 0], nr.at[a, 0], {"seq": x_next})
        if way == 1:
            return send(whole, whole, ns.at[a, 1], nr.at[a, 1], {"seq": y_next})
        if way == 2:
            part = full.at[y_next, low_part, c]
            return send(part, part, ns.at[a, 2], nr.at[a, 2], {"seq": x_next})
        part = full.at[x_next, high_part, c]
        return send(part, part, ns.at[a, 3], nr.at[a, 3], {"seq": y_next})

    def pair(a, i, src):
        part = shards[a][1].at[src, :, c]
        return send(part, part, ms.at[a, i], mr.at[a, i], {"blk": mate})

    for d in range(1, blks):
        slab(d).start()
    for a in range(3):
        for d in range(1, half):
            along(a, d).start()
        pltpu.make_async_copy(shards[a][0], shards[a][1].at[s, k, c], al.at[a]).start()
    own_slab = pltpu.make_async_copy(w_ref.at[b], wall_ref.at[s, b], wl)
    own_slab.start()
    for p in range(parts):
        @pl.when(has_left)
        def _():
            piece(x_ref.at[p], b, p, left, 0).start()

        @pl.when(has_right)
        def _():
            piece(x_ref.at[p], b, p, right, 1).start()
    for p in range(parts):
        piece(x_ref.at[p], b, p, mate, 2).start()
    own = pltpu.make_async_copy(x_ref, o_ref.at[b], own_sem)
    own.start()
    own_slab.wait()
    for d in range(1, blks):
        slab(d).wait_recv()
    for d in range(1, seqs):
        group(d).start()
    for a in range(3):
        pltpu.make_async_copy(shards[a][0], shards[a][1].at[s, k, c], al.at[a]).wait()
        for d in range(1, half):
            along(a, d).wait_recv()
        beside(a, 0).start()
        beside(a, 1).start()
        pair(a, 0, s).start()

    def second(a):
        beside(a, 1).wait_recv()
        beside(a, 2).start()
        pair(a, 2, y_next).start()
        beside(a, 0).wait_recv()
        beside(a, 3).start()
        pair(a, 1, x_next).start()

    def third(a):
        beside(a, 2).wait_recv()
        beside(a, 3).wait_recv()
        pair(a, 3, across).start()

    for t in range(1, half):
        for p in range(parts):
            @pl.when(k - t >= 0)
            def _():
                blk = b - 2 * t
                piece(o_ref.at[blk, p], blk, p, right, 1).wait_recv()

                @pl.when(has_right)
                def _():
                    piece(o_ref.at[blk, p], blk, p, right, 1).start()

                piece(o_ref.at[blk, p], blk, p, mate, 2).start()

            @pl.when(k + t < half)
            def _():
                blk = b + 2 * t
                piece(o_ref.at[blk, p], blk, p, left, 0).wait_recv()

                @pl.when(has_left)
                def _():
                    piece(o_ref.at[blk, p], blk, p, left, 0).start()

                piece(o_ref.at[blk, p], blk, p, mate, 2).start()

        if t == 1:
            second(0)
            second(1)
        if t == 2:
            second(2)
            third(0)
            third(1)
    third(2)
    for j in range(half):
        blk = 2 * j + 1 - c
        for p in range(parts):
            piece(o_ref.at[blk, p], blk, p, mate, 2).wait_recv()
    for j in range(half):
        blk = 2 * j + c
        for p in range(parts):
            piece(o_ref.at[blk, p], blk, p, mate, 2).wait_send()

            @pl.when(jnp.logical_and(has_right, j <= k))
            def _():
                piece(o_ref.at[blk, p], blk, p, right, 1).wait_send()

            @pl.when(jnp.logical_and(has_left, j >= k))
            def _():
                piece(o_ref.at[blk, p], blk, p, left, 0).wait_send()
    own.wait()
    for d in range(1, blks):
        slab(d).wait_send()
    for d in range(1, seqs):
        group(d).wait()
    for a in range(3):
        for i, src in enumerate((s, x_next, y_next, across)):
            pair(a, i, src).wait()
        for way in range(4):
            beside(a, way).wait_send()
        for d in range(1, half):
            along(a, d).wait_send()


def entry(hidden, slabs, shards, seqs, blks, parts):
    rows, width = hidden.shape
    dma = pltpu.SemaphoreType.DMA
    return pl.pallas_call(
        functools.partial(entry_kernel, seqs, blks, parts),
        name="entry",
        out_shape=(
            jax.ShapeDtypeStruct((blks, parts, rows // parts, width), LOW),
            jax.ShapeDtypeStruct((seqs,) + slabs.shape, LOW),
        )
        + tuple(jax.ShapeDtypeStruct((seqs, blks // 2, 2) + x.shape, LOW) for x in shards),
        in_specs=[spec(pltpu.VMEM)] * 5,
        out_specs=(spec(ANY),) * 5,
        scratch_shapes=[
            dma, dma((3, blks, parts)), dma((blks, parts)), dma,
            dma((blks,)), dma((blks,)), dma((seqs,)), dma((seqs,)),
            dma((3,)), dma((3, blks // 2)), dma((3, blks // 2)),
            dma((3, 4)), dma((3, 4)), dma((3, 4)), dma((3, 4)),
        ],
        compiler_params=pltpu.CompilerParams(collective_id=0, has_side_effects=True),
        cost_estimate=pl.CostEstimate(flops=0, transcendentals=0, bytes_accessed=200 * 10**6),
    )(hidden.reshape(parts, rows // parts, width), slabs, *shards)


def return_kernel(blks, nat_ref, pack_ref, even_ref, odd_ref, buf, lsem, ssem, rsem):
    b = lax.axis_index("blk")
    k = b // 2
    c = lax.rem(b, 2)
    greet([{"blk": lax.rem(b + d, blks)} for d in range(1, blks)])
    start_return(blks, b, k, c, nat_ref, pack_ref, even_ref, odd_ref, buf, lsem, ssem, rsem)
    finish_return(blks, b, k, c, nat_ref, pack_ref, even_ref, odd_ref, ssem, rsem)


def full_way(blks, b, d, nat_ref, even_ref, ssem, rsem, slot):
    peer = lax.rem(b + d, blks)
    return send(nat_ref.at[peer], even_ref.at[slot], ssem.at[d], rsem.at[d], {"blk": peer})


def start_return(blks, b, k, c, nat_ref, pack_ref, even_ref, odd_ref, buf, lsem, ssem, rsem):
    @pl.when(c == 0)
    def _():
        for d in range(1, blks):
            full_way(blks, b, d, nat_ref, even_ref, ssem, rsem, k).start()
        inward = pltpu.make_async_copy(nat_ref.at[b], buf, lsem)
        inward.start()
        inward.wait()
        outward = pltpu.make_async_copy(buf, even_ref.at[k], lsem)
        outward.start()
        outward.wait()

    @pl.when(c == 1)
    def _():
        for d in range(1, blks):
            full_way(blks, b, d, pack_ref, odd_ref, ssem, rsem, k).start()
        part = buf.at[pl.ds(0, pack_ref.shape[1])]
        inward = pltpu.make_async_copy(pack_ref.at[b], part, lsem)
        inward.start()
        inward.wait()
        outward = pltpu.make_async_copy(part, odd_ref.at[k], lsem)
        outward.start()
        outward.wait()


def finish_return(blks, b, k, c, nat_ref, pack_ref, even_ref, odd_ref, ssem, rsem):
    for d in range(1, blks):
        source = lax.rem(b + blks - d, blks)

        @pl.when(lax.rem(source, 2) == 0)
        def _():
            full_way(blks, b, d, nat_ref, even_ref, ssem, rsem, source // 2).wait_recv()

        @pl.when(lax.rem(source, 2) == 1)
        def _():
            full_way(blks, b, d, pack_ref, odd_ref, ssem, rsem, source // 2).wait_recv()

    @pl.when(c == 0)
    def _():
        for d in range(1, blks):
            full_way(blks, b, d, nat_ref, even_ref, ssem, rsem, k).wait_send()

    @pl.when(c == 1)
    def _():
        for d in range(1, blks):
            full_way(blks, b, d, pack_ref, odd_ref, ssem, rsem, k).wait_send()


def return_rows(nat, pack, collective_id):
    blks = nat.shape[0]
    dma = pltpu.SemaphoreType.DMA
    return pl.pallas_call(
        functools.partial(return_kernel, blks),
        name="return_rows",
        out_shape=(
            jax.ShapeDtypeStruct((blks // 2,) + nat.shape[1:], LOW),
            jax.ShapeDtypeStruct((blks // 2,) + pack.shape[1:], LOW),
        ),
        in_specs=[spec(ANY)] * 2,
        out_specs=(spec(ANY), spec(ANY)),
        scratch_shapes=[pltpu.VMEM(nat.shape[1:], LOW), dma, dma((blks,)), dma((blks,))],
        compiler_params=pltpu.CompilerParams(collective_id=collective_id, has_side_effects=True),
        cost_estimate=pl.CostEstimate(flops=0, transcendentals=0, bytes_accessed=80 * 10**6),
    )(nat, pack)


def spread_kernel(
    blks, even_ref, odd_ref, grad_ref, nat_ref, pack_ref, total_hbm,
    buf, mine, theirs, total, lsem, ssem, rsem, ml, ms, mr, tl,
):
    b = lax.axis_index("blk")
    c = lax.rem(b, 2)
    mate = b + 1 - 2 * c
    greet([{"blk": lax.rem(b + d, blks)} for d in range(1, blks)])
    swap = send(grad_ref.at[:, 1 - c], theirs, ms, mr, {"blk": mate})
    swap.start()
    load = pltpu.make_async_copy(grad_ref.at[:, c], mine, ml)
    load.start()

    def full(d, slot):
        peer = lax.rem(b + d, blks)
        return send(
            even_ref.at[peer // 2], nat_ref.at[slot], ssem.at[d], rsem.at[d], {"blk": peer}
        )

    def packed(d, slot):
        peer = lax.rem(b + d, blks)
        return send(
            odd_ref.at[peer // 2], pack_ref.at[slot], ssem.at[d], rsem.at[d], {"blk": peer}
        )

    for d in range(1, blks):
        to_even = lax.rem(b + d, 2) == 0

        @pl.when(to_even)
        def _():
            full(d, b).start()

        @pl.when(jnp.logical_not(to_even))
        def _():
            packed(d, b).start()

    load.wait()
    swap.wait()

    @pl.loop(0, total.shape[0])
    def _(o):
        total[o] = (mine[o].astype(F32) + theirs[o].astype(F32)).astype(LOW)

    store = pltpu.make_async_copy(total, total_hbm, tl)
    store.start()

    @pl.when(c == 0)
    def _():
        inward = pltpu.make_async_copy(even_ref.at[b // 2], buf, lsem)
        inward.start()
        inward.wait()
        outward = pltpu.make_async_copy(buf, nat_ref.at[b], lsem)
        outward.start()
        outward.wait()
        for d in range(1, blks):
            full(d, lax.rem(b + blks - d, blks)).wait_recv()

    @pl.when(c == 1)
    def _():
        part = buf.at[pl.ds(0, odd_ref.shape[1])]
        inward = pltpu.make_async_copy(odd_ref.at[b // 2], part, lsem)
        inward.start()
        inward.wait()
        outward = pltpu.make_async_copy(part, pack_ref.at[b], lsem)
        outward.start()
        outward.wait()
        for d in range(1, blks):
            packed(d, lax.rem(b + blks - d, blks)).wait_recv()

    for d in range(1, blks):
        to_even = lax.rem(b + d, 2) == 0

        @pl.when(to_even)
        def _():
            full(d, b).wait_send()

        @pl.when(jnp.logical_not(to_even))
        def _():
            packed(d, b).wait_send()

    store.wait()


def spread_rows(even, odd, grads, collective_id):
    blks = 2 * even.shape[0]
    half_shape = grads.shape[:1] + grads.shape[2:]
    dma = pltpu.SemaphoreType.DMA
    return pl.pallas_call(
        functools.partial(spread_kernel, blks),
        name="spread_rows",
        out_shape=(
            jax.ShapeDtypeStruct((blks,) + even.shape[1:], LOW),
            jax.ShapeDtypeStruct((blks,) + odd.shape[1:], LOW),
            jax.ShapeDtypeStruct(half_shape, LOW),
        ),
        in_specs=[spec(ANY)] * 3,
        out_specs=(spec(ANY),) * 3,
        scratch_shapes=[
            pltpu.VMEM(even.shape[1:], LOW),
            pltpu.VMEM(half_shape, LOW),
            pltpu.VMEM(half_shape, LOW),
            pltpu.VMEM(half_shape, LOW),
            dma, dma((blks,)), dma((blks,)), dma, dma, dma, dma,
        ],
        compiler_params=pltpu.CompilerParams(
            collective_id=collective_id, has_side_effects=True, vmem_limit_bytes=BIG
        ),
        cost_estimate=pl.CostEstimate(flops=0, transcendentals=0, bytes_accessed=80 * 10**6),
    )(even, odd, grads)


def exit_kernel(
    seqs, blks, nat_ref, pack_ref, grad_ref, big_ref, even_ref, odd_ref, out_ref, big_out,
    buf, stage, total, big_stage, big_total,
    lsem, ssem, rsem, us, ur, gl, gs, gr, bl, bu, bv, cl, cs, cr,
):
    s = lax.axis_index("seq")
    b = lax.axis_index("blk")
    k = b // 2
    c = lax.rem(b, 2)
    blk_peers = [{"blk": lax.rem(b + d, blks)} for d in range(1, blks)]
    seq_peers = [{"seq": lax.rem(s + d, seqs)} for d in range(1, seqs)]
    greet(blk_peers + seq_peers)

    def group(d):
        peer = lax.rem(s + d, seqs)
        return send(grad_ref.at[peer], stage.at[d], us.at[d], ur.at[d], {"seq": peer})

    def slab(d):
        peer = lax.rem(b + d, blks)
        return send(total.at[peer], out_ref.at[b], gs.at[d], gr.at[d], {"blk": peer})

    chips = blks // 2
    pieces = big_ref.shape[2]

    def big_group(p, d):
        peer = lax.rem(s + d, seqs)
        return send(
            big_ref.at[peer, :, p], big_stage.at[p, d], bu.at[p, d], bv.at[p, d], {"seq": peer}
        )

    def big_slab(p, d):
        to = lax.rem(k + d, chips)
        return send(
            big_total.at[p, to], big_out.at[k, p], cs.at[p, d], cr.at[p, d], {"blk": 2 * to + c}
        )

    def big_own(p):
        return pltpu.make_async_copy(big_ref.at[s, :, p], big_stage.at[p, 0], bl.at[p])

    for p in range(pieces):
        big_own(p).start()
    for d in range(1, seqs):
        group(d).start()
    for p in range(pieces):
        for d in range(1, seqs):
            big_group(p, d).start()
    start_return(blks, b, k, c, nat_ref, pack_ref, even_ref, odd_ref, buf, lsem, ssem, rsem)
    for d in range(1, seqs):
        group(d).wait_recv()
    for o in range(blks):
        acc = grad_ref[s, o].astype(F32)
        for d in range(1, seqs):
            acc = acc + stage[d, o].astype(F32)
        total[o] = acc.astype(LOW)
    for d in range(1, blks):
        slab(d).start()
    own = pltpu.make_async_copy(total.at[b], out_ref.at[b], gl)
    own.start()
    own.wait()
    for p in range(pieces):
        big_own(p).wait()
        for d in range(1, seqs):
            big_group(p, d).wait_recv()

        @pl.loop(0, chips)
        def _(o):
            acc = big_stage[p, 0, o].astype(F32)
            for d in range(1, seqs):
                acc = acc + big_stage[p, d, o].astype(F32)
            big_total[p, o] = acc.astype(LOW)

        for d in range(1, chips):
            big_slab(p, d).start()
        keep = pltpu.make_async_copy(big_total.at[p, k], big_out.at[k, p], cl.at[p])
        keep.start()
        keep.wait()
    finish_return(blks, b, k, c, nat_ref, pack_ref, even_ref, odd_ref, ssem, rsem)
    for d in range(1, blks):
        slab(d).wait()
    for d in range(1, seqs):
        group(d).wait_send()
    for p in range(pieces):
        for d in range(1, chips):
            big_slab(p, d).wait()
        for d in range(1, seqs):
            big_group(p, d).wait_send()


def leave(nat, pack, grads, big):
    blks = nat.shape[0]
    seqs = grads.shape[0]
    chips, pieces = big.shape[1:3]
    dma = pltpu.SemaphoreType.DMA
    return pl.pallas_call(
        functools.partial(exit_kernel, seqs, blks),
        name="leave",
        out_shape=(
            jax.ShapeDtypeStruct((blks // 2,) + nat.shape[1:], LOW),
            jax.ShapeDtypeStruct((blks // 2,) + pack.shape[1:], LOW),
            jax.ShapeDtypeStruct(grads.shape[1:], LOW),
            jax.ShapeDtypeStruct(big.shape[1:], LOW),
        ),
        in_specs=[spec(ANY), spec(ANY), spec(pltpu.VMEM), spec(ANY)],
        out_specs=(spec(ANY),) * 4,
        scratch_shapes=[
            pltpu.VMEM(nat.shape[1:], LOW),
            pltpu.VMEM(grads.shape, LOW),
            pltpu.VMEM(grads.shape[1:], LOW),
            pltpu.VMEM((pieces, seqs, chips) + big.shape[3:], LOW),
            pltpu.VMEM((pieces, chips) + big.shape[3:], LOW),
            dma, dma((blks,)), dma((blks,)), dma((seqs,)), dma((seqs,)),
            dma, dma((blks,)), dma((blks,)),
            dma((pieces,)), dma((pieces, seqs)), dma((pieces, seqs)),
            dma((pieces,)), dma((pieces, chips)), dma((pieces, chips)),
        ],
        compiler_params=pltpu.CompilerParams(
            collective_id=3, has_side_effects=True, vmem_limit_bytes=BIG
        ),
        cost_estimate=pl.CostEstimate(flops=0, transcendentals=0, bytes_accessed=200 * 10**6),
    )(nat, pack, grads, big)


def owner_facts(hd, chips):
    b = lax.axis_index("blk")
    k = b // 2
    odd = lax.rem(b, 2)
    first = jnp.where(odd == 0, 2 * hd * k, (2 * chips + k) * hd)
    return 2 - odd, first, (2 - odd) * hd


def lane_of(rows):
    return lax.broadcasted_iota(jnp.int32, (rows, 128), 1)


def low_lanes(value, slot, hd):
    lane = lane_of(value.shape[0])
    keep = jnp.logical_and(lane >= slot * hd, lane < (slot + 1) * hd)
    return jnp.where(keep, value, 0.0).astype(LOW)


def part_of(u, t):
    return pl.ds(u * 512 + t, 128, stride=4)


def row_part(ref, u, t):
    return ref[part_of(u, t), :]


def column_softmax(scores):
    weights = jnp.exp(scores - jnp.max(scores, axis=0, keepdims=True))
    return weights * (1.0 / jnp.sum(weights, axis=0, keepdims=True))


def attend_kernel(
    hd, scale, order, hid_hbm, gathered, proj_hbm, nat, pack, vecs, bias_inner,
    rows4, take, take_b, mix, mix_b, back, wide_weight, weight, hid, proj, in_sems, out_sem,
):
    length, width = hid.shape
    blks, step, _ = nat.shape
    devices = gathered.shape[0]
    own_rows = width // devices
    per = bias_inner.shape[1] // devices
    heads_here, first, _ = owner_facts(hd, blks // 2)

    def fetch(i):
        part = pl.ds(pl.multiple_of(i * step, step), step)
        return pltpu.make_async_copy(hid_hbm.at[part], hid.at[part], in_sems.at[i])

    for i in range(length // step):
        fetch(i).start()
    for i in range(devices):
        slab = gathered[i].astype(F32)
        wide_weight[i * own_rows : (i + 1) * own_rows, :] = slab[:own_rows, :]
        vecs[:, i * own_rows : (i + 1) * own_rows] = slab[own_rows:, :own_rows]
        bias_inner[0:1, i * per : (i + 1) * per] = slab[own_rows : own_rows + 1, 128 : 128 + per]
    weight[...] = wide_weight[...].astype(LOW)
    tile = vecs[:, pl.ds(pl.multiple_of(first // 128 * 128, 128), 128)]
    tile = jnp.where(lax.rem(first, 128) == 0, tile, pltpu.roll(tile, 64, 1))
    bias = jnp.concatenate([tile[0:1], jnp.zeros((1, 128), F32), tile[1:2]], axis=1)

    @pl.loop(0, length // step)
    def _(i):
        at = pl.multiple_of(i * step, step)
        fetch(i).wait()
        low = (nn_dot(hid[pl.ds(at, step), :], weight[...]) + bias).astype(LOW)
        proj[pl.ds(at, step), :] = low
        wide = low.astype(F32)
        for t in range(3):
            rows4[pl.ds(4 * at + t, step, stride=4), :] = wide[:, t * 128 : (t + 1) * 128]

    store = pltpu.make_async_copy(proj, proj_hbm, out_sem)
    store.start()
    span = GROUP * 128

    def gather(buf, base):
        for j in range(span):
            buf[4 * j : 4 * j + 4, :] = rows4[pl.ds(pl.multiple_of(4 * order[base + j], 4), 4), :]

    def attend_group(slot, buf, out):
        for u in range(GROUP):
            own = pl.ds(u * 128, 128)
            query = low_lanes(row_part(buf, u, 0) * scale, slot, hd)
            probs = column_softmax(nt_dot(row_part(buf, u, 1).astype(LOW), query))
            out[own, :] = tn_dot(probs.astype(LOW), row_part(buf, u, 2).astype(LOW))

    def scatter(slot, out, base):
        for j in range(span):
            back[pl.ds(slot * length + order[base + j], 1), :] = out[pl.ds(j, 1), :]

    @pl.loop(0, heads_here)
    def _(slot):
        begin = slot * length
        gather(take, begin)

        @pl.loop(0, length // (2 * span))
        def _(i):
            base = begin + 2 * i * span
            gather(take_b, base + span)
            attend_group(slot, take, mix)
            scatter(slot, mix, base)
            gather(take, jnp.minimum(base + 2 * span, begin + length - span))
            attend_group(slot, take_b, mix_b)
            scatter(slot, mix_b, base + span)

    lane = lane_of(step)

    @pl.when(heads_here == 2)
    def _():
        @pl.loop(0, length // step)
        def _(i):
            at = pl.multiple_of(i * step, step)
            nat[i] = jnp.where(
                lane < hd, back[pl.ds(at, step), :], back[pl.ds(length + at, step), :]
            ).astype(LOW)

    half = step // 2

    @pl.when(heads_here == 1)
    def _():
        @pl.loop(0, length // step)
        def _(i):
            at = pl.multiple_of(i * step, step)
            upper = pltpu.roll(back[pl.ds(at + half, half), :], hd, 1)
            pack[i] = jnp.where(lane[:half] < hd, back[pl.ds(at, half), :], upper).astype(LOW)

    store.wait()


def attend(order, hid, gathered, blks, ff, hd, scale):
    length, width = hid.shape
    step = length // blks
    return pl.pallas_call(
        functools.partial(attend_kernel, hd, scale),
        name="attend",
        out_shape=(
            jax.ShapeDtypeStruct((length, 384), LOW),
            jax.ShapeDtypeStruct((blks, step, 128), LOW),
            jax.ShapeDtypeStruct((blks, step // 2, 128), LOW),
            jax.ShapeDtypeStruct((8, width), F32),
            jax.ShapeDtypeStruct((8, ff), F32),
        ),
        in_specs=[spec(pltpu.SMEM), spec(ANY), spec(pltpu.VMEM)],
        out_specs=(spec(ANY),) + (spec(pltpu.VMEM),) * 4,
        scratch_shapes=[
            pltpu.VMEM((4 * length, 128), F32),
            pltpu.VMEM((GROUP * 512, 128), F32),
            pltpu.VMEM((GROUP * 512, 128), F32),
            pltpu.VMEM((GROUP * 128, 128), F32),
            pltpu.VMEM((GROUP * 128, 128), F32),
            pltpu.VMEM((2 * length, 128), F32),
            pltpu.VMEM((width, 384), F32),
            pltpu.VMEM((width, 384), LOW),
            pltpu.VMEM((length, width), LOW),
            pltpu.VMEM((length, 384), LOW),
            pltpu.SemaphoreType.DMA((blks,)),
            pltpu.SemaphoreType.DMA,
        ],
        compiler_params=pltpu.CompilerParams(vmem_limit_bytes=BIG),
        cost_estimate=pl.CostEstimate(
            flops=5 * 10**9, transcendentals=0, bytes_accessed=100 * 10**6
        ),
    )(order, hid, gathered)


def attend_back_kernel(
    hd, scale, order, hidden_hbm, proj, gnat, gpack, extra, znat_hbm, zpack_hbm, slabs,
    rows4, take, take_b, out4, out4_b, back4, hid, wide_grad,
    znat, zpack, sem, nat_sems, pack_sems,
):
    length = proj.shape[0]
    step = gnat.shape[1]
    half = step // 2
    heads_here, first_col, limit = owner_facts(hd, gnat.shape[0] // 2)
    fetch = pltpu.make_async_copy(hidden_hbm, hid, sem)
    fetch.start()

    @pl.loop(0, length // step)
    def _(i):
        at = pl.multiple_of(i * step, step)
        wide = proj[pl.ds(at, step), :].astype(F32)
        for t in range(3):
            rows4[pl.ds(4 * at + t, step, stride=4), :] = wide[:, t * 128 : (t + 1) * 128]

        @pl.when(heads_here == 2)
        def _():
            rows4[pl.ds(4 * at + 3, step, stride=4), :] = gnat[i].astype(F32)

        @pl.when(heads_here == 1)
        def _():
            pair = gpack[i].astype(F32)
            rows4[pl.ds(4 * at + 3, half, stride=4), :] = pair
            rows4[pl.ds(4 * (at + half) + 3, half, stride=4), :] = pltpu.roll(pair, hd, 1)

    span = GROUP * 128

    def gather(buf, base):
        for j in range(span):
            buf[4 * j : 4 * j + 4, :] = rows4[pl.ds(pl.multiple_of(order[base + j], 4), 4), :]

    def attend_group(slot, buf, out):
        for u in range(GROUP):
            own = pl.ds(u * 128, 128)
            query = low_lanes(row_part(buf, u, 0) * scale, slot, hd)
            grad = low_lanes(row_part(buf, u, 3), slot, hd)
            keys = row_part(buf, u, 1).astype(LOW)
            probs = column_softmax(nt_dot(keys, query))
            prob_grad = nt_dot(row_part(buf, u, 2).astype(LOW), grad)
            shift = jnp.sum(probs * prob_grad, axis=0, keepdims=True)
            score_low = (probs * (prob_grad - shift)).astype(LOW)
            out[part_of(u, 0), :] = tn_dot(score_low, keys) * scale
            out[part_of(u, 1), :] = nn_dot(score_low, query)
            out[part_of(u, 2), :] = nn_dot(probs.astype(LOW), grad)

    def scatter(slot, out, base):
        back_slot = back4.at[pl.ds(pl.multiple_of(4 * slot * length, 4 * length), 4 * length), :]
        for j in range(span):
            at = pl.multiple_of(order[base + j], 4)
            back_slot[pl.ds(at, 4), :] = out[4 * j : 4 * j + 4, :]

    @pl.loop(0, heads_here)
    def _(slot):
        begin = slot * length
        gather(take, begin)

        @pl.loop(0, length // (2 * span))
        def _(i):
            base = begin + 2 * i * span
            gather(take_b, base + span)
            attend_group(slot, take, out4)
            scatter(slot, out4, base)
            gather(take, jnp.minimum(base + 2 * span, begin + length - span))
            attend_group(slot, take_b, out4_b)
            scatter(slot, out4_b, base + span)

    lane = lane_of(step)
    fetch.wait()
    wide_grad[...] = jnp.zeros_like(wide_grad)
    zero = jnp.zeros((1, 384), F32)

    def put_nat(i):
        return pltpu.make_async_copy(znat.at[i], znat_hbm.at[i], nat_sems.at[i])

    def put_pack(i):
        return pltpu.make_async_copy(zpack.at[i], zpack_hbm.at[i], pack_sems.at[i])

    def settle(i, sums):
        at = pl.multiple_of(i * step, step)
        parts = []
        for t in range(3):
            cols = pl.ds(t * 128, 128)
            first = back4[pl.ds(4 * at + t, step, stride=4), :]
            second = back4[pl.ds(4 * (length + at) + t, step, stride=4), :]
            second = jnp.where(heads_here == 2, second, jnp.zeros_like(second))
            low = jnp.where(lane < hd, first, second).astype(LOW)
            znat[i, :, cols] = low
            wide = low.astype(F32)
            parts.append(jnp.sum(wide, axis=0, keepdims=True))
            zpack[i, :, cols] = (wide[:half] + pltpu.roll(wide[half:], hd, 1)).astype(LOW)
        put_nat(i).start()
        put_pack(i).start()
        wide_grad[...] += tn_dot(hid[pl.ds(at, step), :], znat[i])
        return sums + jnp.concatenate(parts, axis=1)

    sums = lax.fori_loop(0, length // step, settle, zero)
    devices = slabs.shape[0]
    own = hid.shape[1] // devices
    lane8 = lane_of(8)
    row8 = lax.broadcasted_iota(jnp.int32, (8, 128), 0)
    q_row = jnp.broadcast_to(sums[:, :128], (8, 128))
    v_row = jnp.broadcast_to(sums[:, 256:], (8, 128))
    for i in range(devices):
        begin = i * own - first_col
        q_lane = lane8 + begin
        v_lane = q_lane - 64
        q_part = pltpu.roll(q_row, lax.rem(4096 - begin, 128), 1)
        v_part = pltpu.roll(v_row, lax.rem(4096 - begin + 64, 128), 1)
        q_ok = (lane8 < own) & (q_lane >= 0) & (q_lane < limit)
        v_ok = (lane8 >= 64) & (lane8 < 64 + own) & (v_lane >= 0) & (v_lane < limit)
        line = jnp.where(q_ok, q_part, jnp.where(v_ok, v_part, 0.0))
        tile = jnp.where(row8 == 0, line, extra[i])
        tail = jnp.concatenate([tile, jnp.zeros((8, 256), F32)], axis=1)
        at = i * own
        slabs[i, : own - 8, :] = wide_grad[at : at + own - 8, :].astype(LOW)
        slabs[i, own - 8 :, :] = jnp.concatenate(
            [wide_grad[at + own - 8 : at + own, :], tail], axis=0
        ).astype(LOW)
    for i in range(length // step):
        put_nat(i).wait()
        put_pack(i).wait()


def attend_back(order, hidden_all, proj, gnat, gpack, extra, hd, scale):
    order = 4 * order
    length = proj.shape[0]
    blks, step, _ = gnat.shape
    devices = extra.shape[0]
    width = hidden_all.shape[1]
    return pl.pallas_call(
        functools.partial(attend_back_kernel, hd, scale),
        name="attend_back",
        out_shape=(
            jax.ShapeDtypeStruct((blks, step, 384), LOW),
            jax.ShapeDtypeStruct((blks, step // 2, 384), LOW),
            jax.ShapeDtypeStruct((devices, width // devices + 8, 384), LOW),
        ),
        in_specs=[spec(pltpu.SMEM), spec(ANY)] + [spec(pltpu.VMEM)] * 4,
        out_specs=(spec(ANY), spec(ANY), spec(pltpu.VMEM)),
        scratch_shapes=[
            pltpu.VMEM((4 * length, 128), F32),
            pltpu.VMEM((GROUP * 512, 128), F32),
            pltpu.VMEM((GROUP * 512, 128), F32),
            pltpu.VMEM((GROUP * 512, 128), F32),
            pltpu.VMEM((GROUP * 512, 128), F32),
            pltpu.VMEM((8 * length, 128), F32),
            pltpu.VMEM(hidden_all.shape, LOW),
            pltpu.VMEM((width, 384), F32),
            pltpu.VMEM((blks, step, 384), LOW),
            pltpu.VMEM((blks, step // 2, 384), LOW),
            pltpu.SemaphoreType.DMA,
            pltpu.SemaphoreType.DMA((blks,)),
            pltpu.SemaphoreType.DMA((blks,)),
        ],
        compiler_params=pltpu.CompilerParams(vmem_limit_bytes=BIG),
        cost_estimate=pl.CostEstimate(
            flops=8 * 10**9, transcendentals=0, bytes_accessed=120 * 10**6
        ),
    )(order, hidden_all, proj, gnat, gpack, extra)


def middle_kernel(
    hd, ceven, codd, hidden, first_hbm, outer_hbm, vecs, bias_inner, cot, mask,
    hout, resid, geven, godd, merged_hbm, extra,
    wa, wb, ctx, act, slope, ilow, first, flow, olow, unit, acc, hid_low, sums, inner_sums, merged, sems,
):
    rows, width = hidden.shape
    ff = outer_hbm.shape[0]
    chips = ceven.shape[0]
    get_out = pltpu.make_async_copy(
        first_hbm.at[:, pl.ds(0, width)], wa.at[:, pl.ds(0, width)], sems.at[0]
    )
    get_in = pltpu.make_async_copy(
        first_hbm.at[:, pl.ds(width, ff)], wa.at[:, pl.ds(width, ff)], sems.at[1]
    )
    get_outer = pltpu.make_async_copy(outer_hbm, wb, sems.at[2])
    get_out.start()
    get_in.start()
    get_outer.start()
    half = rows // 2
    lane = lane_of(half)
    low_half = lane < hd
    for z in range(chips):
        ctx[:, z * 128 : (z + 1) * 128] = ceven[z]
    for z in range(0, chips, 2):
        here = codd[z].astype(F32)
        there = codd[z + 1].astype(F32)
        at = chips * 128 + z * 64
        ctx[:half, at : at + 128] = jnp.where(low_half, here, pltpu.roll(there, hd, 1)).astype(LOW)
        ctx[half:, at : at + 128] = jnp.where(low_half, pltpu.roll(here, hd, 1), there).astype(LOW)
    sums[...] = jnp.zeros_like(sums)
    wide = 256
    tile = 64

    def add_rows(row, value):
        sums[row : row + 1, :] += jnp.sum(value, axis=0, keepdims=True)

    get_out.wait()

    @pl.loop(0, width // wide)
    def _(n):
        at = pl.multiple_of(n * wide, wide)
        acc[:, pl.ds(at, wide)] = nn_dot(ctx[...], wa[:, pl.ds(at, wide)])

    @pl.loop(0, rows // tile)
    def _(i):
        own = pl.ds(pl.multiple_of(i * tile, tile), tile)
        value = hidden[own, :].astype(F32) + acc[own, :] + vecs[2:3, :]
        center = value - jnp.mean(value, axis=-1, keepdims=True)
        spread = jnp.mean(center * center, axis=-1, keepdims=True)
        inv = lax.rsqrt(spread + epsilon)
        norm = center * inv * vecs[3:4, :] + vecs[4:5, :]
        first[own, :] = norm
        flow[own, :] = norm.astype(LOW)
        unit[own, :] = center * inv
        resid[own, 0:128] = jnp.broadcast_to(inv, (tile, 128))

    get_in.wait()

    @pl.loop(0, ff // wide)
    def _(j):
        at = pl.multiple_of(j * wide, wide)
        cols = pl.ds(at, wide)
        pre = nn_dot(flow[...], wa[:, pl.ds(width + at, wide)]) + bias_inner[0:1, cols]
        gate = 0.5 + 0.5 * lax.erf(pre * (0.5**0.5))
        act[:, cols] = (pre * gate).astype(LOW)
        slope[:, cols] = gate + pre * jnp.exp(-0.5 * pre * pre) * (0.5 / math.pi) ** 0.5

    get_outer.wait()

    @pl.loop(0, width // wide)
    def _(n):
        at = pl.multiple_of(n * wide, wide)
        acc[:, pl.ds(at, wide)] = nn_dot(act[...], wb[:, pl.ds(at, wide)])

    @pl.loop(0, rows // tile)
    def _(i):
        own = pl.ds(pl.multiple_of(i * tile, tile), tile)
        value = first[own, :] + acc[own, :] + vecs[5:6, :]
        center = value - jnp.mean(value, axis=-1, keepdims=True)
        spread = jnp.mean(center * center, axis=-1, keepdims=True)
        inv = lax.rsqrt(spread + epsilon)
        norm = center * inv
        hout[own, :] = (norm * vecs[6:7, :] + vecs[7:8, :]).astype(LOW)
        out_grad = cot[own, :].astype(F32) * mask[own, :].astype(F32)
        pull = out_grad * vecs[6:7, :]
        pull = pull - jnp.mean(pull, axis=-1, keepdims=True) - norm * jnp.mean(
            pull * norm, axis=-1, keepdims=True
        )
        grad = pull * inv
        low = grad.astype(LOW)
        first[own, :] = grad
        olow[own, :] = low
        add_rows(4, low.astype(F32))
        add_rows(5, out_grad * norm)
        add_rows(6, out_grad)

    @pl.loop(0, ff // wide)
    def _(j):
        cols = pl.ds(pl.multiple_of(j * wide, wide), wide)
        low = (nt_dot(olow[...], wb[cols, :]) * slope[:, cols]).astype(LOW)
        ilow[:, cols] = low
        inner_sums[0:1, cols] = jnp.sum(low.astype(F32), axis=0, keepdims=True)

    @pl.loop(0, width // wide)
    def _(n):
        at = pl.multiple_of(n * wide, wide)
        acc[:, pl.ds(at, wide)] = nt_dot(ilow[...], wa[pl.ds(at, wide), width:])

    @pl.loop(0, rows // tile)
    def _(i):
        own = pl.ds(pl.multiple_of(i * tile, tile), tile)
        grad = acc[own, :] + first[own, :]
        norm = unit[own, :]
        inv = resid[own, 0:1]
        pull = grad * vecs[3:4, :]
        pull = pull - jnp.mean(pull, axis=-1, keepdims=True) - norm * jnp.mean(
            pull * norm, axis=-1, keepdims=True
        )
        back = pull * inv
        low = back.astype(LOW)
        resid[own, :] = back
        hid_low[own, :] = low
        add_rows(1, low.astype(F32))
        add_rows(2, grad * norm)
        add_rows(3, grad)

    @pl.loop(0, width // wide)
    def _(n):
        at = pl.multiple_of(n * wide, wide)
        acc[:, pl.ds(at, wide)] = nt_dot(hid_low[...], wa[pl.ds(at, wide), :width])

    for z in range(chips):
        geven[z] = acc[:, z * 128 : (z + 1) * 128].astype(LOW)
    for z in range(0, chips, 2):
        at = chips * 128 + z * 64
        top = acc[:half, at : at + 128]
        bottom = acc[half:, at : at + 128]
        godd[z] = jnp.where(low_half, top, pltpu.roll(bottom, hd, 1)).astype(LOW)
        godd[z + 1] = jnp.where(low_half, pltpu.roll(top, hd, 1), bottom).astype(LOW)

    devices = merged.shape[0]
    own_rows = width // devices
    outer_rows = ff // devices
    block = 384
    per = block // outer_rows

    @pl.loop(0, ff // block)
    def _(j):
        part = tn_dot(act[:, pl.ds(pl.multiple_of(j * block, block), block)], olow[...])
        for i in range(per):
            merged[j * per + i, :outer_rows, :] = part[
                i * outer_rows : (i + 1) * outer_rows, :
            ].astype(LOW)

    folds = ff // width
    many = block // own_rows
    size = merged.shape[1]
    put_outer = pltpu.make_async_copy(
        merged.at[:, pl.ds(0, outer_rows)], merged_hbm.at[:, pl.ds(0, outer_rows)], sems.at[3]
    )
    put_outer.start()

    def put_rest(m):
        part = (pl.ds(m * many, many), pl.ds(outer_rows, size - outer_rows))
        return pltpu.make_async_copy(merged.at[part], merged_hbm.at[part], sems.at[4 + m])

    for m in range(width // block):
        cols = slice(m * block, (m + 1) * block)
        for h in range(0, folds, 2):
            left = tn_dot(flow[:, cols], ilow[:, h * width : (h + 1) * width])
            right = tn_dot(flow[:, cols], ilow[:, (h + 1) * width : (h + 2) * width])
            at = outer_rows + h * own_rows
            for i in range(many):
                for r in range(0, own_rows, 8):
                    base = i * own_rows + r
                    merged[m * many + i, at + 2 * r : at + 2 * r + 16, :] = jnp.concatenate(
                        [left[base : base + 8, :], right[base : base + 8, :]], axis=0
                    ).astype(LOW)
        part = tn_dot(ctx[:, cols], hid_low[...])
        at = outer_rows + folds * own_rows
        for i in range(many):
            base = i * own_rows
            merged[m * many + i, at : at + 16, :] = part[base : base + 16, :].astype(LOW)
            merged[m * many + i, at + 16 : at + 32, :] = jnp.concatenate(
                [part[base + 16 : base + 24, :], jnp.zeros((8, width), F32)], axis=0
            ).astype(LOW)
        put_rest(m).start()

    row8 = lax.broadcasted_iota(jnp.int32, (8, 128), 0)
    for i in range(devices):
        piece = sums[:, i * own_rows : (i + 1) * own_rows]
        piece = jnp.concatenate([piece, jnp.zeros((8, 128 - own_rows), F32)], axis=1)
        inner = inner_sums[0:1, i * outer_rows : (i + 1) * outer_rows]
        inner = jnp.concatenate([inner, jnp.zeros((1, 128 - outer_rows), F32)], axis=1)
        extra[i] = jnp.where(row8 == 7, jnp.broadcast_to(inner, (8, 128)), piece)
    put_outer.wait()
    for m in range(width // block):
        put_rest(m).wait()


def middle(ceven, codd, hidden, first_half, outer_full, vecs, bias_inner, cot, mask, devices, hd):
    rows, width = hidden.shape
    ff = outer_full.shape[0]
    slab = ff // devices + (ff // width + 1) * (width // devices) + 8
    wide_low = pltpu.VMEM((rows, width), LOW)
    wide_f32 = pltpu.VMEM((rows, width), F32)
    return pl.pallas_call(
        functools.partial(middle_kernel, hd),
        name="middle",
        out_shape=(
            jax.ShapeDtypeStruct((rows, width), LOW),
            jax.ShapeDtypeStruct((rows, width), F32),
            jax.ShapeDtypeStruct(ceven.shape, LOW),
            jax.ShapeDtypeStruct(codd.shape, LOW),
            jax.ShapeDtypeStruct((devices, slab, width), LOW),
            jax.ShapeDtypeStruct((devices, 8, 128), F32),
        ),
        in_specs=[spec(pltpu.VMEM)] * 3 + [spec(ANY)] * 2 + [spec(pltpu.VMEM)] * 4,
        out_specs=(spec(pltpu.VMEM),) * 4 + (spec(ANY), spec(pltpu.VMEM)),
        scratch_shapes=[
            pltpu.VMEM(first_half.shape, LOW),
            pltpu.VMEM(outer_full.shape, LOW),
            wide_low,
            pltpu.VMEM((rows, ff), LOW),
            pltpu.VMEM((rows, ff), F32),
            pltpu.VMEM((rows, ff), LOW),
            wide_f32, wide_low, wide_low, wide_f32, wide_f32, wide_low,
            pltpu.VMEM((8, width), F32),
            pltpu.VMEM((8, ff), F32),
            pltpu.VMEM((devices, slab, width), LOW),
            pltpu.SemaphoreType.DMA((4 + width // 384,)),
        ],
        compiler_params=pltpu.CompilerParams(vmem_limit_bytes=BIG),
        cost_estimate=pl.CostEstimate(
            flops=17 * 10**9, transcendentals=0, bytes_accessed=40 * 10**6
        ),
    )(ceven, codd, hidden, first_half, outer_full, vecs, bias_inner, cot, mask)


def final_kernel(
    hd, zeven, zodd, proj_hbm, resid, proj_grads, shares,
    out, gq, gk, gv, go, gi, gu, g0, g1, g2, g3, g4, g5, g6, g7, g8, wp, triple, sem,
):
    rows, width = resid.shape
    chips = zeven.shape[0]
    fetch = pltpu.make_async_copy(proj_hbm, wp, sem)
    fetch.start()
    half = rows // 2
    low_half = lane_of(half) < hd
    for t in range(3):
        cols = slice(t * 128, (t + 1) * 128)
        for z in range(chips):
            at = t * width + z * 128
            triple[:, at : at + 128] = zeven[z, :, cols]
        for z in range(0, chips, 2):
            at = t * width + chips * 128 + z * 64
            here = zodd[z, :, cols].astype(F32)
            there = zodd[z + 1, :, cols].astype(F32)
            triple[:half, at : at + 128] = jnp.where(
                low_half, here, pltpu.roll(there, hd, 1)
            ).astype(LOW)
            triple[half:, at : at + 128] = jnp.where(
                low_half, pltpu.roll(here, hd, 1), there
            ).astype(LOW)
    own = gq.shape[0]
    keep = lane_of(own) < hd
    for t, ref in enumerate((gq, gk, gv)):
        cols = slice(t * 128, (t + 1) * 128)
        for z in range(chips):
            ref[:, z * 128 : (z + 1) * 128] = proj_grads[2 * z, :, cols].astype(F32)[:own]
        for z in range(0, chips, 2):
            here = proj_grads[2 * z + 1, :, cols].astype(F32)[:own]
            there = proj_grads[2 * z + 3, :, cols].astype(F32)[:own]
            at = chips * 128 + z * 64
            ref[:, at : at + 128] = jnp.where(keep, here, pltpu.roll(there, hd, 1))
    ff = gi.shape[1]
    outer_rows = gu.shape[0]
    folds = ff // width

    def share(at, size):
        total = shares[0, at : at + size, :].astype(F32)
        for z in range(1, chips):
            total = total + shares[z, at : at + size, :].astype(F32)
        return total

    for r in range(0, outer_rows, 16):
        gu[r : r + 16, :] = share(r, 16)
    for h in range(0, folds, 2):
        at = outer_rows + h * own
        for r in range(0, own, 8):
            pair = share(at + 2 * r, 16)
            gi[r : r + 8, h * width : (h + 1) * width] = pair[:8]
            gi[r : r + 8, (h + 1) * width : (h + 2) * width] = pair[8:]
    at = outer_rows + folds * own
    go[...] = share(at, own + 8)[:own]
    total = proj_grads[0, :, :128].astype(F32)[own:]
    for d in range(1, 2 * chips):
        total = total + proj_grads[d, :, :128].astype(F32)[own:]
    g0[...] = total[0, :own]
    g1[...] = total[0, 64 : 64 + own]
    for v, ref in enumerate((g2, g3, g4)):
        ref[...] = total[1 + v, :own]
    g5[...] = total[7, : g5.shape[0]]
    for v, ref in enumerate((g6, g7, g8)):
        ref[...] = total[4 + v, :own]
    fetch.wait()
    wide = 256

    @pl.loop(0, width // wide)
    def _(n):
        at = pl.multiple_of(n * wide, wide)
        cols = pl.ds(at, wide)
        out[:, cols] = nt_dot(triple[...], wp[pl.ds(at, wide), :]) + resid[:, cols]


def final(zeven, zodd, projections, resid, proj_grads, shares, own, ff, hd):
    rows, width = resid.shape
    mats = [(rows, width)] + [(own, width)] * 4 + [(own, ff), (ff * own // width, width)]
    vectors = [(own,)] * 5 + [(ff * own // width,)] + [(own,)] * 3
    return pl.pallas_call(
        functools.partial(final_kernel, hd),
        name="final",
        out_shape=tuple(jax.ShapeDtypeStruct(shape, F32) for shape in mats + vectors),
        in_specs=[spec(pltpu.VMEM)] * 2 + [spec(ANY)] + [spec(pltpu.VMEM)] * 3,
        out_specs=(spec(pltpu.VMEM),) * 16,
        scratch_shapes=[
            pltpu.VMEM(projections.shape, LOW),
            pltpu.VMEM((rows, 3 * width), LOW),
            pltpu.SemaphoreType.DMA,
        ],
        compiler_params=pltpu.CompilerParams(vmem_limit_bytes=BIG),
        cost_estimate=pl.CostEstimate(
            flops=2 * 10**9, transcendentals=0, bytes_accessed=12 * 10**6
        ),
    )(zeven, zodd, projections, resid, proj_grads, shares)


def prelude_kernel(
    hd, q, k, v, o, inner, outer, b0, b1, b2, b3, b4, b5, b6, b7, b8,
    slabs, first_half, outer_low, projections, tile,
):
    own, width = q.shape
    chips = slabs.shape[0] // 2
    first_half[:, :width] = o[...].astype(LOW)
    first_half[:, width:] = inner[...].astype(LOW)
    outer_low[...] = outer[...].astype(LOW)
    for t, ref in enumerate((q, k, v)):
        projections[:, t * width : (t + 1) * width] = ref[...].astype(LOW)
    tile[...] = jnp.zeros_like(tile)
    for i, ref in enumerate((b0, b1, b2, b3, b4, b5, b6, b7)):
        tile[i : i + 1, :own] = ref[...].reshape(1, own)
    tile[0:1, 128 : 128 + b8.shape[0]] = b8[...].reshape(1, b8.shape[0])
    keep = lane_of(own) < hd
    for t, ref in enumerate((q, k, v)):
        cols = slice(t * 128, (t + 1) * 128)
        below = tile[:, cols]
        for d in range(2 * chips):
            z = d // 2
            if d % 2 == 0:
                part = ref[:, z * 128 : (z + 1) * 128]
            else:
                at = chips * 128 + z // 2 * 128
                part = ref[:, at : at + 128]
                if z % 2:
                    part = pltpu.roll(part, hd, 1)
                part = jnp.where(keep, part, 0.0)
            slabs[d, :16, cols] = part[:16].astype(LOW)
            slabs[d, 16:, cols] = jnp.concatenate([part[16:], below], axis=0).astype(LOW)


def prelude(weights, vectors, blks, hd):
    own, width = weights[0].shape
    ff = weights[4].shape[1]
    return pl.pallas_call(
        functools.partial(prelude_kernel, hd),
        name="prelude",
        out_shape=(
            jax.ShapeDtypeStruct((blks, own + 8, 384), LOW),
            jax.ShapeDtypeStruct((own, width + ff), LOW),
            jax.ShapeDtypeStruct(weights[5].shape, LOW),
            jax.ShapeDtypeStruct((own, 3 * width), LOW),
        ),
        in_specs=[spec(pltpu.VMEM)] * 15,
        out_specs=(spec(pltpu.VMEM),) * 4,
        scratch_shapes=[pltpu.VMEM((8, 384), F32)],
        cost_estimate=pl.CostEstimate(flops=10**6, transcendentals=0, bytes_accessed=3 * 10**6),
    )(*weights, *vectors)


def fast_body(seqs, blks, heads):
    def run(
        hidden_in, query_weight, key_weight, value_weight, output_weight, inner_weight,
        outer_weight, query_bias, value_bias, output_bias, attention_gain, attention_shift,
        inner_bias, outer_bias, final_gain, final_shift, cotangent, grad_mask, cluster_order,
    ):
        rows, width = hidden_in.shape
        own = query_weight.shape[0]
        hidden_units = inner_weight.shape[1]
        length = cluster_order.shape[2]
        hd = width // heads
        chips = blks // 2
        scale = 1.0 / math.sqrt(hd)
        devices = seqs * blks
        b = lax.axis_index("blk")
        k = b // 2
        even_core = lax.rem(b, 2) == 0
        slabs, half_own, outer_own, proj_own = prelude(
            (query_weight, key_weight, value_weight, output_weight, inner_weight, outer_weight),
            (
                query_bias, value_bias, output_bias, attention_gain, attention_shift,
                outer_bias, final_gain, final_shift, inner_bias,
            ),
            blks,
            hd,
        )
        hidden_all, gathered, first_half, outer_full, projections = entry(
            hidden_in, slabs, (half_own, outer_own, proj_own), seqs, blks, 2
        )
        first_half = first_half.reshape(width, width + hidden_units)
        outer_full = outer_full.reshape(hidden_units, width)
        projections = projections.reshape(width, 3 * width)
        hidden_all = hidden_all.reshape(length, width)
        gathered = gathered.reshape((devices,) + slabs.shape[1:])
        order = cluster_order[0]
        head_first = jnp.where(even_core, 2 * k, 2 * chips + k)
        order_own = jnp.concatenate(
            [
                lax.dynamic_index_in_dim(order, head_first, 0, keepdims=False),
                lax.dynamic_index_in_dim(order, 2 * k + 1, 0, keepdims=False),
            ]
        )
        proj, cnat, cpack, vecs, bias_inner = attend(
            order_own, hidden_all, gathered, blks, hidden_units, hd, scale
        )
        ceven, codd = return_rows(cnat, cpack, 1)
        hidden_out, residual_grad, geven, godd, merged, extra = middle(
            ceven, codd, hidden_in, first_half, outer_full, vecs, bias_inner, cotangent,
            grad_mask, devices, hd,
        )
        slab = merged.shape[1:]
        gnat, gpack, summed = spread_rows(
            geven, godd, merged.reshape((seqs * chips, 2) + slab), 2
        )
        znat, zpack, grads = attend_back(
            order_own, hidden_all, proj, gnat, gpack, extra, hd, scale
        )
        pieces = 2
        zeven, zodd, proj_grads, big_grads = leave(
            znat, zpack, grads.reshape((seqs, blks) + grads.shape[1:]),
            summed.reshape(seqs, chips, pieces, slab[0] // pieces, width),
        )
        return (hidden_out,) + tuple(
            final(
                zeven, zodd, projections, residual_grad, proj_grads,
                big_grads.reshape((chips,) + slab), own, hidden_units, hd,
            )
        )

    return run


def masked_scores(left, right, left_ids, right_ids, scale):
    scores = back_product(left, right) * scale
    return jnp.where(left_ids[:, None] == right_ids[None, :], scores, -jnp.inf)


def body(
    hidden_in,
    query_weight,
    key_weight,
    value_weight,
    output_weight,
    inner_weight,
    outer_weight,
    query_bias,
    value_bias,
    output_bias,
    attention_gain,
    attention_shift,
    inner_bias,
    outer_bias,
    final_gain,
    final_shift,
    cotangent,
    grad_mask,
    cluster_order,
):
    rows = hidden_in.shape[0]
    width = hidden_in.shape[1]
    heads = cluster_order.shape[1]
    length = cluster_order.shape[2]
    scale = 1.0 / math.sqrt(width // heads)
    masters = (
        query_weight,
        key_weight,
        value_weight,
        output_weight,
        inner_weight,
        outer_weight,
        query_bias,
        value_bias,
        output_bias,
        attention_gain,
        attention_shift,
        inner_bias,
        outer_bias,
        final_gain,
        final_shift,
    )
    lowered = [master.astype(jnp.bfloat16) for master in masters]
    fetched = (
        lax.all_gather(lowered[0], ("seq", "blk"), axis=0, tiled=True),
        lax.all_gather(lowered[1], ("seq", "blk"), axis=0, tiled=True),
        lax.all_gather(lowered[2], ("seq", "blk"), axis=0, tiled=True),
        lax.all_gather(lowered[3], ("seq", "blk"), axis=0, tiled=True),
        lax.all_gather(lowered[4], ("seq", "blk"), axis=0, tiled=True),
        lax.all_gather(lowered[5], ("seq", "blk"), axis=0, tiled=True),
        lax.all_gather(lowered[6], ("seq", "blk"), axis=0, tiled=True),
        lax.all_gather(lowered[7], ("seq", "blk"), axis=0, tiled=True),
        lax.all_gather(lowered[8], ("seq", "blk"), axis=0, tiled=True),
        lax.all_gather(lowered[9], ("seq", "blk"), axis=0, tiled=True),
        lax.all_gather(lowered[10], ("seq", "blk"), axis=0, tiled=True),
        lax.all_gather(lowered[11], ("seq", "blk"), axis=0, tiled=True),
        lax.all_gather(lowered[12], ("seq", "blk"), axis=0, tiled=True),
        lax.all_gather(lowered[13], ("seq", "blk"), axis=0, tiled=True),
        lax.all_gather(lowered[14], ("seq", "blk"), axis=0, tiled=True),
    )
    query_full, key_full, value_full, output_full, inner_full, outer_full = fetched[0:6]
    vectors = [vector.astype(jnp.float32) for vector in fetched[6:15]]
    (
        bias_query,
        bias_value,
        bias_output,
        gain_first,
        shift_first,
        bias_inner,
        bias_outer,
        gain_final,
        shift_final,
    ) = vectors
    hidden = hidden_in.astype(jnp.float32)
    query_low = (
        jnp.dot(hidden_in, query_full, preferred_element_type=jnp.float32) + bias_query
    ).astype(jnp.bfloat16)
    keys_low = jnp.dot(hidden_in, key_full, preferred_element_type=jnp.float32).astype(jnp.bfloat16)
    values_low = (
        jnp.dot(hidden_in, value_full, preferred_element_type=jnp.float32) + bias_value
    ).astype(jnp.bfloat16)
    all_keys, all_values = (
        lax.all_gather(keys_low, "blk", axis=0, tiled=True),
        lax.all_gather(values_low, "blk", axis=0, tiled=True),
    )
    order = cluster_order[0]
    head_rows = jnp.broadcast_to(jnp.arange(heads, dtype=jnp.int32)[:, None], (heads, length))
    positions = jnp.broadcast_to(jnp.arange(length, dtype=jnp.int32)[None, :], (heads, length))
    inverse = jnp.zeros((heads, length), jnp.int32).at[head_rows, order].set(positions)
    key_cluster = inverse // CLUSTER
    member = lax.dynamic_slice_in_dim(key_cluster, lax.axis_index("blk") * rows, rows, 1)
    query_heads = head_major(query_low, heads)
    key_heads = head_major(all_keys, heads)
    value_heads = head_major(all_values, heads)
    head_ids = jnp.arange(heads, dtype=jnp.int32)

    def attend(index):
        scores = masked_scores(
            query_heads[index], key_heads[index], member[index], key_cluster[index], scale
        )
        peak = jnp.max(scores, axis=-1, keepdims=True)
        weights = jnp.exp(scores - peak)
        total = jnp.sum(weights, axis=-1, keepdims=True)
        probs_low = (weights / total).astype(jnp.bfloat16)
        mixed = jnp.dot(probs_low, value_heads[index], preferred_element_type=jnp.float32)
        return (mixed, (peak + jnp.log(total))[:, 0])

    mixed, logsum = lax.map(attend, head_ids)
    context_low = token_major(mixed).astype(jnp.bfloat16)
    attention_out = (
        jnp.dot(context_low, output_full, preferred_element_type=jnp.float32) + bias_output
    )
    first_norm, first_pull = jax.vjp(layer_norm, hidden + attention_out, gain_first, shift_first)
    first_low = first_norm.astype(jnp.bfloat16)
    inner_pre = jnp.dot(first_low, inner_full, preferred_element_type=jnp.float32) + bias_inner
    activated, gelu_pull = jax.vjp(exact_gelu, inner_pre)
    activated_low = activated.astype(jnp.bfloat16)
    outer_out = jnp.dot(activated_low, outer_full, preferred_element_type=jnp.float32) + bias_outer
    final_norm, final_pull = jax.vjp(layer_norm, first_norm + outer_out, gain_final, shift_final)
    hidden_out = final_norm.astype(jnp.bfloat16)
    out_grad = cotangent.astype(jnp.float32) * grad_mask.astype(jnp.float32)
    second_grad, grad_final_gain, grad_final_shift = final_pull(out_grad)
    outer_low = second_grad.astype(jnp.bfloat16)
    back_weights = (
        lax.all_gather(lowered[0], ("seq", "blk"), axis=0, tiled=True),
        lax.all_gather(lowered[1], ("seq", "blk"), axis=0, tiled=True),
        lax.all_gather(lowered[2], ("seq", "blk"), axis=0, tiled=True),
        lax.all_gather(lowered[3], ("seq", "blk"), axis=0, tiled=True),
        lax.all_gather(lowered[4], ("seq", "blk"), axis=0, tiled=True),
        lax.all_gather(lowered[5], ("seq", "blk"), axis=0, tiled=True),
    )
    grad_outer_weight = row_contract(activated_low, outer_low)
    grad_outer_bias = column_sum(outer_low)
    inner_low = gelu_pull(back_product(outer_low, back_weights[5]))[0].astype(jnp.bfloat16)
    grad_inner_weight = row_contract(first_low, inner_low)
    grad_inner_bias = column_sum(inner_low)
    first_grad = back_product(inner_low, back_weights[4]) + second_grad
    residual_grad, grad_attention_gain, grad_attention_shift = first_pull(first_grad)
    attn_low = residual_grad.astype(jnp.bfloat16)
    grad_output_weight = row_contract(context_low, attn_low)
    grad_output_bias = column_sum(attn_low)
    context_grad = back_product(attn_low, back_weights[3]).astype(jnp.bfloat16)
    grad_heads = head_major(context_grad, heads)

    def own_rows_back(index):
        scores = masked_scores(
            query_heads[index], key_heads[index], member[index], key_cluster[index], scale
        )
        probs = jnp.exp(scores - logsum[index][:, None])
        probs_low = probs.astype(jnp.bfloat16)
        grad_part = grad_heads[index]
        prob_grad = back_product(grad_part, value_heads[index])
        weighted = jnp.sum(probs * prob_grad, axis=-1, keepdims=True)
        score_low = (probs * (prob_grad - weighted)).astype(jnp.bfloat16)
        query_grad = (
            jnp.dot(score_low, key_heads[index], preferred_element_type=jnp.float32) * scale
        )
        return (probs_low, score_low, query_grad, weighted[:, 0])

    def attend_back(index):
        probs_low, score_low, query_grad, weighted = own_rows_back(index)
        key_sum = row_contract(score_low, query_heads[index]) * scale
        value_sum = row_contract(probs_low, grad_heads[index])
        return (query_grad, key_sum, value_sum)

    query_grads, key_grads, value_grads = lax.map(attend_back, head_ids)
    key_own, value_own = (
        lax.psum_scatter(token_major(key_grads), "blk", scatter_dimension=0, tiled=True),
        lax.psum_scatter(token_major(value_grads), "blk", scatter_dimension=0, tiled=True),
    )
    query_grad_low = token_major(query_grads).astype(jnp.bfloat16)
    key_grad_low = key_own.astype(jnp.bfloat16)
    value_grad_low = value_own.astype(jnp.bfloat16)
    grad_query_weight = row_contract(hidden_in, query_grad_low)
    grad_key_weight = row_contract(hidden_in, key_grad_low)
    grad_value_weight = row_contract(hidden_in, value_grad_low)
    grad_query_bias = column_sum(query_grad_low)
    grad_value_bias = column_sum(value_grad_low)
    input_grad = (
        back_product(query_grad_low, back_weights[0])
        + back_product(key_grad_low, back_weights[1])
        + back_product(value_grad_low, back_weights[2])
        + residual_grad
    )
    shares = (
        lax.psum_scatter(grad_query_weight, ("seq", "blk"), scatter_dimension=0, tiled=True),
        lax.psum_scatter(grad_key_weight, ("seq", "blk"), scatter_dimension=0, tiled=True),
        lax.psum_scatter(grad_value_weight, ("seq", "blk"), scatter_dimension=0, tiled=True),
        lax.psum_scatter(grad_output_weight, ("seq", "blk"), scatter_dimension=0, tiled=True),
        lax.psum_scatter(grad_inner_weight, ("seq", "blk"), scatter_dimension=0, tiled=True),
        lax.psum_scatter(grad_outer_weight, ("seq", "blk"), scatter_dimension=0, tiled=True),
        lax.psum_scatter(grad_query_bias, ("seq", "blk"), scatter_dimension=0, tiled=True),
        lax.psum_scatter(grad_value_bias, ("seq", "blk"), scatter_dimension=0, tiled=True),
        lax.psum_scatter(grad_output_bias, ("seq", "blk"), scatter_dimension=0, tiled=True),
        lax.psum_scatter(grad_attention_gain, ("seq", "blk"), scatter_dimension=0, tiled=True),
        lax.psum_scatter(grad_attention_shift, ("seq", "blk"), scatter_dimension=0, tiled=True),
        lax.psum_scatter(grad_inner_bias, ("seq", "blk"), scatter_dimension=0, tiled=True),
        lax.psum_scatter(grad_outer_bias, ("seq", "blk"), scatter_dimension=0, tiled=True),
        lax.psum_scatter(grad_final_gain, ("seq", "blk"), scatter_dimension=0, tiled=True),
        lax.psum_scatter(grad_final_shift, ("seq", "blk"), scatter_dimension=0, tiled=True),
    )
    return (hidden_out, input_grad) + tuple(shares)


def solution(mesh):
    placed = (
        P(("seq", "blk"), None),
        P(("seq", "blk"), None),
        P(("seq", "blk"), None),
        P(("seq", "blk"), None),
        P(("seq", "blk"), None),
        P(("seq", "blk"), None),
        P(("seq", "blk"), None),
        P(("seq", "blk")),
        P(("seq", "blk")),
        P(("seq", "blk")),
        P(("seq", "blk")),
        P(("seq", "blk")),
        P(("seq", "blk")),
        P(("seq", "blk")),
        P(("seq", "blk")),
        P(("seq", "blk")),
        P(("seq", "blk"), None),
        P(("seq", "blk"), None),
        P("seq", None, None),
    )
    seqs, blks = mesh.shape["seq"], mesh.shape["blk"]
    heads = 12
    fast = seqs == 4 and blks == 8
    return jax.shard_map(
        fast_body(seqs, blks, heads) if fast else body,
        mesh=mesh,
        in_specs=placed,
        out_specs=(
            P(("seq", "blk"), None),
            P(("seq", "blk"), None),
            P(("seq", "blk"), None),
            P(("seq", "blk"), None),
            P(("seq", "blk"), None),
            P(("seq", "blk"), None),
            P(("seq", "blk"), None),
            P(("seq", "blk"), None),
            P(("seq", "blk")),
            P(("seq", "blk")),
            P(("seq", "blk")),
            P(("seq", "blk")),
            P(("seq", "blk")),
            P(("seq", "blk")),
            P(("seq", "blk")),
            P(("seq", "blk")),
            P(("seq", "blk")),
        ),
        check_vma=False,
    )
```

```python
import functools
import math

import jax
import jax.numpy as jnp
from jax import lax
from jax.experimental import pallas as pl
from jax.experimental.pallas import tpu as pltpu
from jax.sharding import PartitionSpec as P

MESH = pl.DeviceIdType.MESH
ANY = pl.ANY
LOW = jnp.bfloat16
F32 = jnp.float32
BIG = 60 * 2**20
GROUP = 4
CLUSTER = 128


def spec(space):
    return pl.BlockSpec(memory_space=space)


def nt_dot(left, right):
    return lax.dot_general(left, right, (((1,), (1,)), ((), ())), preferred_element_type=F32)


def tn_dot(left, right):
    return lax.dot_general(left, right, (((0,), (0,)), ((), ())), preferred_element_type=F32)


def nn_dot(left, right):
    return jnp.dot(left, right, preferred_element_type=F32)


def greet(targets):
    sem = pltpu.get_barrier_semaphore()
    for target in targets:
        pl.semaphore_signal(sem, inc=1, device_id=target, device_id_type=MESH)
    pl.semaphore_wait(sem, len(targets))


def send(src, dst, send_sem, recv_sem, target):
    return pltpu.make_async_remote_copy(
        src_ref=src,
        dst_ref=dst,
        send_sem=send_sem,
        recv_sem=recv_sem,
        device_id=target,
        device_id_type=MESH,
    )


epsilon = 1e-06


def layer_norm(value, gain, shift):
    center = value - jnp.mean(value, axis=-1, keepdims=True)
    spread = jnp.mean(center * center, axis=-1, keepdims=True)
    return center * lax.rsqrt(spread + epsilon) * gain + shift


def exact_gelu(value):
    return jax.nn.gelu(value, approximate=False)


def row_contract(left, right):
    return lax.dot_general(
        left, right, (((0,), (0,)), ((), ())), preferred_element_type=jnp.float32
    )


def back_product(grad, weight):
    return lax.dot_general(
        grad, weight, (((1,), (1,)), ((), ())), preferred_element_type=jnp.float32
    )


def column_sum(value):
    return jnp.sum(value.astype(jnp.float32), axis=0)


def head_major(value, heads):
    return value.reshape(value.shape[0], heads, -1).transpose(1, 0, 2)


def token_major(value):
    return value.transpose(1, 0, 2).reshape(value.shape[1], value.shape[0] * value.shape[2])


def entry_kernel(
    seqs, blks, parts, x_ref, w_ref, a0, a1, a2, o_ref, wall_ref, f0, f1, f2,
    own_sem, ssem, rsem, wl, ws, wr, us, ur, al, zs, zr, ns, nr, ms, mr,
):
    half = blks // 2
    s = lax.axis_index("seq")
    b = lax.axis_index("blk")
    k = b // 2
    c = lax.rem(b, 2)
    mate = b + 1 - 2 * c
    left = lax.rem(b + blks - 2, blks)
    right = lax.rem(b + 2, blks)
    has_left = k > 0
    has_right = k < half - 1
    blk_peers = [{"blk": lax.rem(b + d, blks)} for d in range(1, blks)]
    seq_peers = [{"seq": lax.rem(s + d, seqs)} for d in range(1, seqs)]
    greet(blk_peers + seq_peers)

    def slab(d):
        peer = lax.rem(b + d, blks)
        return send(w_ref.at[peer], wall_ref.at[s, b], ws.at[d], wr.at[d], {"blk": peer})

    def group(d):
        return send(
            wall_ref.at[s], wall_ref.at[s], us.at[d], ur.at[d], {"seq": lax.rem(s + d, seqs)}
        )

    def piece(src, blk, p, to, way):
        return send(src, o_ref.at[blk, p], ssem.at[way, blk, p], rsem.at[blk, p], {"blk": to})

    shards = ((a0, f0), (a1, f1), (a2, f2))
    x_next = s + 1 - 2 * lax.rem(s, 2)
    y_next = s + 2 - 4 * (s // 2)
    across = 3 - s
    low_part = pl.ds(0, half // 2)
    high_part = pl.ds(half // 2, half // 2)

    def along(a, d):
        own_ref, full = shards[a]
        to = 2 * lax.rem(k + d, half) + c
        return send(own_ref, full.at[s, k, c], zs.at[a, d], zr.at[a, d], {"blk": to})

    def beside(a, way):
        full = shards[a][1]
        whole = full.at[s, :, c]
        if way == 0:
            return send(whole, whole, ns.at[a, 0], nr.at[a, 0], {"seq": x_next})
        if way == 1:
            return send(whole, whole, ns.at[a, 1], nr.at[a, 1], {"seq": y_next})
        if way == 2:
            part = full.at[y_next, low_part, c]
            return send(part, part, ns.at[a, 2], nr.at[a, 2], {"seq": x_next})
        part = full.at[x_next, high_part, c]
        return send(part, part, ns.at[a, 3], nr.at[a, 3], {"seq": y_next})

    def pair(a, i, src):
        part = shards[a][1].at[src, :, c]
        return send(part, part, ms.at[a, i], mr.at[a, i], {"blk": mate})

    for d in range(1, blks):
        slab(d).start()
    for a in range(3):
        for d in range(1, half):
            along(a, d).start()
        pltpu.make_async_copy(shards[a][0], shards[a][1].at[s, k, c], al.at[a]).start()
    own_slab = pltpu.make_async_copy(w_ref.at[b], wall_ref.at[s, b], wl)
    own_slab.start()
    for p in range(parts):
        @pl.when(has_left)
        def _():
            piece(x_ref.at[p], b, p, left, 0).start()

        @pl.when(has_right)
        def _():
            piece(x_ref.at[p], b, p, right, 1).start()
    for p in range(parts):
        piece(x_ref.at[p], b, p, mate, 2).start()
    own = pltpu.make_async_copy(x_ref, o_ref.at[b], own_sem)
    own.start()
    own_slab.wait()
    for d in range(1, blks):
        slab(d).wait_recv()
    for d in range(1, seqs):
        group(d).start()
    for a in range(3):
        pltpu.make_async_copy(shards[a][0], shards[a][1].at[s, k, c], al.at[a]).wait()
        for d in range(1, half):
            along(a, d).wait_recv()
        beside(a, 0).start()
        beside(a, 1).start()
        pair(a, 0, s).start()

    def second(a):
        beside(a, 1).wait_recv()
        beside(a, 2).start()
        pair(a, 2, y_next).start()
        beside(a, 0).wait_recv()
        beside(a, 3).start()
        pair(a, 1, x_next).start()

    def third(a):
        beside(a, 2).wait_recv()
        beside(a, 3).wait_recv()
        pair(a, 3, across).start()

    for t in range(1, half):
        for p in range(parts):
            @pl.when(k - t >= 0)
            def _():
                blk = b - 2 * t
                piece(o_ref.at[blk, p], blk, p, right, 1).wait_recv()

                @pl.when(has_right)
                def _():
                    piece(o_ref.at[blk, p], blk, p, right, 1).start()

                piece(o_ref.at[blk, p], blk, p, mate, 2).start()

            @pl.when(k + t < half)
            def _():
                blk = b + 2 * t
                piece(o_ref.at[blk, p], blk, p, left, 0).wait_recv()

                @pl.when(has_left)
                def _():
                    piece(o_ref.at[blk, p], blk, p, left, 0).start()

                piece(o_ref.at[blk, p], blk, p, mate, 2).start()

        if t == 1:
            second(0)
            second(1)
        if t == 2:
            second(2)
            third(0)
            third(1)
    third(2)
    for j in range(half):
        blk = 2 * j + 1 - c
        for p in range(parts):
            piece(o_ref.at[blk, p], blk, p, mate, 2).wait_recv()
    for j in range(half):
        blk = 2 * j + c
        for p in range(parts):
            piece(o_ref.at[blk, p], blk, p, mate, 2).wait_send()

            @pl.when(jnp.logical_and(has_right, j <= k))
            def _():
                piece(o_ref.at[blk, p], blk, p, right, 1).wait_send()

            @pl.when(jnp.logical_and(has_left, j >= k))
            def _():
                piece(o_ref.at[blk, p], blk, p, left, 0).wait_send()
    own.wait()
    for d in range(1, blks):
        slab(d).wait_send()
    for d in range(1, seqs):
        group(d).wait()
    for a in range(3):
        for i, src in enumerate((s, x_next, y_next, across)):
            pair(a, i, src).wait()
        for way in range(4):
            beside(a, way).wait_send()
        for d in range(1, half):
            along(a, d).wait_send()


def entry(hidden, slabs, shards, seqs, blks, parts):
    rows, width = hidden.shape
    dma = pltpu.SemaphoreType.DMA
    return pl.pallas_call(
        functools.partial(entry_kernel, seqs, blks, parts),
        name="entry",
        out_shape=(
            jax.ShapeDtypeStruct((blks, parts, rows // parts, width), LOW),
            jax.ShapeDtypeStruct((seqs,) + slabs.shape, LOW),
        )
        + tuple(jax.ShapeDtypeStruct((seqs, blks // 2, 2) + x.shape, LOW) for x in shards),
        in_specs=[spec(pltpu.VMEM)] * 5,
        out_specs=(spec(ANY),) * 5,
        scratch_shapes=[
            dma, dma((3, blks, parts)), dma((blks, parts)), dma,
            dma((blks,)), dma((blks,)), dma((seqs,)), dma((seqs,)),
            dma((3,)), dma((3, blks // 2)), dma((3, blks // 2)),
            dma((3, 4)), dma((3, 4)), dma((3, 4)), dma((3, 4)),
        ],
        compiler_params=pltpu.CompilerParams(collective_id=0, has_side_effects=True),
        cost_estimate=pl.CostEstimate(flops=0, transcendentals=0, bytes_accessed=200 * 10**6),
    )(hidden.reshape(parts, rows // parts, width), slabs, *shards)


def return_kernel(blks, nat_ref, pack_ref, even_ref, odd_ref, buf, lsem, ssem, rsem):
    b = lax.axis_index("blk")
    k = b // 2
    c = lax.rem(b, 2)
    greet([{"blk": lax.rem(b + d, blks)} for d in range(1, blks)])
    start_return(blks, b, k, c, nat_ref, pack_ref, even_ref, odd_ref, buf, lsem, ssem, rsem)
    finish_return(blks, b, k, c, nat_ref, pack_ref, even_ref, odd_ref, ssem, rsem)


def full_way(blks, b, d, nat_ref, even_ref, ssem, rsem, slot):
    peer = lax.rem(b + d, blks)
    return send(nat_ref.at[peer], even_ref.at[slot], ssem.at[d], rsem.at[d], {"blk": peer})


def start_return(blks, b, k, c, nat_ref, pack_ref, even_ref, odd_ref, buf, lsem, ssem, rsem):
    @pl.when(c == 0)
    def _():
        for d in range(1, blks):
            full_way(blks, b, d, nat_ref, even_ref, ssem, rsem, k).start()
        inward = pltpu.make_async_copy(nat_ref.at[b], buf, lsem)
        inward.start()
        inward.wait()
        outward = pltpu.make_async_copy(buf, even_ref.at[k], lsem)
        outward.start()
        outward.wait()

    @pl.when(c == 1)
    def _():
        for d in range(1, blks):
            full_way(blks, b, d, pack_ref, odd_ref, ssem, rsem, k).start()
        part = buf.at[pl.ds(0, pack_ref.shape[1])]
        inward = pltpu.make_async_copy(pack_ref.at[b], part, lsem)
        inward.start()
        inward.wait()
        outward = pltpu.make_async_copy(part, odd_ref.at[k], lsem)
        outward.start()
        outward.wait()


def finish_return(blks, b, k, c, nat_ref, pack_ref, even_ref, odd_ref, ssem, rsem):
    for d in range(1, blks):
        source = lax.rem(b + blks - d, blks)

        @pl.when(lax.rem(source, 2) == 0)
        def _():
            full_way(blks, b, d, nat_ref, even_ref, ssem, rsem, source // 2).wait_recv()

        @pl.when(lax.rem(source, 2) == 1)
        def _():
            full_way(blks, b, d, pack_ref, odd_ref, ssem, rsem, source // 2).wait_recv()

    @pl.when(c == 0)
    def _():
        for d in range(1, blks):
            full_way(blks, b, d, nat_ref, even_ref, ssem, rsem, k).wait_send()

    @pl.when(c == 1)
    def _():
        for d in range(1, blks):
            full_way(blks, b, d, pack_ref, odd_ref, ssem, rsem, k).wait_send()


def return_rows(nat, pack, collective_id):
    blks = nat.shape[0]
    dma = pltpu.SemaphoreType.DMA
    return pl.pallas_call(
        functools.partial(return_kernel, blks),
        name="return_rows",
        out_shape=(
            jax.ShapeDtypeStruct((blks // 2,) + nat.shape[1:], LOW),
            jax.ShapeDtypeStruct((blks // 2,) + pack.shape[1:], LOW),
        ),
        in_specs=[spec(ANY)] * 2,
        out_specs=(spec(ANY), spec(ANY)),
        scratch_shapes=[pltpu.VMEM(nat.shape[1:], LOW), dma, dma((blks,)), dma((blks,))],
        compiler_params=pltpu.CompilerParams(collective_id=collective_id, has_side_effects=True),
        cost_estimate=pl.CostEstimate(flops=0, transcendentals=0, bytes_accessed=80 * 10**6),
    )(nat, pack)


def spread_kernel(
    blks, even_ref, odd_ref, grad_ref, nat_ref, pack_ref, total_hbm,
    buf, mine, theirs, total, lsem, ssem, rsem, ml, ms, mr, tl,
):
    b = lax.axis_index("blk")
    c = lax.rem(b, 2)
    mate = b + 1 - 2 * c
    greet([{"blk": lax.rem(b + d, blks)} for d in range(1, blks)])
    swap = send(grad_ref.at[:, 1 - c], theirs, ms, mr, {"blk": mate})
    swap.start()
    load = pltpu.make_async_copy(grad_ref.at[:, c], mine, ml)
    load.start()

    def full(d, slot):
        peer = lax.rem(b + d, blks)
        return send(
            even_ref.at[peer // 2], nat_ref.at[slot], ssem.at[d], rsem.at[d], {"blk": peer}
        )

    def packed(d, slot):
        peer = lax.rem(b + d, blks)
        return send(
            odd_ref.at[peer // 2], pack_ref.at[slot], ssem.at[d], rsem.at[d], {"blk": peer}
        )

    for d in range(1, blks):
        to_even = lax.rem(b + d, 2) == 0

        @pl.when(to_even)
        def _():
            full(d, b).start()

        @pl.when(jnp.logical_not(to_even))
        def _():
            packed(d, b).start()

    load.wait()
    swap.wait()

    @pl.loop(0, total.shape[0])
    def _(o):
        total[o] = (mine[o].astype(F32) + theirs[o].astype(F32)).astype(LOW)

    store = pltpu.make_async_copy(total, total_hbm, tl)
    store.start()

    @pl.when(c == 0)
    def _():
        inward = pltpu.make_async_copy(even_ref.at[b // 2], buf, lsem)
        inward.start()
        inward.wait()
        outward = pltpu.make_async_copy(buf, nat_ref.at[b], lsem)
        outward.start()
        outward.wait()
        for d in range(1, blks):
            full(d, lax.rem(b + blks - d, blks)).wait_recv()

    @pl.when(c == 1)
    def _():
        part = buf.at[pl.ds(0, odd_ref.shape[1])]
        inward = pltpu.make_async_copy(odd_ref.at[b // 2], part, lsem)
        inward.start()
        inward.wait()
        outward = pltpu.make_async_copy(part, pack_ref.at[b], lsem)
        outward.start()
        outward.wait()
        for d in range(1, blks):
            packed(d, lax.rem(b + blks - d, blks)).wait_recv()

    for d in range(1, blks):
        to_even = lax.rem(b + d, 2) == 0

        @pl.when(to_even)
        def _():
            full(d, b).wait_send()

        @pl.when(jnp.logical_not(to_even))
        def _():
            packed(d, b).wait_send()

    store.wait()


def spread_rows(even, odd, grads, collective_id):
    blks = 2 * even.shape[0]
    half_shape = grads.shape[:1] + grads.shape[2:]
    dma = pltpu.SemaphoreType.DMA
    return pl.pallas_call(
        functools.partial(spread_kernel, blks),
        name="spread_rows",
        out_shape=(
            jax.ShapeDtypeStruct((blks,) + even.shape[1:], LOW),
            jax.ShapeDtypeStruct((blks,) + odd.shape[1:], LOW),
            jax.ShapeDtypeStruct(half_shape, LOW),
        ),
        in_specs=[spec(ANY)] * 3,
        out_specs=(spec(ANY),) * 3,
        scratch_shapes=[
            pltpu.VMEM(even.shape[1:], LOW),
            pltpu.VMEM(half_shape, LOW),
            pltpu.VMEM(half_shape, LOW),
            pltpu.VMEM(half_shape, LOW),
            dma, dma((blks,)), dma((blks,)), dma, dma, dma, dma,
        ],
        compiler_params=pltpu.CompilerParams(
            collective_id=collective_id, has_side_effects=True, vmem_limit_bytes=BIG
        ),
        cost_estimate=pl.CostEstimate(flops=0, transcendentals=0, bytes_accessed=80 * 10**6),
    )(even, odd, grads)


def exit_kernel(
    seqs, blks, nat_ref, pack_ref, grad_ref, big_ref, even_ref, odd_ref, out_ref, big_out,
    buf, stage, total, big_stage, big_total,
    lsem, ssem, rsem, us, ur, gl, gs, gr, bl, bu, bv, cl, cs, cr,
):
    s = lax.axis_index("seq")
    b = lax.axis_index("blk")
    k = b // 2
    c = lax.rem(b, 2)
    blk_peers = [{"blk": lax.rem(b + d, blks)} for d in range(1, blks)]
    seq_peers = [{"seq": lax.rem(s + d, seqs)} for d in range(1, seqs)]
    greet(blk_peers + seq_peers)

    def group(d):
        peer = lax.rem(s + d, seqs)
        return send(grad_ref.at[peer], stage.at[d], us.at[d], ur.at[d], {"seq": peer})

    def slab(d):
        peer = lax.rem(b + d, blks)
        return send(total.at[peer], out_ref.at[b], gs.at[d], gr.at[d], {"blk": peer})

    chips = blks // 2
    pieces = big_ref.shape[2]

    def big_group(p, d):
        peer = lax.rem(s + d, seqs)
        return send(
            big_ref.at[peer, :, p], big_stage.at[p, d], bu.at[p, d], bv.at[p, d], {"seq": peer}
        )

    def big_slab(p, d):
        to = lax.rem(k + d, chips)
        return send(
            big_total.at[p, to], big_out.at[k, p], cs.at[p, d], cr.at[p, d], {"blk": 2 * to + c}
        )

    def big_own(p):
        return pltpu.make_async_copy(big_ref.at[s, :, p], big_stage.at[p, 0], bl.at[p])

    for p in range(pieces):
        big_own(p).start()
    for d in range(1, seqs):
        group(d).start()
    for p in range(pieces):
        for d in range(1, seqs):
            big_group(p, d).start()
    start_return(blks, b, k, c, nat_ref, pack_ref, even_ref, odd_ref, buf, lsem, ssem, rsem)
    for d in range(1, seqs):
        group(d).wait_recv()
    for o in range(blks):
        acc = grad_ref[s, o].astype(F32)
        for d in range(1, seqs):
            acc = acc + stage[d, o].astype(F32)
        total[o] = acc.astype(LOW)
    for d in range(1, blks):
        slab(d).start()
    own = pltpu.make_async_copy(total.at[b], out_ref.at[b], gl)
    own.start()
    own.wait()
    for p in range(pieces):
        big_own(p).wait()
        for d in range(1, seqs):
            big_group(p, d).wait_recv()

        @pl.loop(0, chips)
        def _(o):
            acc = big_stage[p, 0, o].astype(F32)
            for d in range(1, seqs):
                acc = acc + big_stage[p, d, o].astype(F32)
            big_total[p, o] = acc.astype(LOW)

        for d in range(1, chips):
            big_slab(p, d).start()
        keep = pltpu.make_async_copy(big_total.at[p, k], big_out.at[k, p], cl.at[p])
        keep.start()
        keep.wait()
    finish_return(blks, b, k, c, nat_ref, pack_ref, even_ref, odd_ref, ssem, rsem)
    for d in range(1, blks):
        slab(d).wait()
    for d in range(1, seqs):
        group(d).wait_send()
    for p in range(pieces):
        for d in range(1, chips):
            big_slab(p, d).wait()
        for d in range(1, seqs):
            big_group(p, d).wait_send()


def leave(nat, pack, grads, big):
    blks = nat.shape[0]
    seqs = grads.shape[0]
    chips, pieces = big.shape[1:3]
    dma = pltpu.SemaphoreType.DMA
    return pl.pallas_call(
        functools.partial(exit_kernel, seqs, blks),
        name="leave",
        out_shape=(
            jax.ShapeDtypeStruct((blks // 2,) + nat.shape[1:], LOW),
            jax.ShapeDtypeStruct((blks // 2,) + pack.shape[1:], LOW),
            jax.ShapeDtypeStruct(grads.shape[1:], LOW),
            jax.ShapeDtypeStruct(big.shape[1:], LOW),
        ),
        in_specs=[spec(ANY), spec(ANY), spec(pltpu.VMEM), spec(ANY)],
        out_specs=(spec(ANY),) * 4,
        scratch_shapes=[
            pltpu.VMEM(nat.shape[1:], LOW),
            pltpu.VMEM(grads.shape, LOW),
            pltpu.VMEM(grads.shape[1:], LOW),
            pltpu.VMEM((pieces, seqs, chips) + big.shape[3:], LOW),
            pltpu.VMEM((pieces, chips) + big.shape[3:], LOW),
            dma, dma((blks,)), dma((blks,)), dma((seqs,)), dma((seqs,)),
            dma, dma((blks,)), dma((blks,)),
            dma((pieces,)), dma((pieces, seqs)), dma((pieces, seqs)),
            dma((pieces,)), dma((pieces, chips)), dma((pieces, chips)),
        ],
        compiler_params=pltpu.CompilerParams(
            collective_id=3, has_side_effects=True, vmem_limit_bytes=BIG
        ),
        cost_estimate=pl.CostEstimate(flops=0, transcendentals=0, bytes_accessed=200 * 10**6),
    )(nat, pack, grads, big)


def owner_facts(hd, chips):
    b = lax.axis_index("blk")
    k = b // 2
    odd = lax.rem(b, 2)
    first = jnp.where(odd == 0, 2 * hd * k, (2 * chips + k) * hd)
    return 2 - odd, first, (2 - odd) * hd


def lane_of(rows):
    return lax.broadcasted_iota(jnp.int32, (rows, 128), 1)


def low_lanes(value, slot, hd):
    lane = lane_of(value.shape[0])
    keep = jnp.logical_and(lane >= slot * hd, lane < (slot + 1) * hd)
    return jnp.where(keep, value, 0.0).astype(LOW)


def part_of(u, t):
    return pl.ds(u * 512 + t, 128, stride=4)


def row_part(ref, u, t):
    return ref[part_of(u, t), :]


def column_softmax(scores):
    weights = jnp.exp(scores - jnp.max(scores, axis=0, keepdims=True))
    return weights * (1.0 / jnp.sum(weights, axis=0, keepdims=True))


def attend_kernel(
    hd, scale, order, hid_hbm, gathered, proj_hbm, nat, pack, vecs, bias_inner,
    rows4, take, take_b, mix, mix_b, back, wide_weight, weight, hid, proj, in_sems, out_sem,
):
    length, width = hid.shape
    blks, step, _ = nat.shape
    devices = gathered.shape[0]
    own_rows = width // devices
    per = bias_inner.shape[1] // devices
    heads_here, first, _ = owner_facts(hd, blks // 2)

    def fetch(i):
        part = pl.ds(pl.multiple_of(i * step, step), step)
        return pltpu.make_async_copy(hid_hbm.at[part], hid.at[part], in_sems.at[i])

    for i in range(length // step):
        fetch(i).start()
    for i in range(devices):
        slab = gathered[i].astype(F32)
        wide_weight[i * own_rows : (i + 1) * own_rows, :] = slab[:own_rows, :]
        vecs[:, i * own_rows : (i + 1) * own_rows] = slab[own_rows:, :own_rows]
        bias_inner[0:1, i * per : (i + 1) * per] = slab[own_rows : own_rows + 1, 128 : 128 + per]
    weight[...] = wide_weight[...].astype(LOW)
    tile = vecs[:, pl.ds(pl.multiple_of(first // 128 * 128, 128), 128)]
    tile = jnp.where(lax.rem(first, 128) == 0, tile, pltpu.roll(tile, 64, 1))
    bias = jnp.concatenate([tile[0:1], jnp.zeros((1, 128), F32), tile[1:2]], axis=1)

    @pl.loop(0, length // step)
    def _(i):
        at = pl.multiple_of(i * step, step)
        fetch(i).wait()
        low = (nn_dot(hid[pl.ds(at, step), :], weight[...]) + bias).astype(LOW)
        proj[pl.ds(at, step), :] = low
        wide = low.astype(F32)
        for t in range(3):
            rows4[pl.ds(4 * at + t, step, stride=4), :] = wide[:, t * 128 : (t + 1) * 128]

    store = pltpu.make_async_copy(proj, proj_hbm, out_sem)
    store.start()
    span = GROUP * 128

    def gather(buf, base):
        for j in range(span):
            buf[4 * j : 4 * j + 4, :] = rows4[pl.ds(pl.multiple_of(4 * order[base + j], 4), 4), :]

    def attend_group(slot, buf, out):
        for u in range(GROUP):
            own = pl.ds(u * 128, 128)
            query = low_lanes(row_part(buf, u, 0) * scale, slot, hd)
            probs = column_softmax(nt_dot(row_part(buf, u, 1).astype(LOW), query))
            out[own, :] = tn_dot(probs.astype(LOW), row_part(buf, u, 2).astype(LOW))

    def scatter(slot, out, base):
        for j in range(span):
            back[pl.ds(slot * length + order[base + j], 1), :] = out[pl.ds(j, 1), :]

    @pl.loop(0, heads_here)
    def _(slot):
        begin = slot * length
        gather(take, begin)

        @pl.loop(0, length // (2 * span))
        def _(i):
            base = begin + 2 * i * span
            gather(take_b, base + span)
            attend_group(slot, take, mix)
            scatter(slot, mix, base)
            gather(take, jnp.minimum(base + 2 * span, begin + length - span))
            attend_group(slot, take_b, mix_b)
            scatter(slot, mix_b, base + span)

    lane = lane_of(step)

    @pl.when(heads_here == 2)
    def _():
        @pl.loop(0, length // step)
        def _(i):
            at = pl.multiple_of(i * step, step)
            nat[i] = jnp.where(
                lane < hd, back[pl.ds(at, step), :], back[pl.ds(length + at, step), :]
            ).astype(LOW)

    half = step // 2

    @pl.when(heads_here == 1)
    def _():
        @pl.loop(0, length // step)
        def _(i):
            at = pl.multiple_of(i * step, step)
            upper = pltpu.roll(back[pl.ds(at + half, half), :], hd, 1)
            pack[i] = jnp.where(lane[:half] < hd, back[pl.ds(at, half), :], upper).astype(LOW)

    store.wait()


def attend(order, hid, gathered, blks, ff, hd, scale):
    length, width = hid.shape
    step = length // blks
    return pl.pallas_call(
        functools.partial(attend_kernel, hd, scale),
        name="attend",
        out_shape=(
            jax.ShapeDtypeStruct((length, 384), LOW),
            jax.ShapeDtypeStruct((blks, step, 128), LOW),
            jax.ShapeDtypeStruct((blks, step // 2, 128), LOW),
            jax.ShapeDtypeStruct((8, width), F32),
            jax.ShapeDtypeStruct((8, ff), F32),
        ),
        in_specs=[spec(pltpu.SMEM), spec(ANY), spec(pltpu.VMEM)],
        out_specs=(spec(ANY),) + (spec(pltpu.VMEM),) * 4,
        scratch_shapes=[
            pltpu.VMEM((4 * length, 128), F32),
            pltpu.VMEM((GROUP * 512, 128), F32),
            pltpu.VMEM((GROUP * 512, 128), F32),
            pltpu.VMEM((GROUP * 128, 128), F32),
            pltpu.VMEM((GROUP * 128, 128), F32),
            pltpu.VMEM((2 * length, 128), F32),
            pltpu.VMEM((width, 384), F32),
            pltpu.VMEM((width, 384), LOW),
            pltpu.VMEM((length, width), LOW),
            pltpu.VMEM((length, 384), LOW),
            pltpu.SemaphoreType.DMA((blks,)),
            pltpu.SemaphoreType.DMA,
        ],
        compiler_params=pltpu.CompilerParams(vmem_limit_bytes=BIG),
        cost_estimate=pl.CostEstimate(
            flops=5 * 10**9, transcendentals=0, bytes_accessed=100 * 10**6
        ),
    )(order, hid, gathered)


def attend_back_kernel(
    hd, scale, order, hidden_hbm, proj, gnat, gpack, extra, znat_hbm, zpack_hbm, slabs,
    rows4, take, take_b, out4, out4_b, back4, hid, wide_grad,
    znat, zpack, sem, nat_sems, pack_sems,
):
    length = proj.shape[0]
    step = gnat.shape[1]
    half = step // 2
    heads_here, first_col, limit = owner_facts(hd, gnat.shape[0] // 2)
    fetch = pltpu.make_async_copy(hidden_hbm, hid, sem)
    fetch.start()

    @pl.loop(0, length // step)
    def _(i):
        at = pl.multiple_of(i * step, step)
        wide = proj[pl.ds(at, step), :].astype(F32)
        for t in range(3):
            rows4[pl.ds(4 * at + t, step, stride=4), :] = wide[:, t * 128 : (t + 1) * 128]

        @pl.when(heads_here == 2)
        def _():
            rows4[pl.ds(4 * at + 3, step, stride=4), :] = gnat[i].astype(F32)

        @pl.when(heads_here == 1)
        def _():
            pair = gpack[i].astype(F32)
            rows4[pl.ds(4 * at + 3, half, stride=4), :] = pair
            rows4[pl.ds(4 * (at + half) + 3, half, stride=4), :] = pltpu.roll(pair, hd, 1)

    span = GROUP * 128

    def gather(buf, base):
        for j in range(span):
            buf[4 * j : 4 * j + 4, :] = rows4[pl.ds(pl.multiple_of(order[base + j], 4), 4), :]

    def attend_group(slot, buf, out):
        for u in range(GROUP):
            own = pl.ds(u * 128, 128)
            query = low_lanes(row_part(buf, u, 0) * scale, slot, hd)
            grad = low_lanes(row_part(buf, u, 3), slot, hd)
            keys = row_part(buf, u, 1).astype(LOW)
            probs = column_softmax(nt_dot(keys, query))
            prob_grad = nt_dot(row_part(buf, u, 2).astype(LOW), grad)
            shift = jnp.sum(probs * prob_grad, axis=0, keepdims=True)
            score_low = (probs * (prob_grad - shift)).astype(LOW)
            out[part_of(u, 0), :] = tn_dot(score_low, keys) * scale
            out[part_of(u, 1), :] = nn_dot(score_low, query)
            out[part_of(u, 2), :] = nn_dot(probs.astype(LOW), grad)

    def scatter(slot, out, base):
        back_slot = back4.at[pl.ds(pl.multiple_of(4 * slot * length, 4 * length), 4 * length), :]
        for j in range(span):
            at = pl.multiple_of(order[base + j], 4)
            back_slot[pl.ds(at, 4), :] = out[4 * j : 4 * j + 4, :]

    @pl.loop(0, heads_here)
    def _(slot):
        begin = slot * length
        gather(take, begin)

        @pl.loop(0, length // (2 * span))
        def _(i):
            base = begin + 2 * i * span
            gather(take_b, base + span)
            attend_group(slot, take, out4)
            scatter(slot, out4, base)
            gather(take, jnp.minimum(base + 2 * span, begin + length - span))
            attend_group(slot, take_b, out4_b)
            scatter(slot, out4_b, base + span)

    lane = lane_of(step)
    fetch.wait()
    wide_grad[...] = jnp.zeros_like(wide_grad)
    zero = jnp.zeros((1, 384), F32)

    def put_nat(i):
        return pltpu.make_async_copy(znat.at[i], znat_hbm.at[i], nat_sems.at[i])

    def put_pack(i):
        return pltpu.make_async_copy(zpack.at[i], zpack_hbm.at[i], pack_sems.at[i])

    def settle(i, sums):
        at = pl.multiple_of(i * step, step)
        parts = []
        for t in range(3):
            cols = pl.ds(t * 128, 128)
            first = back4[pl.ds(4 * at + t, step, stride=4), :]
            second = back4[pl.ds(4 * (length + at) + t, step, stride=4), :]
            second = jnp.where(heads_here == 2, second, jnp.zeros_like(second))
            low = jnp.where(lane < hd, first, second).astype(LOW)
            znat[i, :, cols] = low
            wide = low.astype(F32)
            parts.append(jnp.sum(wide, axis=0, keepdims=True))
            zpack[i, :, cols] = (wide[:half] + pltpu.roll(wide[half:], hd, 1)).astype(LOW)
        put_nat(i).start()
        put_pack(i).start()
        wide_grad[...] += tn_dot(hid[pl.ds(at, step), :], znat[i])
        return sums + jnp.concatenate(parts, axis=1)

    sums = lax.fori_loop(0, length // step, settle, zero)
    devices = slabs.shape[0]
    own = hid.shape[1] // devices
    lane8 = lane_of(8)
    row8 = lax.broadcasted_iota(jnp.int32, (8, 128), 0)
    q_row = jnp.broadcast_to(sums[:, :128], (8, 128))
    v_row = jnp.broadcast_to(sums[:, 256:], (8, 128))
    for i in range(devices):
        begin = i * own - first_col
        q_lane = lane8 + begin
        v_lane = q_lane - 64
        q_part = pltpu.roll(q_row, lax.rem(4096 - begin, 128), 1)
        v_part = pltpu.roll(v_row, lax.rem(4096 - begin + 64, 128), 1)
        q_ok = (lane8 < own) & (q_lane >= 0) & (q_lane < limit)
        v_ok = (lane8 >= 64) & (lane8 < 64 + own) & (v_lane >= 0) & (v_lane < limit)
        line = jnp.where(q_ok, q_part, jnp.where(v_ok, v_part, 0.0))
        tile = jnp.where(row8 == 0, line, extra[i])
        tail = jnp.concatenate([tile, jnp.zeros((8, 256), F32)], axis=1)
        at = i * own
        slabs[i, : own - 8, :] = wide_grad[at : at + own - 8, :].astype(LOW)
        slabs[i, own - 8 :, :] = jnp.concatenate(
            [wide_grad[at + own - 8 : at + own, :], tail], axis=0
        ).astype(LOW)
    for i in range(length // step):
        put_nat(i).wait()
        put_pack(i).wait()


def attend_back(order, hidden_all, proj, gnat, gpack, extra, hd, scale):
    order = 4 * order
    length = proj.shape[0]
    blks, step, _ = gnat.shape
    devices = extra.shape[0]
    width = hidden_all.shape[1]
    return pl.pallas_call(
        functools.partial(attend_back_kernel, hd, scale),
        name="attend_back",
        out_shape=(
            jax.ShapeDtypeStruct((blks, step, 384), LOW),
            jax.ShapeDtypeStruct((blks, step // 2, 384), LOW),
            jax.ShapeDtypeStruct((devices, width // devices + 8, 384), LOW),
        ),
        in_specs=[spec(pltpu.SMEM), spec(ANY)] + [spec(pltpu.VMEM)] * 4,
        out_specs=(spec(ANY), spec(ANY), spec(pltpu.VMEM)),
        scratch_shapes=[
            pltpu.VMEM((4 * length, 128), F32),
            pltpu.VMEM((GROUP * 512, 128), F32),
            pltpu.VMEM((GROUP * 512, 128), F32),
            pltpu.VMEM((GROUP * 512, 128), F32),
            pltpu.VMEM((GROUP * 512, 128), F32),
            pltpu.VMEM((8 * length, 128), F32),
            pltpu.VMEM(hidden_all.shape, LOW),
            pltpu.VMEM((width, 384), F32),
            pltpu.VMEM((blks, step, 384), LOW),
            pltpu.VMEM((blks, step // 2, 384), LOW),
            pltpu.SemaphoreType.DMA,
            pltpu.SemaphoreType.DMA((blks,)),
            pltpu.SemaphoreType.DMA((blks,)),
        ],
        compiler_params=pltpu.CompilerParams(vmem_limit_bytes=BIG),
        cost_estimate=pl.CostEstimate(
            flops=8 * 10**9, transcendentals=0, bytes_accessed=120 * 10**6
        ),
    )(order, hidden_all, proj, gnat, gpack, extra)


def middle_kernel(
    hd, ceven, codd, hidden, first_hbm, outer_hbm, vecs, bias_inner, cot, mask,
    hout, resid, geven, godd, merged_hbm, extra,
    wa, wb, ctx, act, slope, ilow, first, flow, olow, unit, acc, hid_low, sums, inner_sums, merged, sems,
):
    rows, width = hidden.shape
    ff = outer_hbm.shape[0]
    chips = ceven.shape[0]
    get_out = pltpu.make_async_copy(
        first_hbm.at[:, pl.ds(0, width)], wa.at[:, pl.ds(0, width)], sems.at[0]
    )
    get_in = pltpu.make_async_copy(
        first_hbm.at[:, pl.ds(width, ff)], wa.at[:, pl.ds(width, ff)], sems.at[1]
    )
    get_outer = pltpu.make_async_copy(outer_hbm, wb, sems.at[2])
    get_out.start()
    get_in.start()
    get_outer.start()
    half = rows // 2
    lane = lane_of(half)
    low_half = lane < hd
    for z in range(chips):
        ctx[:, z * 128 : (z + 1) * 128] = ceven[z]
    for z in range(0, chips, 2):
        here = codd[z].astype(F32)
        there = codd[z + 1].astype(F32)
        at = chips * 128 + z * 64
        ctx[:half, at : at + 128] = jnp.where(low_half, here, pltpu.roll(there, hd, 1)).astype(LOW)
        ctx[half:, at : at + 128] = jnp.where(low_half, pltpu.roll(here, hd, 1), there).astype(LOW)
    sums[...] = jnp.zeros_like(sums)
    wide = 768
    tile = 128

    def add_rows(row, value):
        sums[row : row + 1, :] += jnp.sum(value, axis=0, keepdims=True)

    get_out.wait()

    @pl.loop(0, width // wide)
    def _(n):
        at = pl.multiple_of(n * wide, wide)
        acc[:, pl.ds(at, wide)] = nn_dot(ctx[...], wa[:, pl.ds(at, wide)])

    @pl.loop(0, rows // tile)
    def _(i):
        own = pl.ds(pl.multiple_of(i * tile, tile), tile)
        value = hidden[own, :].astype(F32) + acc[own, :] + vecs[2:3, :]
        center = value - jnp.mean(value, axis=-1, keepdims=True)
        spread = jnp.mean(center * center, axis=-1, keepdims=True)
        inv = lax.rsqrt(spread + epsilon)
        norm = center * inv * vecs[3:4, :] + vecs[4:5, :]
        first[own, :] = norm
        flow[own, :] = norm.astype(LOW)
        unit[own, :] = center * inv
        resid[own, 0:128] = jnp.broadcast_to(inv, (tile, 128))

    get_in.wait()

    @pl.loop(0, ff // wide)
    def _(j):
        at = pl.multiple_of(j * wide, wide)
        cols = pl.ds(at, wide)
        pre = nn_dot(flow[...], wa[:, pl.ds(width + at, wide)]) + bias_inner[0:1, cols]
        gate = 0.5 + 0.5 * lax.erf(pre * (0.5**0.5))
        act[:, cols] = (pre * gate).astype(LOW)
        slope[:, cols] = gate + pre * jnp.exp(-0.5 * pre * pre) * (0.5 / math.pi) ** 0.5

    get_outer.wait()

    @pl.loop(0, width // wide)
    def _(n):
        at = pl.multiple_of(n * wide, wide)
        acc[:, pl.ds(at, wide)] = nn_dot(act[...], wb[:, pl.ds(at, wide)])

    @pl.loop(0, rows // tile)
    def _(i):
        own = pl.ds(pl.multiple_of(i * tile, tile), tile)
        value = first[own, :] + acc[own, :] + vecs[5:6, :]
        center = value - jnp.mean(value, axis=-1, keepdims=True)
        spread = jnp.mean(center * center, axis=-1, keepdims=True)
        inv = lax.rsqrt(spread + epsilon)
        norm = center * inv
        hout[own, :] = (norm * vecs[6:7, :] + vecs[7:8, :]).astype(LOW)
        out_grad = cot[own, :].astype(F32) * mask[own, :].astype(F32)
        pull = out_grad * vecs[6:7, :]
        pull = pull - jnp.mean(pull, axis=-1, keepdims=True) - norm * jnp.mean(
            pull * norm, axis=-1, keepdims=True
        )
        grad = pull * inv
        low = grad.astype(LOW)
        first[own, :] = grad
        olow[own, :] = low
        add_rows(4, low.astype(F32))
        add_rows(5, out_grad * norm)
        add_rows(6, out_grad)

    @pl.loop(0, ff // wide)
    def _(j):
        cols = pl.ds(pl.multiple_of(j * wide, wide), wide)
        low = (nt_dot(olow[...], wb[cols, :]) * slope[:, cols]).astype(LOW)
        ilow[:, cols] = low
        inner_sums[0:1, cols] = jnp.sum(low.astype(F32), axis=0, keepdims=True)

    @pl.loop(0, width // wide)
    def _(n):
        at = pl.multiple_of(n * wide, wide)
        acc[:, pl.ds(at, wide)] = nt_dot(ilow[...], wa[pl.ds(at, wide), width:])

    @pl.loop(0, rows // tile)
    def _(i):
        own = pl.ds(pl.multiple_of(i * tile, tile), tile)
        grad = acc[own, :] + first[own, :]
        norm = unit[own, :]
        inv = resid[own, 0:1]
        pull = grad * vecs[3:4, :]
        pull = pull - jnp.mean(pull, axis=-1, keepdims=True) - norm * jnp.mean(
            pull * norm, axis=-1, keepdims=True
        )
        back = pull * inv
        low = back.astype(LOW)
        resid[own, :] = back
        hid_low[own, :] = low
        add_rows(1, low.astype(F32))
        add_rows(2, grad * norm)
        add_rows(3, grad)

    @pl.loop(0, width // wide)
    def _(n):
        at = pl.multiple_of(n * wide, wide)
        acc[:, pl.ds(at, wide)] = nt_dot(hid_low[...], wa[pl.ds(at, wide), :width])

    for z in range(chips):
        geven[z] = acc[:, z * 128 : (z + 1) * 128].astype(LOW)
    for z in range(0, chips, 2):
        at = chips * 128 + z * 64
        top = acc[:half, at : at + 128]
        bottom = acc[half:, at : at + 128]
        godd[z] = jnp.where(low_half, top, pltpu.roll(bottom, hd, 1)).astype(LOW)
        godd[z + 1] = jnp.where(low_half, pltpu.roll(top, hd, 1), bottom).astype(LOW)

    devices = merged.shape[0]
    own_rows = width // devices
    outer_rows = ff // devices
    block = 384
    per = block // outer_rows

    @pl.loop(0, ff // block)
    def _(j):
        part = tn_dot(act[:, pl.ds(pl.multiple_of(j * block, block), block)], olow[...])
        for i in range(per):
            merged[j * per + i, :outer_rows, :] = part[
                i * outer_rows : (i + 1) * outer_rows, :
            ].astype(LOW)

    folds = ff // width
    many = block // own_rows
    size = merged.shape[1]
    put_outer = pltpu.make_async_copy(
        merged.at[:, pl.ds(0, outer_rows)], merged_hbm.at[:, pl.ds(0, outer_rows)], sems.at[3]
    )
    put_outer.start()

    def put_rest(m):
        part = (pl.ds(m * many, many), pl.ds(outer_rows, size - outer_rows))
        return pltpu.make_async_copy(merged.at[part], merged_hbm.at[part], sems.at[4 + m])

    for m in range(width // block):
        cols = slice(m * block, (m + 1) * block)
        for h in range(0, folds, 2):
            left = tn_dot(flow[:, cols], ilow[:, h * width : (h + 1) * width])
            right = tn_dot(flow[:, cols], ilow[:, (h + 1) * width : (h + 2) * width])
            at = outer_rows + h * own_rows
            for i in range(many):
                for r in range(0, own_rows, 8):
                    base = i * own_rows + r
                    merged[m * many + i, at + 2 * r : at + 2 * r + 16, :] = jnp.concatenate(
                        [left[base : base + 8, :], right[base : base + 8, :]], axis=0
                    ).astype(LOW)
        part = tn_dot(ctx[:, cols], hid_low[...])
        at = outer_rows + folds * own_rows
        for i in range(many):
            base = i * own_rows
            merged[m * many + i, at : at + 16, :] = part[base : base + 16, :].astype(LOW)
            merged[m * many + i, at + 16 : at + 32, :] = jnp.concatenate(
                [part[base + 16 : base + 24, :], jnp.zeros((8, width), F32)], axis=0
            ).astype(LOW)
        put_rest(m).start()

    row8 = lax.broadcasted_iota(jnp.int32, (8, 128), 0)
    for i in range(devices):
        piece = sums[:, i * own_rows : (i + 1) * own_rows]
        piece = jnp.concatenate([piece, jnp.zeros((8, 128 - own_rows), F32)], axis=1)
        inner = inner_sums[0:1, i * outer_rows : (i + 1) * outer_rows]
        inner = jnp.concatenate([inner, jnp.zeros((1, 128 - outer_rows), F32)], axis=1)
        extra[i] = jnp.where(row8 == 7, jnp.broadcast_to(inner, (8, 128)), piece)
    put_outer.wait()
    for m in range(width // block):
        put_rest(m).wait()


def middle(ceven, codd, hidden, first_half, outer_full, vecs, bias_inner, cot, mask, devices, hd):
    rows, width = hidden.shape
    ff = outer_full.shape[0]
    slab = ff // devices + (ff // width + 1) * (width // devices) + 8
    wide_low = pltpu.VMEM((rows, width), LOW)
    wide_f32 = pltpu.VMEM((rows, width), F32)
    return pl.pallas_call(
        functools.partial(middle_kernel, hd),
        name="middle",
        out_shape=(
            jax.ShapeDtypeStruct((rows, width), LOW),
            jax.ShapeDtypeStruct((rows, width), F32),
            jax.ShapeDtypeStruct(ceven.shape, LOW),
            jax.ShapeDtypeStruct(codd.shape, LOW),
            jax.ShapeDtypeStruct((devices, slab, width), LOW),
            jax.ShapeDtypeStruct((devices, 8, 128), F32),
        ),
        in_specs=[spec(pltpu.VMEM)] * 3 + [spec(ANY)] * 2 + [spec(pltpu.VMEM)] * 4,
        out_specs=(spec(pltpu.VMEM),) * 4 + (spec(ANY), spec(pltpu.VMEM)),
        scratch_shapes=[
            pltpu.VMEM(first_half.shape, LOW),
            pltpu.VMEM(outer_full.shape, LOW),
            wide_low,
            pltpu.VMEM((rows, ff), LOW),
            pltpu.VMEM((rows, ff), F32),
            pltpu.VMEM((rows, ff), LOW),
            wide_f32, wide_low, wide_low, wide_f32, wide_f32, wide_low,
            pltpu.VMEM((8, width), F32),
            pltpu.VMEM((8, ff), F32),
            pltpu.VMEM((devices, slab, width), LOW),
            pltpu.SemaphoreType.DMA((4 + width // 384,)),
        ],
        compiler_params=pltpu.CompilerParams(vmem_limit_bytes=BIG),
        cost_estimate=pl.CostEstimate(
            flops=17 * 10**9, transcendentals=0, bytes_accessed=40 * 10**6
        ),
    )(ceven, codd, hidden, first_half, outer_full, vecs, bias_inner, cot, mask)


def final_kernel(
    hd, zeven, zodd, proj_hbm, resid, proj_grads, shares,
    out, gq, gk, gv, go, gi, gu, g0, g1, g2, g3, g4, g5, g6, g7, g8, wp, triple, sem,
):
    rows, width = resid.shape
    chips = zeven.shape[0]
    fetch = pltpu.make_async_copy(proj_hbm, wp, sem)
    fetch.start()
    half = rows // 2
    low_half = lane_of(half) < hd
    for t in range(3):
        cols = slice(t * 128, (t + 1) * 128)
        for z in range(chips):
            at = t * width + z * 128
            triple[:, at : at + 128] = zeven[z, :, cols]
        for z in range(0, chips, 2):
            at = t * width + chips * 128 + z * 64
            here = zodd[z, :, cols].astype(F32)
            there = zodd[z + 1, :, cols].astype(F32)
            triple[:half, at : at + 128] = jnp.where(
                low_half, here, pltpu.roll(there, hd, 1)
            ).astype(LOW)
            triple[half:, at : at + 128] = jnp.where(
                low_half, pltpu.roll(here, hd, 1), there
            ).astype(LOW)
    own = gq.shape[0]
    keep = lane_of(own) < hd
    for t, ref in enumerate((gq, gk, gv)):
        cols = slice(t * 128, (t + 1) * 128)
        for z in range(chips):
            ref[:, z * 128 : (z + 1) * 128] = proj_grads[2 * z, :, cols].astype(F32)[:own]
        for z in range(0, chips, 2):
            here = proj_grads[2 * z + 1, :, cols].astype(F32)[:own]
            there = proj_grads[2 * z + 3, :, cols].astype(F32)[:own]
            at = chips * 128 + z * 64
            ref[:, at : at + 128] = jnp.where(keep, here, pltpu.roll(there, hd, 1))
    ff = gi.shape[1]
    outer_rows = gu.shape[0]
    folds = ff // width

    def share(at, size):
        total = shares[0, at : at + size, :].astype(F32)
        for z in range(1, chips):
            total = total + shares[z, at : at + size, :].astype(F32)
        return total

    for r in range(0, outer_rows, 16):
        gu[r : r + 16, :] = share(r, 16)
    for h in range(0, folds, 2):
        at = outer_rows + h * own
        for r in range(0, own, 8):
            pair = share(at + 2 * r, 16)
            gi[r : r + 8, h * width : (h + 1) * width] = pair[:8]
            gi[r : r + 8, (h + 1) * width : (h + 2) * width] = pair[8:]
    at = outer_rows + folds * own
    go[...] = share(at, own + 8)[:own]
    total = proj_grads[0, :, :128].astype(F32)[own:]
    for d in range(1, 2 * chips):
        total = total + proj_grads[d, :, :128].astype(F32)[own:]
    g0[...] = total[0, :own]
    g1[...] = total[0, 64 : 64 + own]
    for v, ref in enumerate((g2, g3, g4)):
        ref[...] = total[1 + v, :own]
    g5[...] = total[7, : g5.shape[0]]
    for v, ref in enumerate((g6, g7, g8)):
        ref[...] = total[4 + v, :own]
    fetch.wait()
    wide = 256

    @pl.loop(0, width // wide)
    def _(n):
        at = pl.multiple_of(n * wide, wide)
        cols = pl.ds(at, wide)
        out[:, cols] = nt_dot(triple[...], wp[pl.ds(at, wide), :]) + resid[:, cols]


def final(zeven, zodd, projections, resid, proj_grads, shares, own, ff, hd):
    rows, width = resid.shape
    mats = [(rows, width)] + [(own, width)] * 4 + [(own, ff), (ff * own // width, width)]
    vectors = [(own,)] * 5 + [(ff * own // width,)] + [(own,)] * 3
    return pl.pallas_call(
        functools.partial(final_kernel, hd),
        name="final",
        out_shape=tuple(jax.ShapeDtypeStruct(shape, F32) for shape in mats + vectors),
        in_specs=[spec(pltpu.VMEM)] * 2 + [spec(ANY)] + [spec(pltpu.VMEM)] * 3,
        out_specs=(spec(pltpu.VMEM),) * 16,
        scratch_shapes=[
            pltpu.VMEM(projections.shape, LOW),
            pltpu.VMEM((rows, 3 * width), LOW),
            pltpu.SemaphoreType.DMA,
        ],
        compiler_params=pltpu.CompilerParams(vmem_limit_bytes=BIG),
        cost_estimate=pl.CostEstimate(
            flops=2 * 10**9, transcendentals=0, bytes_accessed=12 * 10**6
        ),
    )(zeven, zodd, projections, resid, proj_grads, shares)


def prelude_kernel(
    hd, q, k, v, o, inner, outer, b0, b1, b2, b3, b4, b5, b6, b7, b8,
    slabs, first_half, outer_low, projections, tile,
):
    own, width = q.shape
    chips = slabs.shape[0] // 2
    first_half[:, :width] = o[...].astype(LOW)
    first_half[:, width:] = inner[...].astype(LOW)
    outer_low[...] = outer[...].astype(LOW)
    for t, ref in enumerate((q, k, v)):
        projections[:, t * width : (t + 1) * width] = ref[...].astype(LOW)
    tile[...] = jnp.zeros_like(tile)
    for i, ref in enumerate((b0, b1, b2, b3, b4, b5, b6, b7)):
        tile[i : i + 1, :own] = ref[...].reshape(1, own)
    tile[0:1, 128 : 128 + b8.shape[0]] = b8[...].reshape(1, b8.shape[0])
    keep = lane_of(own) < hd
    for t, ref in enumerate((q, k, v)):
        cols = slice(t * 128, (t + 1) * 128)
        below = tile[:, cols]
        for d in range(2 * chips):
            z = d // 2
            if d % 2 == 0:
                part = ref[:, z * 128 : (z + 1) * 128]
            else:
                at = chips * 128 + z // 2 * 128
                part = ref[:, at : at + 128]
                if z % 2:
                    part = pltpu.roll(part, hd, 1)
                part = jnp.where(keep, part, 0.0)
            slabs[d, :16, cols] = part[:16].astype(LOW)
            slabs[d, 16:, cols] = jnp.concatenate([part[16:], below], axis=0).astype(LOW)


def prelude(weights, vectors, blks, hd):
    own, width = weights[0].shape
    ff = weights[4].shape[1]
    return pl.pallas_call(
        functools.partial(prelude_kernel, hd),
        name="prelude",
        out_shape=(
            jax.ShapeDtypeStruct((blks, own + 8, 384), LOW),
            jax.ShapeDtypeStruct((own, width + ff), LOW),
            jax.ShapeDtypeStruct(weights[5].shape, LOW),
            jax.ShapeDtypeStruct((own, 3 * width), LOW),
        ),
        in_specs=[spec(pltpu.VMEM)] * 15,
        out_specs=(spec(pltpu.VMEM),) * 4,
        scratch_shapes=[pltpu.VMEM((8, 384), F32)],
        cost_estimate=pl.CostEstimate(flops=10**6, transcendentals=0, bytes_accessed=3 * 10**6),
    )(*weights, *vectors)


def fast_body(seqs, blks, heads):
    def run(
        hidden_in, query_weight, key_weight, value_weight, output_weight, inner_weight,
        outer_weight, query_bias, value_bias, output_bias, attention_gain, attention_shift,
        inner_bias, outer_bias, final_gain, final_shift, cotangent, grad_mask, cluster_order,
    ):
        rows, width = hidden_in.shape
        own = query_weight.shape[0]
        hidden_units = inner_weight.shape[1]
        length = cluster_order.shape[2]
        hd = width // heads
        chips = blks // 2
        scale = 1.0 / math.sqrt(hd)
        devices = seqs * blks
        b = lax.axis_index("blk")
        k = b // 2
        even_core = lax.rem(b, 2) == 0
        slabs, half_own, outer_own, proj_own = prelude(
            (query_weight, key_weight, value_weight, output_weight, inner_weight, outer_weight),
            (
                query_bias, value_bias, output_bias, attention_gain, attention_shift,
                outer_bias, final_gain, final_shift, inner_bias,
            ),
            blks,
            hd,
        )
        hidden_all, gathered, first_half, outer_full, projections = entry(
            hidden_in, slabs, (half_own, outer_own, proj_own), seqs, blks, 2
        )
        first_half = first_half.reshape(width, width + hidden_units)
        outer_full = outer_full.reshape(hidden_units, width)
        projections = projections.reshape(width, 3 * width)
        hidden_all = hidden_all.reshape(length, width)
        gathered = gathered.reshape((devices,) + slabs.shape[1:])
        order = cluster_order[0]
        head_first = jnp.where(even_core, 2 * k, 2 * chips + k)
        order_own = jnp.concatenate(
            [
                lax.dynamic_index_in_dim(order, head_first, 0, keepdims=False),
                lax.dynamic_index_in_dim(order, 2 * k + 1, 0, keepdims=False),
            ]
        )
        proj, cnat, cpack, vecs, bias_inner = attend(
            order_own, hidden_all, gathered, blks, hidden_units, hd, scale
        )
        ceven, codd = return_rows(cnat, cpack, 1)
        hidden_out, residual_grad, geven, godd, merged, extra = middle(
            ceven, codd, hidden_in, first_half, outer_full, vecs, bias_inner, cotangent,
            grad_mask, devices, hd,
        )
        slab = merged.shape[1:]
        gnat, gpack, summed = spread_rows(
            geven, godd, merged.reshape((seqs * chips, 2) + slab), 2
        )
        znat, zpack, grads = attend_back(
            order_own, hidden_all, proj, gnat, gpack, extra, hd, scale
        )
        pieces = 2
        zeven, zodd, proj_grads, big_grads = leave(
            znat, zpack, grads.reshape((seqs, blks) + grads.shape[1:]),
            summed.reshape(seqs, chips, pieces, slab[0] // pieces, width),
        )
        return (hidden_out,) + tuple(
            final(
                zeven, zodd, projections, residual_grad, proj_grads,
                big_grads.reshape((chips,) + slab), own, hidden_units, hd,
            )
        )

    return run


def masked_scores(left, right, left_ids, right_ids, scale):
    scores = back_product(left, right) * scale
    return jnp.where(left_ids[:, None] == right_ids[None, :], scores, -jnp.inf)


def body(
    hidden_in,
    query_weight,
    key_weight,
    value_weight,
    output_weight,
    inner_weight,
    outer_weight,
    query_bias,
    value_bias,
    output_bias,
    attention_gain,
    attention_shift,
    inner_bias,
    outer_bias,
    final_gain,
    final_shift,
    cotangent,
    grad_mask,
    cluster_order,
):
    rows = hidden_in.shape[0]
    width = hidden_in.shape[1]
    heads = cluster_order.shape[1]
    length = cluster_order.shape[2]
    scale = 1.0 / math.sqrt(width // heads)
    masters = (
        query_weight,
        key_weight,
        value_weight,
        output_weight,
        inner_weight,
        outer_weight,
        query_bias,
        value_bias,
        output_bias,
        attention_gain,
        attention_shift,
        inner_bias,
        outer_bias,
        final_gain,
        final_shift,
    )
    lowered = [master.astype(jnp.bfloat16) for master in masters]
    fetched = (
        lax.all_gather(lowered[0], ("seq", "blk"), axis=0, tiled=True),
        lax.all_gather(lowered[1], ("seq", "blk"), axis=0, tiled=True),
        lax.all_gather(lowered[2], ("seq", "blk"), axis=0, tiled=True),
        lax.all_gather(lowered[3], ("seq", "blk"), axis=0, tiled=True),
        lax.all_gather(lowered[4], ("seq", "blk"), axis=0, tiled=True),
        lax.all_gather(lowered[5], ("seq", "blk"), axis=0, tiled=True),
        lax.all_gather(lowered[6], ("seq", "blk"), axis=0, tiled=True),
        lax.all_gather(lowered[7], ("seq", "blk"), axis=0, tiled=True),
        lax.all_gather(lowered[8], ("seq", "blk"), axis=0, tiled=True),
        lax.all_gather(lowered[9], ("seq", "blk"), axis=0, tiled=True),
        lax.all_gather(lowered[10], ("seq", "blk"), axis=0, tiled=True),
        lax.all_gather(lowered[11], ("seq", "blk"), axis=0, tiled=True),
        lax.all_gather(lowered[12], ("seq", "blk"), axis=0, tiled=True),
        lax.all_gather(lowered[13], ("seq", "blk"), axis=0, tiled=True),
        lax.all_gather(lowered[14], ("seq", "blk"), axis=0, tiled=True),
    )
    query_full, key_full, value_full, output_full, inner_full, outer_full = fetched[0:6]
    vectors = [vector.astype(jnp.float32) for vector in fetched[6:15]]
    (
        bias_query,
        bias_value,
        bias_output,
        gain_first,
        shift_first,
        bias_inner,
        bias_outer,
        gain_final,
        shift_final,
    ) = vectors
    hidden = hidden_in.astype(jnp.float32)
    query_low = (
        jnp.dot(hidden_in, query_full, preferred_element_type=jnp.float32) + bias_query
    ).astype(jnp.bfloat16)
    keys_low = jnp.dot(hidden_in, key_full, preferred_element_type=jnp.float32).astype(jnp.bfloat16)
    values_low = (
        jnp.dot(hidden_in, value_full, preferred_element_type=jnp.float32) + bias_value
    ).astype(jnp.bfloat16)
    all_keys, all_values = (
        lax.all_gather(keys_low, "blk", axis=0, tiled=True),
        lax.all_gather(values_low, "blk", axis=0, tiled=True),
    )
    order = cluster_order[0]
    head_rows = jnp.broadcast_to(jnp.arange(heads, dtype=jnp.int32)[:, None], (heads, length))
    positions = jnp.broadcast_to(jnp.arange(length, dtype=jnp.int32)[None, :], (heads, length))
    inverse = jnp.zeros((heads, length), jnp.int32).at[head_rows, order].set(positions)
    key_cluster = inverse // CLUSTER
    member = lax.dynamic_slice_in_dim(key_cluster, lax.axis_index("blk") * rows, rows, 1)
    query_heads = head_major(query_low, heads)
    key_heads = head_major(all_keys, heads)
    value_heads = head_major(all_values, heads)
    head_ids = jnp.arange(heads, dtype=jnp.int32)

    def attend(index):
        scores = masked_scores(
            query_heads[index], key_heads[index], member[index], key_cluster[index], scale
        )
        peak = jnp.max(scores, axis=-1, keepdims=True)
        weights = jnp.exp(scores - peak)
        total = jnp.sum(weights, axis=-1, keepdims=True)
        probs_low = (weights / total).astype(jnp.bfloat16)
        mixed = jnp.dot(probs_low, value_heads[index], preferred_element_type=jnp.float32)
        return (mixed, (peak + jnp.log(total))[:, 0])

    mixed, logsum = lax.map(attend, head_ids)
    context_low = token_major(mixed).astype(jnp.bfloat16)
    attention_out = (
        jnp.dot(context_low, output_full, preferred_element_type=jnp.float32) + bias_output
    )
    first_norm, first_pull = jax.vjp(layer_norm, hidden + attention_out, gain_first, shift_first)
    first_low = first_norm.astype(jnp.bfloat16)
    inner_pre = jnp.dot(first_low, inner_full, preferred_element_type=jnp.float32) + bias_inner
    activated, gelu_pull = jax.vjp(exact_gelu, inner_pre)
    activated_low = activated.astype(jnp.bfloat16)
    outer_out = jnp.dot(activated_low, outer_full, preferred_element_type=jnp.float32) + bias_outer
    final_norm, final_pull = jax.vjp(layer_norm, first_norm + outer_out, gain_final, shift_final)
    hidden_out = final_norm.astype(jnp.bfloat16)
    out_grad = cotangent.astype(jnp.float32) * grad_mask.astype(jnp.float32)
    second_grad, grad_final_gain, grad_final_shift = final_pull(out_grad)
    outer_low = second_grad.astype(jnp.bfloat16)
    back_weights = (
        lax.all_gather(lowered[0], ("seq", "blk"), axis=0, tiled=True),
        lax.all_gather(lowered[1], ("seq", "blk"), axis=0, tiled=True),
        lax.all_gather(lowered[2], ("seq", "blk"), axis=0, tiled=True),
        lax.all_gather(lowered[3], ("seq", "blk"), axis=0, tiled=True),
        lax.all_gather(lowered[4], ("seq", "blk"), axis=0, tiled=True),
        lax.all_gather(lowered[5], ("seq", "blk"), axis=0, tiled=True),
    )
    grad_outer_weight = row_contract(activated_low, outer_low)
    grad_outer_bias = column_sum(outer_low)
    inner_low = gelu_pull(back_product(outer_low, back_weights[5]))[0].astype(jnp.bfloat16)
    grad_inner_weight = row_contract(first_low, inner_low)
    grad_inner_bias = column_sum(inner_low)
    first_grad = back_product(inner_low, back_weights[4]) + second_grad
    residual_grad, grad_attention_gain, grad_attention_shift = first_pull(first_grad)
    attn_low = residual_grad.astype(jnp.bfloat16)
    grad_output_weight = row_contract(context_low, attn_low)
    grad_output_bias = column_sum(attn_low)
    context_grad = back_product(attn_low, back_weights[3]).astype(jnp.bfloat16)
    grad_heads = head_major(context_grad, heads)

    def own_rows_back(index):
        scores = masked_scores(
            query_heads[index], key_heads[index], member[index], key_cluster[index], scale
        )
        probs = jnp.exp(scores - logsum[index][:, None])
        probs_low = probs.astype(jnp.bfloat16)
        grad_part = grad_heads[index]
        prob_grad = back_product(grad_part, value_heads[index])
        weighted = jnp.sum(probs * prob_grad, axis=-1, keepdims=True)
        score_low = (probs * (prob_grad - weighted)).astype(jnp.bfloat16)
        query_grad = (
            jnp.dot(score_low, key_heads[index], preferred_element_type=jnp.float32) * scale
        )
        return (probs_low, score_low, query_grad, weighted[:, 0])

    def attend_back(index):
        probs_low, score_low, query_grad, weighted = own_rows_back(index)
        key_sum = row_contract(score_low, query_heads[index]) * scale
        value_sum = row_contract(probs_low, grad_heads[index])
        return (query_grad, key_sum, value_sum)

    query_grads, key_grads, value_grads = lax.map(attend_back, head_ids)
    key_own, value_own = (
        lax.psum_scatter(token_major(key_grads), "blk", scatter_dimension=0, tiled=True),
        lax.psum_scatter(token_major(value_grads), "blk", scatter_dimension=0, tiled=True),
    )
    query_grad_low = token_major(query_grads).astype(jnp.bfloat16)
    key_grad_low = key_own.astype(jnp.bfloat16)
    value_grad_low = value_own.astype(jnp.bfloat16)
    grad_query_weight = row_contract(hidden_in, query_grad_low)
    grad_key_weight = row_contract(hidden_in, key_grad_low)
    grad_value_weight = row_contract(hidden_in, value_grad_low)
    grad_query_bias = column_sum(query_grad_low)
    grad_value_bias = column_sum(value_grad_low)
    input_grad = (
        back_product(query_grad_low, back_weights[0])
        + back_product(key_grad_low, back_weights[1])
        + back_product(value_grad_low, back_weights[2])
        + residual_grad
    )
    shares = (
        lax.psum_scatter(grad_query_weight, ("seq", "blk"), scatter_dimension=0, tiled=True),
        lax.psum_scatter(grad_key_weight, ("seq", "blk"), scatter_dimension=0, tiled=True),
        lax.psum_scatter(grad_value_weight, ("seq", "blk"), scatter_dimension=0, tiled=True),
        lax.psum_scatter(grad_output_weight, ("seq", "blk"), scatter_dimension=0, tiled=True),
        lax.psum_scatter(grad_inner_weight, ("seq", "blk"), scatter_dimension=0, tiled=True),
        lax.psum_scatter(grad_outer_weight, ("seq", "blk"), scatter_dimension=0, tiled=True),
        lax.psum_scatter(grad_query_bias, ("seq", "blk"), scatter_dimension=0, tiled=True),
        lax.psum_scatter(grad_value_bias, ("seq", "blk"), scatter_dimension=0, tiled=True),
        lax.psum_scatter(grad_output_bias, ("seq", "blk"), scatter_dimension=0, tiled=True),
        lax.psum_scatter(grad_attention_gain, ("seq", "blk"), scatter_dimension=0, tiled=True),
        lax.psum_scatter(grad_attention_shift, ("seq", "blk"), scatter_dimension=0, tiled=True),
        lax.psum_scatter(grad_inner_bias, ("seq", "blk"), scatter_dimension=0, tiled=True),
        lax.psum_scatter(grad_outer_bias, ("seq", "blk"), scatter_dimension=0, tiled=True),
        lax.psum_scatter(grad_final_gain, ("seq", "blk"), scatter_dimension=0, tiled=True),
        lax.psum_scatter(grad_final_shift, ("seq", "blk"), scatter_dimension=0, tiled=True),
    )
    return (hidden_out, input_grad) + tuple(shares)


def solution(mesh):
    placed = (
        P(("seq", "blk"), None),
        P(("seq", "blk"), None),
        P(("seq", "blk"), None),
        P(("seq", "blk"), None),
        P(("seq", "blk"), None),
        P(("seq", "blk"), None),
        P(("seq", "blk"), None),
        P(("seq", "blk")),
        P(("seq", "blk")),
        P(("seq", "blk")),
        P(("seq", "blk")),
        P(("seq", "blk")),
        P(("seq", "blk")),
        P(("seq", "blk")),
        P(("seq", "blk")),
        P(("seq", "blk")),
        P(("seq", "blk"), None),
        P(("seq", "blk"), None),
        P("seq", None, None),
    )
    seqs, blks = mesh.shape["seq"], mesh.shape["blk"]
    heads = 12
    fast = seqs == 4 and blks == 8
    return jax.shard_map(
        fast_body(seqs, blks, heads) if fast else body,
        mesh=mesh,
        in_specs=placed,
        out_specs=(
            P(("seq", "blk"), None),
            P(("seq", "blk"), None),
            P(("seq", "blk"), None),
            P(("seq", "blk"), None),
            P(("seq", "blk"), None),
            P(("seq", "blk"), None),
            P(("seq", "blk"), None),
            P(("seq", "blk"), None),
            P(("seq", "blk")),
            P(("seq", "blk")),
            P(("seq", "blk")),
            P(("seq", "blk")),
            P(("seq", "blk")),
            P(("seq", "blk")),
            P(("seq", "blk")),
            P(("seq", "blk")),
            P(("seq", "blk")),
        ),
        check_vma=False,
    )
```
